128 devices in a mesh: rep: 4 (over x), expert: 32 (over z, y, core).
Axes of the slice: x: 4, y: 4, z: 4, core: 2. Of those that a mesh axis runs over, the one named last changes fastest.
Arguments:
- tokens: bfloat16 [32768, 1536], P(('rep', 'expert')), may hold values from -6 to 6
- routes: int32 [32768, 4], P(('rep', 'expert')), may hold values from 0 to 31, all different within a row; in each aligned block of 256 rows (0 to 255, 256 to 511, ...) at most 64 rows name the same one
- history: int32 [128], P(('rep', 'expert')), may hold values from 0 to 12287, as said below
- cache_keys: bfloat16 [128, 2, 4100, 128], P(('rep', 'expert')), may hold values from -400 to 400
- cache_values: bfloat16 [128, 2, 4100, 128], P(('rep', 'expert')), may hold values from -6 to 6
- attn_gain: bfloat16 [1536], replicated, may hold values from 0.099609375 to 1.8984375
- w_query: bfloat16 [1536, 1536], replicated, may hold values from -0.15625 to 0.15625
- w_key: bfloat16 [1536, 256], replicated, may hold values from -0.15625 to 0.15625
- w_value: bfloat16 [1536, 256], replicated, may hold values from -0.15625 to 0.15625
- w_out: bfloat16 [1536, 1536], replicated, may hold values from -0.15625 to 0.15625
- ffn_gain: bfloat16 [1536], replicated, may hold values from 0.099609375 to 1.8984375
- w_router: bfloat16 [1536, 32], replicated, may hold values from -0.15625 to 0.15625
- expert_gate: bfloat16 [32, 1536, 768], P('expert'), may hold values from -0.15625 to 0.15625
- expert_up: bfloat16 [32, 1536, 768], P('expert'), may hold values from -0.15625 to 0.15625
- expert_down: bfloat16 [32, 768, 1536], P('expert'), may hold values from -0.21875 to 0.21875
Outputs:
- layer_out: bfloat16 [32768, 1536], P(('rep', 'expert'))
- new_keys: bfloat16 [32768, 256], P(('rep', 'expert'))
- new_values: bfloat16 [32768, 256], P(('rep', 'expert'))
The draws below stay inside these ranges and needn't reach their ends.
Inputs may be any that keep to these rules, and one draw needn't show every extreme that they name: `routes`: each row names 4 different experts. Among the rows of one request no expert is named by more than 64 rows, and in every draw some expert is named by exactly 64 rows of some request. Some request has no history and some has 12287 tokens.
All inputs are finite; a program needn't handle non-finite values.
Results may differ from the reference program's by a relative error of at most 0.007.
The reference program's roundings to bfloat16 on the way count: a program that leaves them out, or rounds other values in their place, can miss the bound.
Values may be sent and summed in bfloat16 or wider, within the bound.
A program may use at most 192 MiB of HBM per device.

```python
import math
from functools import partial
import jax
import jax.numpy as jnp
import numpy as np
from jax import lax

D = 1536
HEADS = 12
KV_HEADS = 2
HEAD_DIM = 128
FF = 768
TOP = 4
SINK = 4
WINDOW = 4096
STRETCH = 256
EXPERTS = 32
REQUESTS = 128
TOKENS = 32768
SLOTS = 4100
MOST = 64


def draw_history(key, part):
    key_one, key_two, key_three = jax.random.split(key, 3)
    upper_end = 3 * WINDOW
    first_draw = jax.random.randint(key_one, (REQUESTS,), 0, upper_end, dtype=jnp.int32)
    second_draw = jax.random.randint(key_two, (REQUESTS,), 0, upper_end, dtype=jnp.int32)
    lengths_drawn = first_draw * second_draw // upper_end
    shuffled = jax.random.permutation(key_three, REQUESTS)
    lengths_drawn = lengths_drawn.at[shuffled[0]].set(upper_end - 1)
    lengths_drawn = lengths_drawn.at[shuffled[1]].set(0)
    return lengths_drawn.astype(jnp.int32)


def draw_cache_keys(key, part):
    key_one = jax.random.fold_in(key, 0)
    base_draw = jnp.clip(jax.random.normal(key_one, (REQUESTS, KV_HEADS, SLOTS, HEAD_DIM), dtype=jnp.float32), -6.0, 6.0)
    return base_draw.astype(jnp.bfloat16)


def block_levels(stream_key, dims, cuts, low, top_value):
    level, own = 1.0, jax.random.fold_in(stream_key, 6)
    for dim, shards_of in cuts:
        draws = jnp.exp(jax.random.uniform(jax.random.fold_in(own, dim), (shards_of,), jnp.float32, low / len(cuts), top_value / len(cuts)))
        level = level * jnp.repeat(draws, dims[dim] // shards_of).reshape([-1 if axis == dim else 1 for axis in range(len(dims))])
    return level


def routed_block(stream_key, own, number, rows, number_of, top, most, skew):
    sequence = jax.random.permutation(stream_key, number_of)
    heavy_load, common = shares(number_of, rows * top, most, skew, True), shares(number_of, rows * top, most, skew, False)
    places = jnp.arange(number_of)

    def named(lengths, offset_by):
        used = int((lengths > 0).sum())
        fixed = max(1, used // 4)
        passed = fixed + (places - fixed + offset_by * (used - fixed)) % max(1, number_of - fixed)
        return jnp.zeros((number_of,), jnp.int32).at[sequence[jnp.where(places < fixed, places, passed)]].set(jnp.asarray(lengths, jnp.int32))

    lengths = jnp.where(number % 4 == 0, named(heavy_load, number // 4), named(common, number - number // 4 - 1))
    mixed = jax.random.permutation(jax.random.fold_in(own, 3), number_of)
    source_of, taker = mixed[0:number_of // 2 * 2:2], mixed[1:number_of // 2 * 2:2]
    margin = jnp.minimum(lengths[source_of] - 1, most - lengths[taker]) // 2
    margin = jnp.where((source_of == sequence[0]) | (taker == sequence[0]) | (lengths[taker] == 0), 0, jnp.maximum(margin, 0))
    passed = jax.random.randint(jax.random.fold_in(own, 4), (number_of // 2,), 0, 1 << 20) % (margin + 1)
    lengths = lengths.at[source_of].add(-passed).at[taker].add(passed)
    labels = jnp.searchsorted(jnp.cumsum(lengths), jnp.arange(rows * top), side="right").astype(jnp.int32)
    table = labels.reshape(top, rows).T
    table = table[jax.random.permutation(jax.random.fold_in(own, 1), rows)]
    offset_by = jax.random.randint(jax.random.fold_in(own, 2), (rows, 1), 0, top)
    return jnp.take_along_axis(table, (jnp.arange(top)[None, :] + offset_by) % top, axis=1)


def shares(number_of, total, limit, slope, full):
    weights = [(1 << 20) // math.isqrt(standing ** slope) + 1 for standing in range(1, number_of + 1)]
    largest = limit if full else min(limit, max(-(-total // number_of), total * weights[0] // sum(weights)))
    least = 1 if total - largest >= number_of - 1 else 0
    holding, spare = [largest] + [least] * (number_of - 1), total - largest - least * (number_of - 1)
    while spare > 0:
        movable = [i for i in range(1, number_of) if holding[i] < largest] or [i for i in range(1, number_of) if holding[i] < limit]
        whole, left = sum([weights[i] for i in movable]), spare
        for i in movable:
            extra = min(limit - holding[i], max(1, left * weights[i] // whole), spare)
            holding[i] = holding[i] + extra
            spare = spare - extra
    return np.array(holding)


def normal_values(stream_key, dims, spread, limit, pieces=(), held_as=jnp.bfloat16):
    entries = spread * jax.random.normal(stream_key, dims, jnp.float32)
    if pieces:
        entries = entries * block_levels(stream_key, dims, pieces, -0.22, 0.18)
    return jnp.clip(entries, -limit, limit).astype(held_as)


def setup_inputs(seed: int = 0) -> dict:
    key_list = jax.random.split(jax.random.key(seed), 16)
    tokens = normal_values(key_list[0], (TOKENS, D), 1.0, 6.0, ((0, 128),))
    routes_keys = jax.random.split(jax.random.fold_in(key_list[1], 1), TOKENS // STRETCH)
    routes_turns = jax.random.permutation(jax.random.fold_in(key_list[1], 3), TOKENS // STRETCH)
    routes = jax.vmap(lambda own, number: routed_block(jax.random.fold_in(key_list[1], 2), own, number, STRETCH, EXPERTS, TOP, MOST, 2))(routes_keys, routes_turns).reshape((TOKENS, TOP))
    history = draw_history(jax.random.fold_in(key_list[15], 71), 0)
    cache_keys = draw_cache_keys(jax.random.fold_in(key_list[15], 71), 0)
    cache_values = normal_values(key_list[4], (REQUESTS, KV_HEADS, SLOTS, HEAD_DIM), 1.0, 6.0, ((0, 128),))
    attn_gain = jnp.clip(1.0 + 0.18 * jax.random.normal(key_list[5], (D,), jnp.float32), 0.099609375, 1.8984375).astype(jnp.bfloat16)
    w_query = normal_values(key_list[6], (D, HEADS * HEAD_DIM), D ** -0.5, 0.15625)
    w_key = normal_values(key_list[7], (D, KV_HEADS * HEAD_DIM), D ** -0.5, 0.15625)
    w_value = normal_values(key_list[8], (D, KV_HEADS * HEAD_DIM), D ** -0.5, 0.15625)
    w_out = normal_values(key_list[9], (HEADS * HEAD_DIM, D), (HEADS * HEAD_DIM) ** -0.5, 0.15625)
    ffn_gain = jnp.clip(1.0 + 0.18 * jax.random.normal(key_list[10], (D,), jnp.float32), 0.099609375, 1.8984375).astype(jnp.bfloat16)
    w_router = normal_values(key_list[11], (D, EXPERTS), D ** -0.5, 0.15625)
    expert_gate = normal_values(key_list[12], (EXPERTS, D, FF), D ** -0.5, 0.15625, ((0, 32),))
    expert_up = normal_values(key_list[13], (EXPERTS, D, FF), D ** -0.5, 0.15625, ((0, 32),))
    expert_down = normal_values(key_list[14], (EXPERTS, FF, D), FF ** -0.5, 0.21875, ((0, 32),))
    return {"tokens": tokens, "routes": routes, "history": history, "cache_keys": cache_keys, "cache_values": cache_values, "attn_gain": attn_gain, "w_query": w_query, "w_key": w_key, "w_value": w_value, "w_out": w_out, "ffn_gain": ffn_gain, "w_router": w_router, "expert_gate": expert_gate, "expert_up": expert_up, "expert_down": expert_down}


theta_base = 1000000.0
eps_norm = 1e-06

def rms_norm(values, gain):
    mean_square = lax.optimization_barrier(jnp.mean(values * values, axis=-1, keepdims=True))
    return values * lax.rsqrt(mean_square + eps_norm) * gain.astype(jnp.float32)

def rotate(vectors, positions):
    half_dim = vectors.shape[-1] // 2
    exponent = jnp.arange(half_dim, dtype=jnp.float32) * (2.0 / vectors.shape[-1])
    inverse_freq = theta_base ** (-exponent)
    angles = positions.astype(jnp.float32)[:, None] * inverse_freq[None, :]
    cosine = jnp.cos(angles)[:, None, :]
    sine_part = jnp.sin(angles)[:, None, :]
    first = vectors[..., :half_dim]
    second = vectors[..., half_dim:]
    return jnp.concatenate([first * cosine - second * sine_part, second * cosine + first * sine_part], axis=-1)

def attention_request(packed, weights):
    hidden_in, past_tokens, keys_old, values_old = packed
    attn_gain, w_query, w_key, w_value, w_out, ffn_gain = weights
    residual_in = hidden_in.astype(jnp.float32)
    normed = rms_norm(residual_in, attn_gain).astype(jnp.bfloat16)
    positions = past_tokens + jnp.arange(STRETCH, dtype=jnp.int32)
    queries = rotate(jnp.dot(normed, w_query, preferred_element_type=jnp.float32).reshape(STRETCH, HEADS, HEAD_DIM), positions).astype(jnp.bfloat16)
    keys_new = rotate(jnp.dot(normed, w_key, preferred_element_type=jnp.float32).reshape(STRETCH, KV_HEADS, HEAD_DIM), positions).astype(jnp.bfloat16)
    values_new = jnp.dot(normed, w_value, preferred_element_type=jnp.float32).astype(jnp.bfloat16).reshape(STRETCH, KV_HEADS, HEAD_DIM)
    keys_all = jnp.concatenate([keys_old, jnp.transpose(keys_new, (1, 0, 2))], axis=1)
    values_all = jnp.concatenate([values_old, jnp.transpose(values_new, (1, 0, 2))], axis=1)
    slot_ids = jnp.arange(SLOTS, dtype=jnp.int32)
    slot_pos = jnp.where(slot_ids < SINK, slot_ids, slot_ids + WINDOW * ((past_tokens - 1 - slot_ids) // WINDOW))
    key_pos = jnp.concatenate([slot_pos, positions])
    key_live = jnp.concatenate([slot_ids < past_tokens, jnp.ones((STRETCH,), dtype=bool)])
    allowed = key_live[None, :] & (key_pos[None, :] <= positions[:, None]) & ((key_pos[None, :] < SINK) | (key_pos[None, :] > positions[:, None] - WINDOW))
    grouped = queries.reshape(STRETCH, KV_HEADS, HEADS // KV_HEADS, HEAD_DIM)
    scores = jnp.einsum('tkgd,ksd->kgts', grouped.astype(jnp.float32), keys_all.astype(jnp.float32)) * HEAD_DIM ** (-0.5)
    scores = jnp.where(allowed[None, None], scores, -1e+30)
    row_max = lax.optimization_barrier(jnp.max(scores, axis=-1, keepdims=True))
    expo = jnp.exp(scores - row_max)
    probability = (expo / lax.optimization_barrier(jnp.sum(expo, axis=-1, keepdims=True))).astype(jnp.bfloat16)
    attended = jnp.einsum('kgts,ksd->tkgd', probability.astype(jnp.float32), values_all.astype(jnp.float32)).astype(jnp.bfloat16).reshape(STRETCH, HEADS * HEAD_DIM)
    mixed_rows = residual_in + jnp.dot(attended, w_out, preferred_element_type=jnp.float32)
    ffn_in = rms_norm(mixed_rows, ffn_gain).astype(jnp.bfloat16)
    return (mixed_rows, ffn_in, keys_new.reshape(STRETCH, KV_HEADS * HEAD_DIM), values_new.reshape(STRETCH, KV_HEADS * HEAD_DIM))

def reference(tokens, routes, history, cache_keys, cache_values, attn_gain, w_query, w_key, w_value, w_out, ffn_gain, w_router, expert_gate, expert_up, expert_down):
    weights = (attn_gain, w_query, w_key, w_value, w_out, ffn_gain)
    mixed_rows, ffn_in, keys_new, values_new = lax.map(partial(attention_request, weights=weights), (tokens.reshape(REQUESTS, STRETCH, D), history, cache_keys, cache_values))
    mixed_rows = mixed_rows.reshape(TOKENS, D)
    ffn_in = ffn_in.reshape(TOKENS, D)
    keys_new = keys_new.reshape(TOKENS, KV_HEADS * HEAD_DIM)
    values_new = values_new.reshape(TOKENS, KV_HEADS * HEAD_DIM)
    logits = jnp.dot(ffn_in, w_router, preferred_element_type=jnp.float32)
    chosen_logits = jnp.take_along_axis(logits, routes, axis=1)
    gate_scores = jax.nn.sigmoid(chosen_logits)
    mix_weights = gate_scores / lax.optimization_barrier(jnp.sum(gate_scores, axis=1, keepdims=True))
    expert_ids = routes.reshape(-1).astype(jnp.int32)
    row_total = TOKENS * TOP
    one_hot = (expert_ids[:, None] == jnp.arange(EXPERTS, dtype=jnp.int32)[None, :]).astype(jnp.int32)
    per_device = one_hot.reshape(REQUESTS, STRETCH * TOP, EXPERTS)
    rank_within = lax.optimization_barrier(jnp.sum((jnp.cumsum(per_device, axis=1) - per_device) * per_device, axis=2)).reshape(-1).astype(jnp.int32)
    device_of = jnp.arange(row_total, dtype=jnp.int32) // (STRETCH * TOP)
    source_table = jnp.full((EXPERTS, REQUESTS * MOST), row_total, dtype=jnp.int32)
    source_table = source_table.at[expert_ids, device_of * MOST + rank_within].set(jnp.arange(row_total, dtype=jnp.int32))
    ffn_padded = jnp.concatenate([ffn_in, jnp.zeros((1, D), dtype=jnp.bfloat16)], axis=0)
    weight_padded = jnp.concatenate([mix_weights.reshape(-1), jnp.zeros((1,), dtype=jnp.float32)])

    def one_expert(combined, packed):
        row_index, gate_w, up_w, down_w = packed
        token_index = row_index // TOP
        rows_in = ffn_padded[token_index]
        gate_part = jnp.dot(rows_in, gate_w, preferred_element_type=jnp.float32)
        up_part = jnp.dot(rows_in, up_w, preferred_element_type=jnp.float32)
        hidden = (jnp.maximum(gate_part, 0.0) * up_part).astype(jnp.bfloat16)
        expert_out = jnp.dot(hidden, down_w, preferred_element_type=jnp.float32).astype(jnp.bfloat16)
        contribution = expert_out.astype(jnp.float32) * weight_padded[row_index][:, None]
        return (combined.at[token_index].add(contribution), None)
    combined, unused = lax.scan(one_expert, jnp.zeros((TOKENS + 1, D), dtype=jnp.float32), (source_table, expert_gate, expert_up, expert_down))
    layer_out = (mixed_rows + combined[:TOKENS]).astype(jnp.bfloat16)
    return (layer_out, keys_new, values_new)
```

```python
import functools

import jax
import jax.numpy as jnp
from jax import lax
from jax.experimental import pallas as pl
from jax.experimental.pallas import tpu as pltpu
from jax.sharding import PartitionSpec as P

HEADS = 12
KV_HEADS = 2
HEAD_DIM = 128
TOP = 4
SINK = 4
WINDOW = 4096
CAP = 64
EXPERTS = 32

theta_base = 1000000.0
eps_norm = 1e-06

f32 = jnp.float32
bf16 = jnp.bfloat16
MB = 1024 * 1024


def dot(a, b):
    return jnp.dot(a, b, preferred_element_type=f32)


def dot_nt(a, b):
    return lax.dot_general(a, b, (((1,), (1,)), ((), ())), preferred_element_type=f32)


def rope_tables(positions):
    half = HEAD_DIM // 2
    exponent = jnp.arange(half, dtype=f32) * (2.0 / HEAD_DIM)
    inverse_freq = theta_base ** (-exponent)
    angles = positions.astype(f32)[:, None] * inverse_freq[None, :]
    cosine, sine = jnp.cos(angles), jnp.sin(angles)
    return jnp.concatenate([cosine, cosine], 1), jnp.concatenate([-sine, sine], 1)


def norm_rows(x, gain):
    mean_square = jnp.mean(x * x, axis=-1, keepdims=True)
    return (x * lax.rsqrt(mean_square + eps_norm) * gain).astype(bf16)


Q_BLOCK = 512


def qkv_kernel(tok_ref, gain_ref, wq_ref, wk_ref, wv_ref, cos_ref, sin_ref, q_ref, k_ref, v_ref, normed):
    cosine, sine = cos_ref[...], sin_ref[...]

    def rope(x):
        return (x * cosine + pltpu.roll(x, HEAD_DIM // 2, 1) * sine).astype(bf16)

    @pl.when(pl.program_id(0) == 0)
    def _():
        normed[...] = norm_rows(tok_ref[...].astype(f32), gain_ref[...].astype(f32))
        keys = dot(normed[...], wk_ref[...])
        for h in range(KV_HEADS):
            k_ref[:, h * HEAD_DIM:(h + 1) * HEAD_DIM] = rope(keys[:, h * HEAD_DIM:(h + 1) * HEAD_DIM])
        v_ref[...] = dot(normed[...], wv_ref[...]).astype(bf16)

    y = dot(normed[...], wq_ref[...])
    for h in range(Q_BLOCK // HEAD_DIM):
        q_ref[h] = rope(y[:, h * HEAD_DIM:(h + 1) * HEAD_DIM])


def project(tokens, gain, w_query, w_key, w_value, cosine, sine):
    rows, width = tokens.shape
    kv = w_key.shape[1]
    heads = Q_BLOCK // HEAD_DIM
    full = lambda a: pl.BlockSpec(a.shape, lambda i: (0,) * a.ndim)
    return pl.pallas_call(
        qkv_kernel,
        grid=(w_query.shape[1] // Q_BLOCK,),
        in_specs=[
            full(tokens), full(gain),
            pl.BlockSpec((width, Q_BLOCK), lambda i: (0, i)),
            full(w_key), full(w_value), full(cosine), full(sine),
        ],
        out_specs=[
            pl.BlockSpec((heads, rows, HEAD_DIM), lambda i: (i, 0, 0)),
            pl.BlockSpec((rows, kv), lambda i: (0, 0)),
            pl.BlockSpec((rows, kv), lambda i: (0, 0)),
        ],
        out_shape=[
            jax.ShapeDtypeStruct((HEADS, rows, HEAD_DIM), bf16),
            jax.ShapeDtypeStruct((rows, kv), bf16),
            jax.ShapeDtypeStruct((rows, kv), bf16),
        ],
        scratch_shapes=[pltpu.VMEM((rows, width), bf16)],
        compiler_params=pltpu.CompilerParams(vmem_limit_bytes=32 * MB),
        name="project",
    )(tokens, gain, w_query, w_key, w_value, cosine, sine)


KB = 512
HT = 3
EXTRA = 384
SCALE2 = HEAD_DIM ** (-0.5) * 1.4426950408889634
LOW = -1e30


def attn_kernel(past_ref, q_ref, kc_ref, vc_ref, kn_ref, vn_ref, o_ref, s_main, s_tail, m_scr, l_scr, acc, kx, vx):
    rows = kn_ref.shape[0]
    tile = HT * rows
    past = past_ref[0]

    @pl.when(pl.program_id(1) == 0)
    def _():
        for new, cache, out in ((kn_ref, kc_ref, kx), (vn_ref, vc_ref, vx)):
            out[0:rows] = new[...]
            out[rows:EXTRA] = jnp.zeros((EXTRA - rows, HEAD_DIM), bf16)
            out[rows:rows + SINK] = cache[0, 0, WINDOW:WINDOW + SINK]

    q = q_ref[...].reshape(tile, HEAD_DIM)
    row = lax.broadcasted_iota(jnp.int32, (tile, 1), 0) & (rows - 1)
    blocks = jnp.minimum((past + (KB - 1)) // KB, WINDOW // KB)

    def limit(slot):
        back = (slot - past) & (WINDOW - 1)
        return jnp.where(slot < past, jnp.where(slot < SINK, 1 << 20, back), 0)

    def lane_max(s):
        out = s[:, 0:128]
        for c in range(1, s.shape[1] // 128):
            out = jnp.maximum(out, s[:, c * 128:(c + 1) * 128])
        return out

    def lane_sum(s):
        out = s[:, 0:128]
        for c in range(1, s.shape[1] // 128):
            out = out + s[:, c * 128:(c + 1) * 128]
        return out

    column = lax.broadcasted_iota(jnp.int32, (1, EXTRA), 1)
    tail_limit = limit(column + (WINDOW - rows))
    tail_limit = jnp.where(column < rows, rows, jnp.where(column < rows + SINK, tail_limit, 0))
    first_row = jnp.where(column < rows, column, 0)
    s = dot_nt(q, kx[...]) * SCALE2
    s = jnp.where((row >= first_row) & (row < tail_limit), s, LOW)
    s_tail[...] = s
    m_scr[...] = lane_max(s)

    def score(j, carry):
        start = pl.multiple_of(j * KB, KB)
        s = dot_nt(q, kc_ref[0, 0, pl.ds(start, KB), :]) * SCALE2
        offset = (start - past) & (WINDOW - 1)
        plain = (start + KB <= past) & (offset >= rows) & (offset + KB <= WINDOW)

        @pl.when(plain)
        def _():
            s_main[j] = s
            m_scr[...] = jnp.maximum(m_scr[...], lane_max(s))

        @pl.when(jnp.logical_not(plain))
        def _():
            slot = lax.broadcasted_iota(jnp.int32, (1, KB), 1) + start
            masked = jnp.where(row < limit(slot), s, LOW)
            s_main[j] = masked
            m_scr[...] = jnp.maximum(m_scr[...], lane_max(masked))

        return carry

    lax.fori_loop(0, blocks, score, 0)
    top = jnp.max(m_scr[...], axis=1, keepdims=True)
    p = jnp.exp2(s_tail[...] - top)
    l_scr[...] = lane_sum(p)
    acc[...] = dot(p.astype(bf16), vx[...])

    def weigh(j, carry):
        start = pl.multiple_of(j * KB, KB)
        p = jnp.exp2(s_main[j] - top)
        l_scr[...] += lane_sum(p)
        acc[...] += dot(p.astype(bf16), vc_ref[0, 0, pl.ds(start, KB), :])
        return carry

    lax.fori_loop(0, blocks, weigh, 0)
    total = jnp.sum(l_scr[...], axis=1, keepdims=True)
    out = (acc[...] / total).astype(bf16)
    for h in range(HT):
        o_ref[:, h * HEAD_DIM:(h + 1) * HEAD_DIM] = out[h * rows:(h + 1) * rows]


def attend(past, q, cache_keys, cache_values, keys_new, values_new):
    rows = keys_new.shape[0]
    slots = cache_keys.shape[2]
    tile = HT * rows
    per_group = HEADS // KV_HEADS // HT
    cache_spec = pl.BlockSpec((1, 1, slots, HEAD_DIM), lambda g, i, *_: (0, g, 0, 0))
    new_spec = pl.BlockSpec((rows, HEAD_DIM), lambda g, i, *_: (0, g))
    return pl.pallas_call(
        attn_kernel,
        grid_spec=pltpu.PrefetchScalarGridSpec(
            num_scalar_prefetch=1,
            grid=(KV_HEADS, per_group),
            in_specs=[
                pl.BlockSpec((HT, rows, HEAD_DIM), lambda g, i, *_: (g * per_group + i, 0, 0)),
                cache_spec, cache_spec, new_spec, new_spec,
            ],
            out_specs=pl.BlockSpec((rows, HT * HEAD_DIM), lambda g, i, *_: (0, g * per_group + i)),
            scratch_shapes=[
                pltpu.VMEM((WINDOW // KB, tile, KB), f32),
                pltpu.VMEM((tile, EXTRA), f32),
                pltpu.VMEM((tile, 128), f32),
                pltpu.VMEM((tile, 128), f32),
                pltpu.VMEM((tile, HEAD_DIM), f32),
                pltpu.VMEM((EXTRA, HEAD_DIM), bf16),
                pltpu.VMEM((EXTRA, HEAD_DIM), bf16),
            ],
        ),
        out_shape=jax.ShapeDtypeStruct((rows, HEADS * HEAD_DIM), bf16),
        compiler_params=pltpu.CompilerParams(vmem_limit_bytes=48 * MB),
        name="attend",
    )(past, q, cache_keys, cache_values, keys_new, values_new)


O_BLOCK = 512
PACK = 4


def out_kernel(att_ref, wo_ref, tok_ref, gain_ref, wr_ref, routes_ref, routes_t_ref,
               mixed_ref, mix_ref, rank_ref, send_ref, ffn, rank_t):
    n = pl.program_id(0)
    rows, width = tok_ref.shape
    steps = width // O_BLOCK
    experts = wr_ref.shape[1]
    block = PACK * CAP

    @pl.when(n < steps)
    def _():
        cols = pl.ds(pl.multiple_of(n * O_BLOCK, O_BLOCK), O_BLOCK)
        mixed_ref[:, cols] = tok_ref[:, cols].astype(f32) + dot(att_ref[...], wo_ref[...])

    @pl.when(n == steps - 1)
    def _():
        ffn[...] = norm_rows(mixed_ref[...], gain_ref[...].astype(f32))
        expert = lax.broadcasted_iota(jnp.int32, (rows, experts), 1)
        expert_t = lax.broadcasted_iota(jnp.int32, (experts, rows), 0)
        named = routes_ref[:, 0:1] == expert
        named_t = routes_t_ref[0:1, :] == expert_t
        for j in range(1, TOP):
            named = named | (routes_ref[:, j:j + 1] == expert)
            named_t = named_t | (routes_t_ref[j:j + 1, :] == expert_t)
        a = lax.broadcasted_iota(jnp.int32, (rows, rows), 0)
        b = lax.broadcasted_iota(jnp.int32, (rows, rows), 1)
        one, zero = jnp.ones((), f32), jnp.zeros((), f32)
        before = jnp.where(b < a, one, zero).astype(bf16)
        before_t = jnp.where(a < b, one, zero).astype(bf16)
        ranks = dot(before, jnp.where(named, one, zero).astype(bf16))
        ranks_t = dot(jnp.where(named_t, one, zero).astype(bf16), before_t)
        rank_ref[...] = jnp.where(named, ranks, -1.0).astype(bf16)
        rank_t[...] = jnp.where(named_t, ranks_t, -1.0).astype(bf16)
        logits = dot(ffn[...], wr_ref[...])
        score = jnp.where(named, jax.nn.sigmoid(logits), 0.0)
        mix_ref[...] = score / jnp.sum(score, axis=1, keepdims=True)

    @pl.when(n >= steps)
    def _():
        first = (n - steps) * PACK
        slot = lax.broadcasted_iota(jnp.int32, (block, experts), 0)
        expert = lax.broadcasted_iota(jnp.int32, (block, experts), 1)
        spread = jnp.where(slot // CAP + first == expert, 1.0, 0.0).astype(bf16)
        wanted = dot(spread, rank_t[...])
        place = (lax.broadcasted_iota(jnp.int32, (block, rows), 0) % CAP).astype(f32)
        select = jnp.where(wanted == place, 1.0, 0.0).astype(bf16)
        send_ref[...] = dot(select, ffn[...]).astype(bf16)


def finish(attended, w_out, tokens, gain, w_router, routes, routes_t):
    rows, width = tokens.shape
    experts = w_router.shape[1]
    steps = width // O_BLOCK
    packs = experts // PACK
    full = lambda a: pl.BlockSpec(a.shape, lambda n: (0,) * a.ndim)
    whole = lambda shape: pl.BlockSpec(shape, lambda n: (0, 0))
    return pl.pallas_call(
        out_kernel,
        grid=(steps + packs,),
        in_specs=[
            full(attended),
            pl.BlockSpec((width, O_BLOCK), lambda n: (0, jnp.minimum(n, steps - 1))),
            full(tokens), full(gain), full(w_router), full(routes), full(routes_t),
        ],
        out_specs=[
            whole((rows, width)), whole((rows, experts)), whole((rows, experts)),
            pl.BlockSpec((PACK * CAP, width), lambda n: (jnp.maximum(n - steps, 0), 0)),
        ],
        out_shape=[
            jax.ShapeDtypeStruct((rows, width), f32),
            jax.ShapeDtypeStruct((rows, experts), f32),
            jax.ShapeDtypeStruct((rows, experts), bf16),
            jax.ShapeDtypeStruct((experts * CAP, width), bf16),
        ],
        scratch_shapes=[pltpu.VMEM((rows, width), bf16), pltpu.VMEM((experts, rows), bf16)],
        compiler_params=pltpu.CompilerParams(vmem_limit_bytes=32 * MB),
        name="finish",
    )(attended, w_out, tokens, gain, w_router, routes, routes_t)


def combine_kernel(mixed_ref, mix_ref, rank_ref, rows_ref, out_ref, total):
    n = pl.program_id(0)
    rows, experts = mix_ref.shape
    block = PACK * CAP
    expert = lax.broadcasted_iota(jnp.int32, (experts, block), 0)
    slot = lax.broadcasted_iota(jnp.int32, (experts, block), 1)
    spread = jnp.where(slot // CAP + n * PACK == expert, 1.0, 0.0).astype(bf16)
    mix = mix_ref[...]
    high = mix.astype(bf16)
    low = (mix - high.astype(f32)).astype(bf16)
    place = (lax.broadcasted_iota(jnp.int32, (rows, block), 1) % CAP).astype(f32)
    here = dot(rank_ref[...], spread) == place
    c_high = jnp.where(here, dot(high, spread), 0.0).astype(bf16)
    c_low = jnp.where(here, dot(low, spread), 0.0).astype(bf16)
    part = dot(c_high, rows_ref[...]) + dot(c_low, rows_ref[...])

    @pl.when(n == 0)
    def _():
        total[...] = part

    @pl.when(n > 0)
    def _():
        total[...] += part

    @pl.when(n == pl.num_programs(0) - 1)
    def _():
        out_ref[...] = (mixed_ref[...] + total[...]).astype(bf16)


def combine(mixed, mix, rank, returned):
    rows, width = mixed.shape
    experts = mix.shape[1]
    full = lambda a: pl.BlockSpec(a.shape, lambda n: (0,) * a.ndim)
    return pl.pallas_call(
        combine_kernel,
        grid=(experts // PACK,),
        in_specs=[full(mixed), full(mix), full(rank), pl.BlockSpec((PACK * CAP, width), lambda n: (n, 0))],
        out_specs=pl.BlockSpec((rows, width), lambda n: (0, 0)),
        out_shape=jax.ShapeDtypeStruct((rows, width), bf16),
        scratch_shapes=[pltpu.VMEM((rows, width), f32)],
        compiler_params=pltpu.CompilerParams(vmem_limit_bytes=32 * MB),
        name="combine",
    )(mixed, mix, rank, returned)


def shards(tokens, routes, history, cache_keys, cache_values, attn_gain, w_query, w_key, w_value, w_out,
           ffn_gain, w_router, expert_gate, expert_up, expert_down):
    rows, width = tokens.shape
    positions = history[0] + jnp.arange(rows, dtype=jnp.int32)
    cosine, sine = rope_tables(positions)
    q, keys_new, values_new = project(tokens, attn_gain[None], w_query, w_key, w_value, cosine, sine)
    attended = attend(history, q, cache_keys, cache_values, keys_new, values_new)
    mixed, mix, rank, send = finish(
        attended, w_out, tokens, ffn_gain[None], w_router, routes, jnp.transpose(routes)
    )
    experts = w_router.shape[1]
    received = lax.all_to_all(
        send.reshape(experts, CAP, width), "expert", split_axis=0, concat_axis=0, tiled=True
    )
    flat = received.reshape(-1, width)
    gate_part = dot(flat, expert_gate[0])
    up_part = dot(flat, expert_up[0])
    hidden = (jnp.maximum(gate_part, 0.0) * up_part).astype(bf16)
    expert_out = dot(hidden, expert_down[0]).astype(bf16)
    returned = lax.all_to_all(
        expert_out.reshape(received.shape), "expert", split_axis=0, concat_axis=0, tiled=True
    )
    layer_out = combine(mixed, mix, rank, returned.reshape(-1, width))
    return layer_out, keys_new, values_new


def solution(mesh):
    both = ("rep", "expert")
    in_specs = (
        P(both, None), P(both, None), P(both), P(both, None, None, None), P(both, None, None, None),
        P(), P(), P(), P(), P(), P(), P(),
        P("expert", None, None), P("expert", None, None), P("expert", None, None),
    )
    out_specs = (P(both, None), P(both, None), P(both, None))
    return jax.shard_map(shards, mesh=mesh, in_specs=in_specs, out_specs=out_specs, check_vma=False)
```

```python
import functools

import jax
import jax.numpy as jnp
from jax import lax
from jax.experimental import pallas as pl
from jax.experimental.pallas import tpu as pltpu
from jax.sharding import PartitionSpec as P

HEADS = 12
KV_HEADS = 2
HEAD_DIM = 128
TOP = 4
SINK = 4
WINDOW = 4096
CAP = 64
EXPERTS = 32

theta_base = 1000000.0
eps_norm = 1e-06

f32 = jnp.float32
bf16 = jnp.bfloat16
MB = 1024 * 1024


def dot(a, b):
    return jnp.dot(a, b, preferred_element_type=f32)


def dot_nt(a, b):
    return lax.dot_general(a, b, (((1,), (1,)), ((), ())), preferred_element_type=f32)


def rope_tables(positions):
    half = HEAD_DIM // 2
    exponent = jnp.arange(half, dtype=f32) * (2.0 / HEAD_DIM)
    inverse_freq = theta_base ** (-exponent)
    angles = positions.astype(f32)[:, None] * inverse_freq[None, :]
    cosine, sine = jnp.cos(angles), jnp.sin(angles)
    return jnp.concatenate([cosine, cosine], 1), jnp.concatenate([-sine, sine], 1)


def norm_rows(x, gain):
    mean_square = jnp.mean(x * x, axis=-1, keepdims=True)
    return (x * lax.rsqrt(mean_square + eps_norm) * gain).astype(bf16)


Q_BLOCK = 512


def qkv_kernel(tok_ref, gain_ref, wq_ref, wk_ref, wv_ref, cos_ref, sin_ref, q_ref, k_ref, v_ref, normed):
    cosine, sine = cos_ref[...], sin_ref[...]

    def rope(x):
        return (x * cosine + pltpu.roll(x, HEAD_DIM // 2, 1) * sine).astype(bf16)

    @pl.when(pl.program_id(0) == 0)
    def _():
        normed[...] = norm_rows(tok_ref[...].astype(f32), gain_ref[...].astype(f32))
        keys = dot(normed[...], wk_ref[...])
        for h in range(KV_HEADS):
            k_ref[:, h * HEAD_DIM:(h + 1) * HEAD_DIM] = rope(keys[:, h * HEAD_DIM:(h + 1) * HEAD_DIM])
        v_ref[...] = dot(normed[...], wv_ref[...]).astype(bf16)

    y = dot(normed[...], wq_ref[...])
    for h in range(Q_BLOCK // HEAD_DIM):
        q_ref[h] = rope(y[:, h * HEAD_DIM:(h + 1) * HEAD_DIM])


def project(tokens, gain, w_query, w_key, w_value, cosine, sine):
    rows, width = tokens.shape
    kv = w_key.shape[1]
    heads = Q_BLOCK // HEAD_DIM
    full = lambda a: pl.BlockSpec(a.shape, lambda i: (0,) * a.ndim)
    return pl.pallas_call(
        qkv_kernel,
        grid=(w_query.shape[1] // Q_BLOCK,),
        in_specs=[
            full(tokens), full(gain),
            pl.BlockSpec((width, Q_BLOCK), lambda i: (0, i)),
            full(w_key), full(w_value), full(cosine), full(sine),
        ],
        out_specs=[
            pl.BlockSpec((heads, rows, HEAD_DIM), lambda i: (i, 0, 0)),
            pl.BlockSpec((rows, kv), lambda i: (0, 0)),
            pl.BlockSpec((rows, kv), lambda i: (0, 0)),
        ],
        out_shape=[
            jax.ShapeDtypeStruct((HEADS, rows, HEAD_DIM), bf16),
            jax.ShapeDtypeStruct((rows, kv), bf16),
            jax.ShapeDtypeStruct((rows, kv), bf16),
        ],
        scratch_shapes=[pltpu.VMEM((rows, width), bf16)],
        compiler_params=pltpu.CompilerParams(vmem_limit_bytes=32 * MB),
        name="project",
    )(tokens, gain, w_query, w_key, w_value, cosine, sine)


KB = 512
HT = 3
EXTRA = 384
SCALE2 = HEAD_DIM ** (-0.5) * 1.4426950408889634
LOW = -1e30


def attn_kernel(past_ref, q_ref, kc_ref, vc_ref, kn_ref, vn_ref, o_ref, s_main, s_tail, m_scr, l_scr, acc, kx, vx):
    rows = kn_ref.shape[0]
    tile = HT * rows
    past = past_ref[0]

    @pl.when(pl.program_id(1) == 0)
    def _():
        for new, cache, out in ((kn_ref, kc_ref, kx), (vn_ref, vc_ref, vx)):
            out[0:rows] = new[...]
            out[rows:EXTRA] = jnp.zeros((EXTRA - rows, HEAD_DIM), bf16)
            out[rows:rows + SINK] = cache[0, 0, WINDOW:WINDOW + SINK]

    q = q_ref[...].reshape(tile, HEAD_DIM)
    row = lax.broadcasted_iota(jnp.int32, (tile, 1), 0) & (rows - 1)
    blocks = jnp.minimum((past + (KB - 1)) // KB, WINDOW // KB)

    def limit(slot):
        back = (slot - past) & (WINDOW - 1)
        return jnp.where(slot < past, jnp.where(slot < SINK, 1 << 20, back), 0)

    def lane_max(s):
        out = s[:, 0:128]
        for c in range(1, s.shape[1] // 128):
            out = jnp.maximum(out, s[:, c * 128:(c + 1) * 128])
        return out

    def lane_sum(s):
        out = s[:, 0:128]
        for c in range(1, s.shape[1] // 128):
            out = out + s[:, c * 128:(c + 1) * 128]
        return out

    column = lax.broadcasted_iota(jnp.int32, (1, EXTRA), 1)
    tail_limit = limit(column + (WINDOW - rows))
    tail_limit = jnp.where(column < rows, rows, jnp.where(column < rows + SINK, tail_limit, 0))
    first_row = jnp.where(column < rows, column, 0)
    s = dot_nt(q, kx[...]) * SCALE2
    s = jnp.where((row >= first_row) & (row < tail_limit), s, LOW)
    s_tail[...] = s
    m_scr[...] = lane_max(s)

    def score(j, carry):
        start = pl.multiple_of(j * KB, KB)
        s = dot_nt(q, kc_ref[0, 0, pl.ds(start, KB), :]) * SCALE2
        offset = (start - past) & (WINDOW - 1)
        plain = (start + KB <= past) & (offset >= rows) & (offset + KB <= WINDOW)

        @pl.when(plain)
        def _():
            s_main[j] = s
            m_scr[...] = jnp.maximum(m_scr[...], lane_max(s))

        @pl.when(jnp.logical_not(plain))
        def _():
            slot = lax.broadcasted_iota(jnp.int32, (1, KB), 1) + start
            masked = jnp.where(row < limit(slot), s, LOW)
            s_main[j] = masked
            m_scr[...] = jnp.maximum(m_scr[...], lane_max(masked))

        return carry

    lax.fori_loop(0, blocks, score, 0)
    top = jnp.max(m_scr[...], axis=1, keepdims=True)
    p = jnp.exp2(s_tail[...] - top)
    l_scr[...] = lane_sum(p)
    acc[...] = dot(p.astype(bf16), vx[...])

    def weigh(j, carry):
        start = pl.multiple_of(j * KB, KB)
        p = jnp.exp2(s_main[j] - top)
        l_scr[...] += lane_sum(p)
        acc[...] += dot(p.astype(bf16), vc_ref[0, 0, pl.ds(start, KB), :])
        return carry

    lax.fori_loop(0, blocks, weigh, 0)
    total = jnp.sum(l_scr[...], axis=1, keepdims=True)
    out = (acc[...] / total).astype(bf16)
    for h in range(HT):
        o_ref[:, h * HEAD_DIM:(h + 1) * HEAD_DIM] = out[h * rows:(h + 1) * rows]


def attend(past, q, cache_keys, cache_values, keys_new, values_new):
    rows = keys_new.shape[0]
    slots = cache_keys.shape[2]
    tile = HT * rows
    per_group = HEADS // KV_HEADS // HT
    cache_spec = pl.BlockSpec((1, 1, slots, HEAD_DIM), lambda g, i, *_: (0, g, 0, 0))
    new_spec = pl.BlockSpec((rows, HEAD_DIM), lambda g, i, *_: (0, g))
    return pl.pallas_call(
        attn_kernel,
        grid_spec=pltpu.PrefetchScalarGridSpec(
            num_scalar_prefetch=1,
            grid=(KV_HEADS, per_group),
            in_specs=[
                pl.BlockSpec((HT, rows, HEAD_DIM), lambda g, i, *_: (g * per_group + i, 0, 0)),
                cache_spec, cache_spec, new_spec, new_spec,
            ],
            out_specs=pl.BlockSpec((rows, HT * HEAD_DIM), lambda g, i, *_: (0, g * per_group + i)),
            scratch_shapes=[
                pltpu.VMEM((WINDOW // KB, tile, KB), f32),
                pltpu.VMEM((tile, EXTRA), f32),
                pltpu.VMEM((tile, 128), f32),
                pltpu.VMEM((tile, 128), f32),
                pltpu.VMEM((tile, HEAD_DIM), f32),
                pltpu.VMEM((EXTRA, HEAD_DIM), bf16),
                pltpu.VMEM((EXTRA, HEAD_DIM), bf16),
            ],
        ),
        out_shape=jax.ShapeDtypeStruct((rows, HEADS * HEAD_DIM), bf16),
        compiler_params=pltpu.CompilerParams(vmem_limit_bytes=48 * MB),
        name="attend",
    )(past, q, cache_keys, cache_values, keys_new, values_new)


O_BLOCK = 512
META = 128


def out_kernel(att_ref, wo_ref, tok_ref, gain_ref, wr_ref, routes_ref, mixed_ref, pay_ref):
    n = pl.program_id(0)
    rows, width = tok_ref.shape
    steps = width // O_BLOCK
    half = width // 2
    experts = wr_ref.shape[1]
    cols = pl.ds(pl.multiple_of(n * O_BLOCK, O_BLOCK), O_BLOCK)
    mixed_ref[:, cols] = tok_ref[:, cols].astype(f32) + dot(att_ref[...], wo_ref[...])

    @pl.when(n == steps - 1)
    def _():
        ffn = norm_rows(mixed_ref[...], gain_ref[...].astype(f32))
        expert = lax.broadcasted_iota(jnp.int32, (rows, experts), 1)
        named = routes_ref[:, 0:1] == expert
        for j in range(1, TOP):
            named = named | (routes_ref[:, j:j + 1] == expert)
        a = lax.broadcasted_iota(jnp.int32, (rows, rows), 0)
        b = lax.broadcasted_iota(jnp.int32, (rows, rows), 1)
        before = jnp.where(b < a, 1.0, 0.0).astype(bf16)
        rank = jnp.where(named, dot(before, jnp.where(named, 1.0, 0.0).astype(bf16)), -1.0).astype(bf16)
        score = jnp.where(named, jax.nn.sigmoid(dot(ffn, wr_ref[...])), 0.0)
        mix = score / jnp.sum(score, axis=1, keepdims=True)
        high = mix.astype(bf16)
        low = (mix - high.astype(f32)).astype(bf16)
        source = lax.broadcasted_iota(jnp.int32, (experts, META), 0)
        column = lax.broadcasted_iota(jnp.int32, (experts, META), 1)
        put = lambda x, i: dot(x, jnp.where(column == source + i * experts, 1.0, 0.0).astype(bf16))
        meta = (put(high, 0) + put(low, 1) + put(rank, 2)).astype(bf16)
        for h in range(2):
            pay_ref[h, :, 0:half] = ffn[:, h * half:(h + 1) * half]
            pay_ref[h, :, half:half + META] = meta


def finish(attended, w_out, tokens, gain, w_router, routes):
    rows, width = tokens.shape
    full = lambda a: pl.BlockSpec(a.shape, lambda n: (0,) * a.ndim)
    return pl.pallas_call(
        out_kernel,
        grid=(width // O_BLOCK,),
        in_specs=[
            full(attended), pl.BlockSpec((width, O_BLOCK), lambda n: (0, n)),
            full(tokens), full(gain), full(w_router), full(routes),
        ],
        out_specs=[
            pl.BlockSpec((rows, width), lambda n: (0, 0)),
            pl.BlockSpec((2, rows, width // 2 + META), lambda n: (0, 0, 0)),
        ],
        out_shape=[
            jax.ShapeDtypeStruct((rows, width), f32),
            jax.ShapeDtypeStruct((2, rows, width // 2 + META), bf16),
        ],
        compiler_params=pltpu.CompilerParams(vmem_limit_bytes=32 * MB),
        name="finish",
    )(attended, w_out, tokens, gain, w_router, routes)


SIDE = 4
GROUPS = 2 * SIDE


def position():
    me = lax.axis_index("expert")
    return me // (2 * SIDE), (me // 2) % SIDE, me % 2


def peer(axis, step, flip):
    z, y, core = position()
    if axis == 0:
        z = (z + step) % SIDE
    else:
        y = (y + step) % SIDE
    return z * 2 * SIDE + y * 2 + (core + flip) % 2


def remote(src, dst, sems, i, to):
    return pltpu.make_async_remote_copy(
        src_ref=src, dst_ref=dst, send_sem=sems.at[0, i], recv_sem=sems.at[1, i],
        device_id={"expert": to}, device_id_type=pl.DeviceIdType.MESH,
    )


def greet():
    barrier = pltpu.get_barrier_semaphore()
    others = [peer(0, 0, 1)]
    for axis in range(2):
        for step in (1, SIDE - 1):
            for flip in range(2):
                others.append(peer(axis, step, flip))
    for other in others:
        pl.semaphore_signal(barrier, inc=1, device_id={"expert": other}, device_id_type=pl.DeviceIdType.MESH)
    pl.semaphore_wait(barrier, len(others))


def group_expert(h, index):
    z, y, core = position()
    step, flip = index >> 1, index & 1
    if h == 0:
        y = (y + step) & (SIDE - 1)
    else:
        z = (z + step) & (SIDE - 1)
    return z * (2 * SIDE) + y * 2 + ((core + flip) & 1)


class Spread:
    def __init__(self, h, src, dst, relay, sems, base):
        axis = 1 - h
        unit = lambda step, flip: src.at[h, step * 2 + flip]
        slot = lambda step, flip: dst.at[h, (SIDE - step) % SIDE * 2 + flip]
        self.relays = [
            remote(unit(2, 0), relay.at[h, 0], sems, base, peer(axis, 1, 0)),
            remote(unit(2, 1), relay.at[h, 1], sems, base + 1, peer(axis, SIDE - 1, 0)),
        ]
        self.direct = [
            remote(unit(step, flip), slot(step, flip), sems, base + 2 + i, peer(axis, step, flip))
            for i, (step, flip) in enumerate(((1, 0), (3, 0), (1, 1), (3, 1), (0, 1)))
        ]
        self.onward = [
            remote(relay.at[h, 0], slot(2, 0), sems, base + 7, peer(axis, 1, 0)),
            remote(relay.at[h, 1], slot(2, 1), sems, base + 8, peer(axis, SIDE - 1, 1)),
        ]

    def start(self):
        for copy in self.relays + self.direct:
            copy.start()

    def forward(self):
        for first, then in zip(self.relays, self.onward):
            first.wait_recv()
            then.start()

    def finish(self):
        for copy in self.direct + self.onward:
            copy.wait_recv()
        for copy in self.relays + self.direct + self.onward:
            copy.wait_send()


SPREAD_COPIES = 9


def dispatch_kernel(pay_ref, x_ref, near_ref, send, relay, own_sem, sems):
    rows = pay_ref.shape[1]
    half = x_ref.shape[3]
    mid = rows // 2
    slots = GROUPS * CAP
    greet()
    top, low = pl.ds(0, mid), pl.ds(mid, mid)
    own = [pltpu.make_async_copy(pay_ref.at[h], near_ref.at[h, 0], own_sem.at[h]) for h in range(2)]
    gather, passing, spreads = [], [], []
    for h in range(2):
        up, down = peer(h, 1, 0), peer(h, SIDE - 1, 0)
        base = h * 15
        gather.append([
            remote(pay_ref.at[h, top], near_ref.at[h, 3, top], sems, base, up),
            remote(pay_ref.at[h, low], near_ref.at[h, 1, low], sems, base + 1, down),
            remote(pay_ref.at[h, low], near_ref.at[h, 3, low], sems, base + 2, up),
            remote(pay_ref.at[h, top], near_ref.at[h, 1, top], sems, base + 3, down),
        ])
        passing.append([
            remote(near_ref.at[h, 3, top], near_ref.at[h, 2, top], sems, base + 4, up),
            remote(near_ref.at[h, 1, low], near_ref.at[h, 2, low], sems, base + 5, down),
        ])
        spreads.append(Spread(h, send, x_ref, relay, sems, base + 6))
    for i in range(4):
        for h in range(2):
            gather[h][i].start()
    for h in range(2):
        own[h].start()

    place = (lax.broadcasted_iota(jnp.int32, (slots, rows), 0) % CAP).astype(f32)
    group = lax.broadcasted_iota(jnp.int32, (slots, META), 0) // CAP
    column = lax.broadcasted_iota(jnp.int32, (slots, META), 1)

    def choose(h, s):
        spread = jnp.where(column == group_expert(h, group) + 2 * 4 * GROUPS, 1.0, 0.0).astype(bf16)
        wanted = dot_nt(spread, near_ref[h, s, :, half:half + META])
        select = jnp.where(wanted == place, 1.0, 0.0).astype(bf16)
        chosen = dot(select, near_ref[h, s, :, 0:half]).astype(bf16)
        for g in range(GROUPS):
            send[h, g, s * CAP:(s + 1) * CAP] = chosen[g * CAP:(g + 1) * CAP]

    for h in range(2):
        own[h].wait()
        choose(h, 0)
    for i in range(2):
        for h in range(2):
            gather[h][i].wait_recv()
            passing[h][i].start()
    for i, s in ((2, 3), (3, 1)):
        for h in range(2):
            gather[h][i].wait_recv()
            choose(h, s)
    for h in range(2):
        for copy in passing[h]:
            copy.wait_recv()
        choose(h, 2)
        spreads[h].start()
    for h in range(2):
        x_ref[h, 0] = send[h, 0]
    for h in range(2):
        spreads[h].forward()
    for h in range(2):
        spreads[h].finish()
        for copy in gather[h] + passing[h]:
            copy.wait_send()


def dispatch(pay):
    _, rows, wide = pay.shape
    half = wide - META
    vmem = pl.BlockSpec(memory_space=pltpu.VMEM)
    return pl.pallas_call(
        dispatch_kernel,
        in_specs=[vmem],
        out_specs=[vmem, vmem],
        out_shape=[
            jax.ShapeDtypeStruct((2, GROUPS, SIDE * CAP, half), bf16),
            jax.ShapeDtypeStruct((2, SIDE, rows, wide), bf16),
        ],
        scratch_shapes=[
            pltpu.VMEM((2, GROUPS, SIDE * CAP, half), bf16),
            pltpu.VMEM((2, 2, SIDE * CAP, half), bf16),
            pltpu.SemaphoreType.DMA((2,)),
            pltpu.SemaphoreType.DMA((2, 30)),
        ],
        compiler_params=pltpu.CompilerParams(collective_id=1, has_side_effects=True, vmem_limit_bytes=40 * MB),
        name="dispatch",
    )(pay)


def expert_kernel(x_ref, gate_ref, up_ref, down_ref, y_ref):
    half = x_ref.shape[3]

    def block(g, carry):
        step, flip = g // 2, g % 2
        spot = pl.ds(pl.multiple_of(step * CAP, CAP), CAP)
        a = x_ref[0, g]
        b = jnp.concatenate([x_ref[1, 2 * s + flip, spot] for s in range(SIDE)], axis=0)
        gate = dot(a, gate_ref[0, 0:half]) + dot(b, gate_ref[0, half:2 * half])
        up = dot(a, up_ref[0, 0:half]) + dot(b, up_ref[0, half:2 * half])
        hidden = (jnp.maximum(gate, 0.0) * up).astype(bf16)
        y_ref[0, g] = dot(hidden, down_ref[0, :, 0:half]).astype(bf16)
        other = dot(hidden, down_ref[0, :, half:2 * half]).astype(bf16)
        for s in range(SIDE):
            y_ref[1, 2 * s + flip, spot] = other[s * CAP:(s + 1) * CAP]
        return carry

    lax.fori_loop(0, GROUPS, block, 0)


def run_expert(x, gate, up, down):
    vmem = pl.BlockSpec(memory_space=pltpu.VMEM)
    return pl.pallas_call(
        expert_kernel,
        in_specs=[vmem] * 4,
        out_specs=vmem,
        out_shape=jax.ShapeDtypeStruct(x.shape, bf16),
        compiler_params=pltpu.CompilerParams(vmem_limit_bytes=40 * MB),
        name="expert",
    )(x, gate, up, down)


def return_kernel(y_ref, near_ref, mixed_ref, out_ref, back, relay, parts, passed, final, sems):
    rows, width = mixed_ref.shape
    half = width // 2
    mid = rows // 2
    slots = GROUPS * CAP
    greet()
    top, low = pl.ds(0, mid), pl.ds(mid, mid)
    spreads, passing, last = [], [], []
    for h in range(2):
        up, down = peer(h, 1, 0), peer(h, SIDE - 1, 0)
        base = h * 13
        spreads.append(Spread(h, y_ref, back, relay, sems, base))
        passing.append([
            remote(parts.at[h, 1, top], passed.at[h, 0], sems, base + 9, up),
            remote(parts.at[h, 1, low], passed.at[h, 1], sems, base + 10, down),
        ])
        last.append([
            remote(parts.at[h, 0], final.at[h, 0], sems, base + 11, up),
            remote(parts.at[h, 2], final.at[h, 1], sems, base + 12, down),
        ])
    for h in range(2):
        spreads[h].start()
    for h in range(2):
        back[h, 0] = y_ref[h, 0]
    for h in range(2):
        spreads[h].forward()
    for h in range(2):
        spreads[h].finish()

    place = (lax.broadcasted_iota(jnp.int32, (rows, slots), 1) % CAP).astype(f32)
    column = lax.broadcasted_iota(jnp.int32, (META, slots), 0)
    group = lax.broadcasted_iota(jnp.int32, (META, slots), 1) // CAP

    def weigh(h, s):
        meta = near_ref[h, s, :, half:half + META]
        expert = group_expert(h, group)
        take = lambda i: dot(meta, jnp.where(column == expert + i * 4 * GROUPS, 1.0, 0.0).astype(bf16))
        here = take(2) == place
        outs = jnp.concatenate([back[h, g, s * CAP:(s + 1) * CAP] for g in range(GROUPS)], axis=0)
        high = jnp.where(here, take(0), 0.0).astype(bf16)
        rest = jnp.where(here, take(1), 0.0).astype(bf16)
        return dot(high, outs) + dot(rest, outs)

    for h in range(2):
        parts[h, 1] = weigh(h, 2).astype(bf16)
        for copy in passing[h]:
            copy.start()
    sums = [[weigh(h, 1), weigh(h, 3)] for h in range(2)]
    for h in range(2):
        first, second = sums[h]
        passing[h][0].wait_recv()
        parts[h, 0, 0:mid] = (first[0:mid] + passed[h, 0].astype(f32)).astype(bf16)
        parts[h, 0, mid:rows] = first[mid:rows].astype(bf16)
        last[h][0].start()
        passing[h][1].wait_recv()
        parts[h, 2, 0:mid] = second[0:mid].astype(bf16)
        parts[h, 2, mid:rows] = (second[mid:rows] + passed[h, 1].astype(f32)).astype(bf16)
        last[h][1].start()
    mine = [weigh(h, 0) for h in range(2)]
    for h in range(2):
        for copy in last[h]:
            copy.wait_recv()
        cols = slice(h * half, (h + 1) * half)
        out_ref[:, cols] = (
            mixed_ref[:, cols] + (mine[h] + final[h, 0].astype(f32) + final[h, 1].astype(f32))
        ).astype(bf16)
    for h in range(2):
        for copy in passing[h] + last[h]:
            copy.wait_send()


def give_back(y, near, mixed):
    rows, width = mixed.shape
    half = width // 2
    vmem = pl.BlockSpec(memory_space=pltpu.VMEM)
    return pl.pallas_call(
        return_kernel,
        in_specs=[vmem] * 3,
        out_specs=vmem,
        out_shape=jax.ShapeDtypeStruct((rows, width), bf16),
        scratch_shapes=[
            pltpu.VMEM((2, GROUPS, SIDE * CAP, half), bf16),
            pltpu.VMEM((2, 2, SIDE * CAP, half), bf16),
            pltpu.VMEM((2, 3, rows, half), bf16),
            pltpu.VMEM((2, 2, rows // 2, half), bf16),
            pltpu.VMEM((2, 2, rows, half), bf16),
            pltpu.SemaphoreType.DMA((2, 26)),
        ],
        compiler_params=pltpu.CompilerParams(collective_id=2, has_side_effects=True, vmem_limit_bytes=48 * MB),
        name="give_back",
    )(y, near, mixed)


def shards(tokens, routes, history, cache_keys, cache_values, attn_gain, w_query, w_key, w_value, w_out,
           ffn_gain, w_router, expert_gate, expert_up, expert_down):
    rows, width = tokens.shape
    positions = history[0] + jnp.arange(rows, dtype=jnp.int32)
    cosine, sine = rope_tables(positions)
    q, keys_new, values_new = project(tokens, attn_gain[None], w_query, w_key, w_value, cosine, sine)
    attended = attend(history, q, cache_keys, cache_values, keys_new, values_new)
    mixed, pay = finish(attended, w_out, tokens, ffn_gain[None], w_router, routes)
    x, near = dispatch(pay)
    y = run_expert(x, expert_gate, expert_up, expert_down)
    layer_out = give_back(y, near, mixed)
    return layer_out, keys_new, values_new


def solution(mesh):
    both = ("rep", "expert")
    in_specs = (
        P(both, None), P(both, None), P(both), P(both, None, None, None), P(both, None, None, None),
        P(), P(), P(), P(), P(), P(), P(),
        P("expert", None, None), P("expert", None, None), P("expert", None, None),
    )
    out_specs = (P(both, None), P(both, None), P(both, None))
    return jax.shard_map(shards, mesh=mesh, in_specs=in_specs, out_specs=out_specs, check_vma=False)
```

```python
import functools

import jax
import jax.numpy as jnp
from jax import lax
from jax.experimental import pallas as pl
from jax.experimental.pallas import tpu as pltpu
from jax.sharding import PartitionSpec as P

HEADS = 12
KV_HEADS = 2
HEAD_DIM = 128
TOP = 4
SINK = 4
WINDOW = 4096
CAP = 64
EXPERTS = 32

theta_base = 1000000.0
eps_norm = 1e-06

f32 = jnp.float32
bf16 = jnp.bfloat16
MB = 1024 * 1024


def dot(a, b):
    return jnp.dot(a, b, preferred_element_type=f32)


def dot_nt(a, b):
    return lax.dot_general(a, b, (((1,), (1,)), ((), ())), preferred_element_type=f32)


def rope_tables(positions):
    half = HEAD_DIM // 2
    exponent = jnp.arange(half, dtype=f32) * (2.0 / HEAD_DIM)
    inverse_freq = theta_base ** (-exponent)
    angles = positions.astype(f32)[:, None] * inverse_freq[None, :]
    cosine, sine = jnp.cos(angles), jnp.sin(angles)
    return jnp.concatenate([cosine, cosine], 1), jnp.concatenate([-sine, sine], 1)


def norm_rows(x, gain):
    mean_square = jnp.mean(x * x, axis=-1, keepdims=True)
    return (x * lax.rsqrt(mean_square + eps_norm) * gain).astype(bf16)


Q_BLOCK = 512


def qkv_kernel(tok_ref, gain_ref, wq_ref, wk_ref, wv_ref, cos_ref, sin_ref, q_ref, k_ref, v_ref, k2_ref, v2_ref, normed):
    cosine, sine = cos_ref[...], sin_ref[...]

    def rope(x):
        return (x * cosine + pltpu.roll(x, HEAD_DIM // 2, 1) * sine).astype(bf16)

    @pl.when(pl.program_id(0) == 0)
    def _():
        normed[...] = norm_rows(tok_ref[...].astype(f32), gain_ref[0:1])
        keys = dot(normed[...], wk_ref[...])
        for h in range(KV_HEADS):
            turned = rope(keys[:, h * HEAD_DIM:(h + 1) * HEAD_DIM])
            k_ref[:, h * HEAD_DIM:(h + 1) * HEAD_DIM] = turned
            k2_ref[:, h * HEAD_DIM:(h + 1) * HEAD_DIM] = turned
        values = dot(normed[...], wv_ref[...]).astype(bf16)
        v_ref[...] = values
        v2_ref[...] = values

    y = dot(normed[...], wq_ref[...])
    for h in range(Q_BLOCK // HEAD_DIM):
        q_ref[h] = rope(y[:, h * HEAD_DIM:(h + 1) * HEAD_DIM])


def project(tokens, gain, w_query, w_key, w_value, cosine, sine):
    rows, width = tokens.shape
    kv = w_key.shape[1]
    heads = Q_BLOCK // HEAD_DIM
    full = lambda a: pl.BlockSpec(a.shape, lambda i: (0,) * a.ndim)
    return pl.pallas_call(
        qkv_kernel,
        grid=(w_query.shape[1] // Q_BLOCK,),
        in_specs=[
            full(tokens), full(gain),
            pl.BlockSpec((width, Q_BLOCK), lambda i: (0, i)),
            full(w_key), full(w_value), full(cosine), full(sine),
        ],
        out_specs=[
            pl.BlockSpec((heads, rows, HEAD_DIM), lambda i: (i, 0, 0)),
        ] + [pl.BlockSpec((rows, kv), lambda i: (0, 0))] * 4,
        out_shape=[
            jax.ShapeDtypeStruct((HEADS, rows, HEAD_DIM), bf16),
        ] + [jax.ShapeDtypeStruct((rows, kv), bf16)] * 4,
        scratch_shapes=[pltpu.VMEM((rows, width), bf16)],
        compiler_params=pltpu.CompilerParams(vmem_limit_bytes=32 * MB),
        name="project",
    )(tokens, gain, w_query, w_key, w_value, cosine, sine)


KB = 512
HT = 3
EXTRA = 384
SCALE2 = HEAD_DIM ** (-0.5) * 1.4426950408889634
LOW = -1e30


def attn_kernel(past_ref, q_ref, kc_ref, vc_ref, kn_ref, vn_ref, o_ref, s_main, s_tail, m_scr, l_scr, acc, kx, vx):
    rows = kn_ref.shape[0]
    tile = HT * rows
    past = past_ref[0]

    @pl.when(pl.program_id(1) == 0)
    def _():
        for new, cache, out in ((kn_ref, kc_ref, kx), (vn_ref, vc_ref, vx)):
            out[0:rows] = new[...]
            out[rows:EXTRA] = jnp.zeros((EXTRA - rows, HEAD_DIM), bf16)
            out[rows:rows + SINK] = cache[0, 0, WINDOW:WINDOW + SINK]

    q = q_ref[...].reshape(tile, HEAD_DIM)
    row = lax.broadcasted_iota(jnp.int32, (tile, 1), 0) & (rows - 1)
    blocks = jnp.minimum((past + (KB - 1)) // KB, WINDOW // KB)

    def limit(slot):
        back = (slot - past) & (WINDOW - 1)
        return jnp.where(slot < past, jnp.where(slot < SINK, 1 << 20, back), 0)

    def lane_max(s):
        out = s[:, 0:128]
        for c in range(1, s.shape[1] // 128):
            out = jnp.maximum(out, s[:, c * 128:(c + 1) * 128])
        return out

    def lane_sum(s):
        out = s[:, 0:128]
        for c in range(1, s.shape[1] // 128):
            out = out + s[:, c * 128:(c + 1) * 128]
        return out

    column = lax.broadcasted_iota(jnp.int32, (1, EXTRA), 1)
    tail_limit = limit(column + (WINDOW - rows))
    tail_limit = jnp.where(column < rows, rows, jnp.where(column < rows + SINK, tail_limit, 0))
    first_row = jnp.where(column < rows, column, 0)
    s = dot_nt(q, kx[...]) * SCALE2
    s = jnp.where((row >= first_row) & (row < tail_limit), s, LOW)
    s_tail[...] = s
    m_scr[...] = lane_max(s)

    def score(j, carry):
        start = pl.multiple_of(j * KB, KB)
        s = dot_nt(q, kc_ref[0, 0, pl.ds(start, KB), :]) * SCALE2
        offset = (start - past) & (WINDOW - 1)
        plain = (start + KB <= past) & (offset >= rows) & (offset + KB <= WINDOW)

        @pl.when(plain)
        def _():
            s_main[j] = s
            m_scr[...] = jnp.maximum(m_scr[...], lane_max(s))

        @pl.when(jnp.logical_not(plain))
        def _():
            slot = lax.broadcasted_iota(jnp.int32, (1, KB), 1) + start
            masked = jnp.where(row < limit(slot), s, LOW)
            s_main[j] = masked
            m_scr[...] = jnp.maximum(m_scr[...], lane_max(masked))

        return carry

    lax.fori_loop(0, blocks, score, 0)
    top = jnp.max(m_scr[...], axis=1, keepdims=True)
    p = jnp.exp2(s_tail[...] - top)
    l_scr[...] = lane_sum(p)
    acc[...] = dot(p.astype(bf16), vx[...])

    def weigh(j, carry):
        start = pl.multiple_of(j * KB, KB)
        p = jnp.exp2(s_main[j] - top)
        l_scr[...] += lane_sum(p)
        acc[...] += dot(p.astype(bf16), vc_ref[0, 0, pl.ds(start, KB), :])
        return carry

    lax.fori_loop(0, blocks, weigh, 0)
    total = jnp.sum(l_scr[...], axis=1, keepdims=True)
    out = (acc[...] / total).astype(bf16)
    for h in range(HT):
        o_ref[:, h * HEAD_DIM:(h + 1) * HEAD_DIM] = out[h * rows:(h + 1) * rows]


def attend(past, q, cache_keys, cache_values, keys_new, values_new):
    rows = keys_new.shape[0]
    slots = cache_keys.shape[2]
    tile = HT * rows
    per_group = HEADS // KV_HEADS // HT
    cache_spec = pl.BlockSpec((1, 1, slots, HEAD_DIM), lambda g, i, *_: (0, g, 0, 0))
    new_spec = pl.BlockSpec((rows, HEAD_DIM), lambda g, i, *_: (0, g))
    return pl.pallas_call(
        attn_kernel,
        grid_spec=pltpu.PrefetchScalarGridSpec(
            num_scalar_prefetch=1,
            grid=(KV_HEADS, per_group),
            in_specs=[
                pl.BlockSpec((HT, rows, HEAD_DIM), lambda g, i, *_: (g * per_group + i, 0, 0)),
                cache_spec, cache_spec, new_spec, new_spec,
            ],
            out_specs=pl.BlockSpec((rows, HT * HEAD_DIM), lambda g, i, *_: (0, g * per_group + i)),
            scratch_shapes=[
                pltpu.VMEM((WINDOW // KB, tile, KB), f32),
                pltpu.VMEM((tile, EXTRA), f32),
                pltpu.VMEM((tile, 128), f32),
                pltpu.VMEM((tile, 128), f32),
                pltpu.VMEM((tile, HEAD_DIM), f32),
                pltpu.VMEM((EXTRA, HEAD_DIM), bf16),
                pltpu.VMEM((EXTRA, HEAD_DIM), bf16),
            ],
        ),
        out_shape=jax.ShapeDtypeStruct((rows, HEADS * HEAD_DIM), bf16),
        compiler_params=pltpu.CompilerParams(vmem_limit_bytes=48 * MB),
        name="attend",
    )(past, q, cache_keys, cache_values, keys_new, values_new)


O_BLOCK = 512
META = 128


def out_kernel(att_ref, wo_ref, tok_ref, gain_ref, wr_t_ref, routes_t_ref, mixed_ref, pay_ref):
    n = pl.program_id(0)
    rows, width = tok_ref.shape
    steps = width // O_BLOCK
    half = width // 2
    experts = wr_t_ref.shape[0]
    cols = pl.ds(pl.multiple_of(n * O_BLOCK, O_BLOCK), O_BLOCK)
    mixed_ref[:, cols] = tok_ref[:, cols].astype(f32) + dot(att_ref[...], wo_ref[...])

    @pl.when(n == steps - 1)
    def _():
        ffn = norm_rows(mixed_ref[...], gain_ref[1:2])
        expert = lax.broadcasted_iota(jnp.int32, (experts, rows), 0)
        named_t = routes_t_ref[0:1] == expert
        for j in range(1, TOP):
            named_t = named_t | (routes_t_ref[j:j + 1] == expert)
        named_t = jnp.where(named_t, 1.0, 0.0).astype(bf16)
        a = lax.broadcasted_iota(jnp.int32, (rows, rows), 0)
        b = lax.broadcasted_iota(jnp.int32, (rows, rows), 1)
        named = dot_nt(jnp.where(a == b, 1.0, 0.0).astype(bf16), named_t) > 0.5
        ranks = dot_nt(jnp.where(b < a, 1.0, 0.0).astype(bf16), named_t)
        rank = jnp.where(named, ranks, -1.0).astype(bf16)
        score = jnp.where(named, jax.nn.sigmoid(dot_nt(ffn, wr_t_ref[...])), 0.0)
        mix = score / jnp.sum(score, axis=1, keepdims=True)
        high = mix.astype(bf16)
        low = (mix - high.astype(f32)).astype(bf16)
        source = lax.broadcasted_iota(jnp.int32, (experts, META), 0)
        column = lax.broadcasted_iota(jnp.int32, (experts, META), 1)
        put = lambda x, i: dot(x, jnp.where(column == source + i * experts, 1.0, 0.0).astype(bf16))
        meta = (put(high, 0) + put(low, 1) + put(rank, 2)).astype(bf16)
        for h in range(2):
            pay_ref[h, :, 0:half] = ffn[:, h * half:(h + 1) * half]
            pay_ref[h, :, half:half + META] = meta


def finish(attended, w_out, tokens, gain, router_t, routes_t):
    rows, width = tokens.shape
    full = lambda a: pl.BlockSpec(a.shape, lambda n: (0,) * a.ndim)
    return pl.pallas_call(
        out_kernel,
        grid=(width // O_BLOCK,),
        in_specs=[
            full(attended), pl.BlockSpec((width, O_BLOCK), lambda n: (0, n)),
            full(tokens), full(gain), full(router_t), full(routes_t),
        ],
        out_specs=[
            pl.BlockSpec((rows, width), lambda n: (0, 0)),
            pl.BlockSpec((2, rows, width // 2 + META), lambda n: (0, 0, 0)),
        ],
        out_shape=[
            jax.ShapeDtypeStruct((rows, width), f32),
            jax.ShapeDtypeStruct((2, rows, width // 2 + META), bf16),
        ],
        compiler_params=pltpu.CompilerParams(vmem_limit_bytes=32 * MB),
        name="finish",
    )(attended, w_out, tokens, gain, router_t, routes_t)


SIDE = 4
GROUPS = 2 * SIDE


def position():
    me = lax.axis_index("expert")
    return me // (2 * SIDE), (me // 2) % SIDE, me % 2


def peer(axis, step, flip):
    z, y, core = position()
    if axis == 0:
        z = (z + step) % SIDE
    else:
        y = (y + step) % SIDE
    return z * 2 * SIDE + y * 2 + (core + flip) % 2


def remote(src, dst, sems, i, to):
    return pltpu.make_async_remote_copy(
        src_ref=src, dst_ref=dst, send_sem=sems.at[0, i], recv_sem=sems.at[1, i],
        device_id={"expert": to}, device_id_type=pl.DeviceIdType.MESH,
    )


def greet():
    barrier = pltpu.get_barrier_semaphore()
    others = [peer(0, 0, 1)]
    for axis in range(2):
        for step in (1, SIDE - 1):
            for flip in range(2):
                others.append(peer(axis, step, flip))
    for other in others:
        pl.semaphore_signal(barrier, inc=1, device_id={"expert": other}, device_id_type=pl.DeviceIdType.MESH)
    pl.semaphore_wait(barrier, len(others))


def group_expert(h, index):
    z, y, core = position()
    step, flip = index >> 1, index & 1
    if h == 0:
        y = (y + step) & (SIDE - 1)
    else:
        z = (z + step) & (SIDE - 1)
    return z * (2 * SIDE) + y * 2 + ((core + flip) & 1)


class Spread:
    copies = 7

    def __init__(self, h, flip, src, dst, relay, sems, base):
        axis, rows = 1 - h, src.shape[2]
        top, low = pl.ds(0, rows // 2), pl.ds(rows // 2, rows // 2)
        unit = lambda step: (h, step * 2 + flip)
        slot = lambda step: (h, (SIDE - step) % SIDE * 2 + flip)
        self.relays, self.onward = [], []
        for i, (step, part) in enumerate(((1, top), (SIDE - 1, low))):
            self.relays.append(
                remote(src.at[unit(2) + (part,)], relay.at[h, flip, i], sems, base + i, peer(axis, step, 0)))
            self.onward.append(
                remote(relay.at[h, flip, i], dst.at[slot(2) + (part,)], sems, base + 2 + i, peer(axis, step, flip)))
        self.direct = [
            remote(src.at[unit(step)], dst.at[slot(step)], sems, base + 4 + i, peer(axis, step, flip))
            for i, step in enumerate((1, SIDE - 1, 0)[:2 + flip])
        ]

    def forward(self):
        for first, then in zip(self.relays, self.onward):
            first.wait_recv()
            then.start()

    def wait_recv(self):
        for copy in self.direct + self.onward:
            copy.wait_recv()

    def wait_src(self):
        for copy in self.relays + self.direct:
            copy.wait_send()

    def wait_onward(self):
        for copy in self.onward:
            copy.wait_send()


def start(copies):
    for copy in copies:
        copy.start()


def experts_kernel(pay_ref, mixed_ref, gate_hbm, up_hbm, down_hbm, out_ref, near, send, x, relay_out, back, relay_in,
                   sums, parts, passed, final, gate_w, up_w, down_w, own_sem, weight_sem, sems):
    rows, width = mixed_ref.shape
    half = width // 2
    mid = rows // 2
    slots = SIDE * CAP
    top, low = pl.ds(0, mid), pl.ds(mid, mid)
    both = (0, 1)
    weights = [
        pltpu.make_async_copy(src.at[0], dst, weight_sem.at[i])
        for i, (src, dst) in enumerate(((gate_hbm, gate_w), (up_hbm, up_w), (down_hbm, down_w)))
    ]
    own = [pltpu.make_async_copy(pay_ref.at[h], near.at[h, 0], own_sem.at[h]) for h in both]
    start(own)
    greet()
    gather, passing, out, home, pass_back, last = [], [], [], [], [], []
    for h in both:
        up, down = peer(h, 1, 0), peer(h, SIDE - 1, 0)
        base = h * 38
        gather.append([
            remote(pay_ref.at[h, top], near.at[h, 3, top], sems, base, up),
            remote(pay_ref.at[h, low], near.at[h, 1, low], sems, base + 1, down),
            remote(pay_ref.at[h, low], near.at[h, 3, low], sems, base + 2, up),
            remote(pay_ref.at[h, top], near.at[h, 1, top], sems, base + 3, down),
        ])
        passing.append([
            remote(near.at[h, 3, top], near.at[h, 2, top], sems, base + 4, up),
            remote(near.at[h, 1, low], near.at[h, 2, low], sems, base + 5, down),
        ])
        out.append([Spread(h, d, send, x, relay_out, sems, base + 6 + d * Spread.copies) for d in both])
        home.append([Spread(h, d, send, back, relay_in, sems, base + 20 + d * Spread.copies) for d in both])
        pass_back.append([
            remote(parts.at[h, 1, top], passed.at[h, 0], sems, base + 34, up),
            remote(parts.at[h, 1, low], passed.at[h, 1], sems, base + 35, down),
        ])
        last.append([
            remote(parts.at[h, 0], final.at[h, 0], sems, base + 36, up),
            remote(parts.at[h, 2], final.at[h, 1], sems, base + 37, down),
        ])

    for i in range(4):
        for h in both:
            gather[h][i].start()
    start(weights)

    place = (lax.broadcasted_iota(jnp.int32, (slots, rows), 0) % CAP).astype(f32)
    step_rows = (lax.broadcasted_iota(jnp.int32, (slots, META), 0) // CAP) * 2
    meta_column = lax.broadcasted_iota(jnp.int32, (slots, META), 1)

    def choose(h, s, d):
        spread = jnp.where(meta_column == group_expert(h, step_rows + d) + 2 * EXPERTS, 1.0, 0.0).astype(bf16)
        wanted = dot_nt(spread, near[h, s, :, half:half + META])
        select = jnp.where(wanted == place, 1.0, 0.0).astype(bf16)
        chosen = dot(select, near[h, s, :, 0:half]).astype(bf16)
        for k in range(SIDE):
            send[h, 2 * k + d, s * CAP:(s + 1) * CAP] = chosen[k * CAP:(k + 1) * CAP]

    for h in both:
        own[h].wait()
        for d in both:
            choose(h, 0, d)
    for i in both:
        for h in both:
            gather[h][i].wait_recv()
            passing[h][i].start()
    for i, s in ((2, 3), (3, 1)):
        for h in both:
            gather[h][i].wait_recv()
            for d in both:
                choose(h, s, d)
    for h in both:
        for copy in passing[h]:
            copy.wait_recv()
        choose(h, 2, 0)
        start(out[h][0].relays + out[h][0].direct)
    for h in both:
        choose(h, 2, 1)
        start(out[h][1].relays)
    for h in both:
        x[h, 0] = send[h, 0]
    for d in both:
        for h in both:
            out[h][d].forward()
    for h in both:
        start(out[h][1].direct)
    for copy in weights:
        copy.wait()

    def run_expert(d):
        def block(k, carry):
            spot = pl.ds(pl.multiple_of(k * CAP, CAP), CAP)
            a = x[0, 2 * k + d]
            b = jnp.concatenate([x[1, 2 * s + d, spot] for s in range(SIDE)], axis=0)
            gate = dot(a, gate_w[0:half]) + dot(b, gate_w[half:2 * half])
            up = dot(a, up_w[0:half]) + dot(b, up_w[half:2 * half])
            hidden = (jnp.maximum(gate, 0.0) * up).astype(bf16)
            send[0, 2 * k + d] = dot(hidden, down_w[:, 0:half]).astype(bf16)
            other = dot(hidden, down_w[:, half:2 * half]).astype(bf16)
            for s in range(SIDE):
                send[1, 2 * s + d, spot] = other[s * CAP:(s + 1) * CAP]
            return carry

        for h in both:
            out[h][d].wait_recv()
            out[h][d].wait_src()
        lax.fori_loop(0, SIDE, block, 0)

    run_expert(0)
    for h in both:
        start(home[h][0].relays + home[h][0].direct)
    run_expert(1)
    for h in both:
        start(home[h][1].relays)
    for h in both:
        back[h, 0] = send[h, 0]
    for d in both:
        for h in both:
            home[h][d].forward()
    for h in both:
        start(home[h][1].direct)

    place_back = (lax.broadcasted_iota(jnp.int32, (rows, slots), 1) % CAP).astype(f32)
    meta_row = lax.broadcasted_iota(jnp.int32, (META, slots), 0)
    step_columns = (lax.broadcasted_iota(jnp.int32, (META, slots), 1) // CAP) * 2

    def weigh(h, s, d):
        meta = near[h, s, :, half:half + META]
        expert = group_expert(h, step_columns + d)
        take = lambda i: dot(meta, jnp.where(meta_row == expert + i * EXPERTS, 1.0, 0.0).astype(bf16))
        here = take(2) == place_back
        outs = jnp.concatenate([back[h, 2 * k + d, s * CAP:(s + 1) * CAP] for k in range(SIDE)], axis=0)
        high = jnp.where(here, take(0), 0.0).astype(bf16)
        rest = jnp.where(here, take(1), 0.0).astype(bf16)
        return dot(high, outs) + dot(rest, outs)

    for h in both:
        home[h][0].wait_recv()
        for s in range(SIDE):
            sums[h, s] = weigh(h, s, 0)
    for h in both:
        home[h][1].wait_recv()
        parts[h, 1] = (sums[h, 2] + weigh(h, 2, 1)).astype(bf16)
        start(pass_back[h])
    for h in both:
        for s in (1, 3):
            sums[h, s] += weigh(h, s, 1)
    for h in both:
        pass_back[h][0].wait_recv()
        parts[h, 0, 0:mid] = (sums[h, 1, 0:mid] + passed[h, 0].astype(f32)).astype(bf16)
        parts[h, 0, mid:rows] = sums[h, 1, mid:rows].astype(bf16)
        last[h][0].start()
        pass_back[h][1].wait_recv()
        parts[h, 2, 0:mid] = sums[h, 3, 0:mid].astype(bf16)
        parts[h, 2, mid:rows] = (sums[h, 3, mid:rows] + passed[h, 1].astype(f32)).astype(bf16)
        last[h][1].start()
    for h in both:
        sums[h, 0] += weigh(h, 0, 1)
    for h in both:
        for copy in last[h]:
            copy.wait_recv()
        cols = slice(h * half, (h + 1) * half)
        out_ref[:, cols] = (
            mixed_ref[:, cols] + (sums[h, 0] + final[h, 0].astype(f32) + final[h, 1].astype(f32))
        ).astype(bf16)
    for h in both:
        for copy in gather[h] + passing[h] + pass_back[h] + last[h]:
            copy.wait_send()
        for d in both:
            out[h][d].wait_onward()
            home[h][d].wait_src()
            home[h][d].wait_onward()


def run_experts(pay, mixed, gate, up, down):
    rows, width = mixed.shape
    half, ff = width // 2, gate.shape[2]
    vmem = pl.BlockSpec(memory_space=pltpu.VMEM)
    hbm = pl.BlockSpec(memory_space=pl.ANY)
    unit = (SIDE * CAP, half)
    part = (SIDE * CAP // 2, half)
    return pl.pallas_call(
        experts_kernel,
        in_specs=[vmem, vmem, hbm, hbm, hbm],
        out_specs=vmem,
        out_shape=jax.ShapeDtypeStruct((rows, width), bf16),
        scratch_shapes=[
            pltpu.VMEM((2, SIDE, rows, half + META), bf16),
            pltpu.VMEM((2, GROUPS) + unit, bf16),
            pltpu.VMEM((2, GROUPS) + unit, bf16),
            pltpu.VMEM((2, 2, 2) + part, bf16),
            pltpu.VMEM((2, GROUPS) + unit, bf16),
            pltpu.VMEM((2, 2, 2) + part, bf16),
            pltpu.VMEM((2, SIDE, rows, half), f32),
            pltpu.VMEM((2, 3, rows, half), bf16),
            pltpu.VMEM((2, 2, rows // 2, half), bf16),
            pltpu.VMEM((2, 2, rows, half), bf16),
            pltpu.VMEM((width, ff), bf16),
            pltpu.VMEM((width, ff), bf16),
            pltpu.VMEM((ff, width), bf16),
            pltpu.SemaphoreType.DMA((2,)),
            pltpu.SemaphoreType.DMA((3,)),
            pltpu.SemaphoreType.DMA((2, 76)),
        ],
        compiler_params=pltpu.CompilerParams(collective_id=1, has_side_effects=True, vmem_limit_bytes=50 * MB),
        name="experts",
    )(pay, mixed, gate, up, down)


def shards(tokens, routes, history, cache_keys, cache_values, attn_gain, w_query, w_key, w_value, w_out,
           ffn_gain, w_router, expert_gate, expert_up, expert_down):
    rows, width = tokens.shape
    positions = history[0] + jnp.arange(rows, dtype=jnp.int32)
    cosine, sine = rope_tables(positions)
    gains = jnp.stack([attn_gain, ffn_gain]).astype(f32)
    q, keys_new, values_new, keys_near, values_near = project(tokens, gains, w_query, w_key, w_value, cosine, sine)
    attended = attend(history, q, cache_keys, cache_values, keys_near, values_near)
    mixed, pay = finish(attended, w_out, tokens, gains, jnp.transpose(w_router), jnp.transpose(routes))
    layer_out = run_experts(pay, mixed, expert_gate, expert_up, expert_down)
    return layer_out, keys_new, values_new


def solution(mesh):
    both = ("rep", "expert")
    in_specs = (
        P(both, None), P(both, None), P(both), P(both, None, None, None), P(both, None, None, None),
        P(), P(), P(), P(), P(), P(), P(),
        P("expert", None, None), P("expert", None, None), P("expert", None, None),
    )
    out_specs = (P(both, None), P(both, None), P(both, None))
    return jax.shard_map(shards, mesh=mesh, in_specs=in_specs, out_specs=out_specs, check_vma=False)
```

```python
import functools

import jax
import jax.numpy as jnp
from jax import lax
from jax.experimental import pallas as pl
from jax.experimental.pallas import tpu as pltpu
from jax.sharding import PartitionSpec as P

HEADS = 12
KV_HEADS = 2
HEAD_DIM = 128
TOP = 4
SINK = 4
WINDOW = 4096
CAP = 64
EXPERTS = 32

theta_base = 1000000.0
eps_norm = 1e-06

f32 = jnp.float32
bf16 = jnp.bfloat16
MB = 1024 * 1024


def dot(a, b):
    return jnp.dot(a, b, preferred_element_type=f32)


def dot_nt(a, b):
    return lax.dot_general(a, b, (((1,), (1,)), ((), ())), preferred_element_type=f32)


def rope_tables(positions):
    half = HEAD_DIM // 2
    exponent = jnp.arange(half, dtype=f32) * (2.0 / HEAD_DIM)
    inverse_freq = theta_base ** (-exponent)
    angles = positions.astype(f32)[:, None] * inverse_freq[None, :]
    cosine, sine = jnp.cos(angles), jnp.sin(angles)
    return jnp.concatenate([cosine, cosine], 1), jnp.concatenate([-sine, sine], 1)


def norm_rows(x, gain):
    mean_square = jnp.mean(x * x, axis=-1, keepdims=True)
    return (x * lax.rsqrt(mean_square + eps_norm) * gain).astype(bf16)


Q_BLOCK = 512


def qkv_kernel(tok_ref, gain_ref, wq_ref, wk_ref, wv_ref, cos_ref, sin_ref, q_ref, k_ref, v_ref, k2_ref, v2_ref, normed):
    cosine, sine = cos_ref[...], sin_ref[...]

    def rope(x):
        return (x * cosine + pltpu.roll(x, HEAD_DIM // 2, 1) * sine).astype(bf16)

    @pl.when(pl.program_id(0) == 0)
    def _():
        normed[...] = norm_rows(tok_ref[...].astype(f32), gain_ref[0:1])
        keys = dot(normed[...], wk_ref[...])
        for h in range(KV_HEADS):
            turned = rope(keys[:, h * HEAD_DIM:(h + 1) * HEAD_DIM])
            k_ref[:, h * HEAD_DIM:(h + 1) * HEAD_DIM] = turned
            k2_ref[:, h * HEAD_DIM:(h + 1) * HEAD_DIM] = turned
        values = dot(normed[...], wv_ref[...]).astype(bf16)
        v_ref[...] = values
        v2_ref[...] = values

    y = dot(normed[...], wq_ref[...])
    for h in range(Q_BLOCK // HEAD_DIM):
        q_ref[h] = rope(y[:, h * HEAD_DIM:(h + 1) * HEAD_DIM])


def project(tokens, gain, w_query, w_key, w_value, cosine, sine):
    rows, width = tokens.shape
    kv = w_key.shape[1]
    heads = Q_BLOCK // HEAD_DIM
    full = lambda a: pl.BlockSpec(a.shape, lambda i: (0,) * a.ndim)
    return pl.pallas_call(
        qkv_kernel,
        grid=(w_query.shape[1] // Q_BLOCK,),
        in_specs=[
            full(tokens), full(gain),
            pl.BlockSpec((width, Q_BLOCK), lambda i: (0, i)),
            full(w_key), full(w_value), full(cosine), full(sine),
        ],
        out_specs=[
            pl.BlockSpec((heads, rows, HEAD_DIM), lambda i: (i, 0, 0)),
        ] + [pl.BlockSpec((rows, kv), lambda i: (0, 0))] * 4,
        out_shape=[
            jax.ShapeDtypeStruct((HEADS, rows, HEAD_DIM), bf16),
        ] + [jax.ShapeDtypeStruct((rows, kv), bf16)] * 4,
        scratch_shapes=[pltpu.VMEM((rows, width), bf16)],
        compiler_params=pltpu.CompilerParams(vmem_limit_bytes=32 * MB),
        name="project",
    )(tokens, gain, w_query, w_key, w_value, cosine, sine)


KB = 1024
HT = 6
EXTRA = 384
SCALE2 = HEAD_DIM ** (-0.5) * 1.4426950408889634
LOW = -1e30


def attn_kernel(past_ref, q_ref, kc_ref, vc_ref, kn_ref, vn_ref, o_ref, s_main, s_tail, m_scr, l_scr, acc, kx, vx):
    rows = kn_ref.shape[0]
    tile = HT * rows
    past = past_ref[0]

    @pl.when(pl.program_id(1) == 0)
    def _():
        for new, cache, out in ((kn_ref, kc_ref, kx), (vn_ref, vc_ref, vx)):
            out[0:rows] = new[...]
            out[rows:EXTRA] = jnp.zeros((EXTRA - rows, HEAD_DIM), bf16)
            out[rows:rows + SINK] = cache[0, 0, WINDOW:WINDOW + SINK]

    q = q_ref[...].reshape(tile, HEAD_DIM)
    row = lax.broadcasted_iota(jnp.int32, (tile, 1), 0) & (rows - 1)
    blocks = jnp.minimum((past + (KB - 1)) // KB, WINDOW // KB)

    def limit(slot):
        back = (slot - past) & (WINDOW - 1)
        return jnp.where(slot < past, jnp.where(slot < SINK, 1 << 20, back), 0)

    def lane_max(s):
        out = s[:, 0:128]
        for c in range(1, s.shape[1] // 128):
            out = jnp.maximum(out, s[:, c * 128:(c + 1) * 128])
        return out

    def lane_sum(s):
        out = s[:, 0:128]
        for c in range(1, s.shape[1] // 128):
            out = out + s[:, c * 128:(c + 1) * 128]
        return out

    column = lax.broadcasted_iota(jnp.int32, (1, EXTRA), 1)
    tail_limit = limit(column + (WINDOW - rows))
    tail_limit = jnp.where(column < rows, rows, jnp.where(column < rows + SINK, tail_limit, 0))
    first_row = jnp.where(column < rows, column, 0)
    s = dot_nt(q, kx[...]) * SCALE2
    s = jnp.where((row >= first_row) & (row < tail_limit), s, LOW)
    s_tail[...] = s
    m_scr[...] = lane_max(s)

    def score(j, carry):
        start = pl.multiple_of(j * KB, KB)
        raw = lambda: dot_nt(q, kc_ref[0, 0, pl.ds(start, KB), :]) * SCALE2
        offset = (start - past) & (WINDOW - 1)
        plain = (start + KB <= past) & (offset >= rows) & (offset + KB <= WINDOW)

        @pl.when(plain)
        def _():
            s = raw()
            s_main[j] = s
            m_scr[...] = jnp.maximum(m_scr[...], lane_max(s))

        @pl.when(jnp.logical_not(plain))
        def _():
            slot = lax.broadcasted_iota(jnp.int32, (1, KB), 1) + start
            s = jnp.where(row < limit(slot), raw(), LOW)
            s_main[j] = s
            m_scr[...] = jnp.maximum(m_scr[...], lane_max(s))

        return carry

    lax.fori_loop(0, blocks, score, 0)
    top = jnp.max(m_scr[...], axis=1, keepdims=True)
    p = jnp.exp2(s_tail[...] - top)
    l_scr[...] = lane_sum(p)
    acc[...] = dot(p.astype(bf16), vx[...])

    def weigh(j, carry):
        start = pl.multiple_of(j * KB, KB)
        p = jnp.exp2(s_main[j] - top)
        l_scr[...] += lane_sum(p)
        acc[...] += dot(p.astype(bf16), vc_ref[0, 0, pl.ds(start, KB), :])
        return carry

    lax.fori_loop(0, blocks, weigh, 0)
    total = jnp.sum(l_scr[...], axis=1, keepdims=True)
    out = (acc[...] / total).astype(bf16)
    for h in range(HT):
        o_ref[:, h * HEAD_DIM:(h + 1) * HEAD_DIM] = out[h * rows:(h + 1) * rows]


def attend(past, q, cache_keys, cache_values, keys_new, values_new):
    rows = keys_new.shape[0]
    slots = cache_keys.shape[2]
    tile = HT * rows
    per_group = HEADS // KV_HEADS // HT
    cache_spec = pl.BlockSpec((1, 1, slots, HEAD_DIM), lambda g, i, *_: (0, g, 0, 0))
    new_spec = pl.BlockSpec((rows, HEAD_DIM), lambda g, i, *_: (0, g))
    return pl.pallas_call(
        attn_kernel,
        grid_spec=pltpu.PrefetchScalarGridSpec(
            num_scalar_prefetch=1,
            grid=(KV_HEADS, per_group),
            in_specs=[
                pl.BlockSpec((HT, rows, HEAD_DIM), lambda g, i, *_: (g * per_group + i, 0, 0)),
                cache_spec, cache_spec, new_spec, new_spec,
            ],
            out_specs=pl.BlockSpec((rows, HT * HEAD_DIM), lambda g, i, *_: (0, g * per_group + i)),
            scratch_shapes=[
                pltpu.VMEM((WINDOW // KB, tile, KB), f32),
                pltpu.VMEM((tile, EXTRA), f32),
                pltpu.VMEM((tile, 128), f32),
                pltpu.VMEM((tile, 128), f32),
                pltpu.VMEM((tile, HEAD_DIM), f32),
                pltpu.VMEM((EXTRA, HEAD_DIM), bf16),
                pltpu.VMEM((EXTRA, HEAD_DIM), bf16),
            ],
        ),
        out_shape=jax.ShapeDtypeStruct((rows, HEADS * HEAD_DIM), bf16),
        compiler_params=pltpu.CompilerParams(vmem_limit_bytes=48 * MB),
        name="attend",
    )(past, q, cache_keys, cache_values, keys_new, values_new)


O_BLOCK = 512
META = 128


def out_kernel(att_ref, wo_ref, tok_ref, gain_ref, wr_t_ref, routes_t_ref, mixed_ref, pay_ref):
    n = pl.program_id(0)
    rows, width = tok_ref.shape
    steps = width // O_BLOCK
    half = width // 2
    experts = wr_t_ref.shape[0]
    cols = pl.ds(pl.multiple_of(n * O_BLOCK, O_BLOCK), O_BLOCK)
    mixed_ref[:, cols] = tok_ref[:, cols].astype(f32) + dot(att_ref[...], wo_ref[...])

    @pl.when(n == steps - 1)
    def _():
        ffn = norm_rows(mixed_ref[...], gain_ref[1:2])
        expert = lax.broadcasted_iota(jnp.int32, (experts, rows), 0)
        named_t = routes_t_ref[0:1] == expert
        for j in range(1, TOP):
            named_t = named_t | (routes_t_ref[j:j + 1] == expert)
        named_t = jnp.where(named_t, 1.0, 0.0).astype(bf16)
        a = lax.broadcasted_iota(jnp.int32, (rows, rows), 0)
        b = lax.broadcasted_iota(jnp.int32, (rows, rows), 1)
        named = dot_nt(jnp.where(a == b, 1.0, 0.0).astype(bf16), named_t) > 0.5
        ranks = dot_nt(jnp.where(b < a, 1.0, 0.0).astype(bf16), named_t)
        rank = jnp.where(named, ranks, -1.0).astype(bf16)
        score = jnp.where(named, jax.nn.sigmoid(dot_nt(ffn, wr_t_ref[...])), 0.0)
        mix = score / jnp.sum(score, axis=1, keepdims=True)
        high = mix.astype(bf16)
        low = (mix - high.astype(f32)).astype(bf16)
        source = lax.broadcasted_iota(jnp.int32, (experts, META), 0)
        column = lax.broadcasted_iota(jnp.int32, (experts, META), 1)
        put = lambda x, i: dot(x, jnp.where(column == source + i * experts, 1.0, 0.0).astype(bf16))
        meta = (put(high, 0) + put(low, 1) + put(rank, 2)).astype(bf16)
        for h in range(2):
            pay_ref[h, :, 0:half] = ffn[:, h * half:(h + 1) * half]
            pay_ref[h, :, half:half + META] = meta


def finish(attended, w_out, tokens, gain, router_t, routes_t):
    rows, width = tokens.shape
    full = lambda a: pl.BlockSpec(a.shape, lambda n: (0,) * a.ndim)
    return pl.pallas_call(
        out_kernel,
        grid=(width // O_BLOCK,),
        in_specs=[
            full(attended), pl.BlockSpec((width, O_BLOCK), lambda n: (0, n)),
            full(tokens), full(gain), full(router_t), full(routes_t),
        ],
        out_specs=[
            pl.BlockSpec((rows, width), lambda n: (0, 0)),
            pl.BlockSpec((2, rows, width // 2 + META), lambda n: (0, 0, 0)),
        ],
        out_shape=[
            jax.ShapeDtypeStruct((rows, width), f32),
            jax.ShapeDtypeStruct((2, rows, width // 2 + META), bf16),
        ],
        compiler_params=pltpu.CompilerParams(vmem_limit_bytes=32 * MB),
        name="finish",
    )(attended, w_out, tokens, gain, router_t, routes_t)


SIDE = 4
GROUPS = 2 * SIDE


def position():
    me = lax.axis_index("expert")
    return me // (2 * SIDE), (me // 2) % SIDE, me % 2


def peer(axis, step, flip):
    z, y, core = position()
    if axis == 0:
        z = (z + step) % SIDE
    else:
        y = (y + step) % SIDE
    return z * 2 * SIDE + y * 2 + (core + flip) % 2


def remote(src, dst, sems, i, to):
    return pltpu.make_async_remote_copy(
        src_ref=src, dst_ref=dst, send_sem=sems.at[0, i], recv_sem=sems.at[1, i],
        device_id={"expert": to}, device_id_type=pl.DeviceIdType.MESH,
    )


def greet():
    barrier = pltpu.get_barrier_semaphore()
    others = [peer(0, 0, 1)]
    for axis in range(2):
        for step in (1, SIDE - 1):
            for flip in range(2):
                others.append(peer(axis, step, flip))
    for other in others:
        pl.semaphore_signal(barrier, inc=1, device_id={"expert": other}, device_id_type=pl.DeviceIdType.MESH)
    pl.semaphore_wait(barrier, len(others))


def group_expert(h, index):
    z, y, core = position()
    step, flip = index >> 1, index & 1
    if h == 0:
        y = (y + step) & (SIDE - 1)
    else:
        z = (z + step) & (SIDE - 1)
    return z * (2 * SIDE) + y * 2 + ((core + flip) & 1)


def lane(s):
    return (3 * s) % SIDE


class Spread:
    copies = 10

    def __init__(self, h, flip, src, dst, relay, sems, base, split=False):
        axis, rows = 1 - h, src.shape[2]
        top, low = pl.ds(0, rows // 2), pl.ds(rows // 2, rows // 2)
        unit = lambda step: (h, step * 2 + flip)
        slot = lambda step: (h, (SIDE - step) % SIDE * 2 + flip)
        ways = (1, SIDE - 1) if flip == 0 else (SIDE - 1, 1)
        self.relays, self.onward = [], []
        for i, (step, part) in enumerate(zip(ways, (top, low))):
            self.relays.append(
                remote(src.at[unit(2) + (part,)], relay.at[h, flip, i], sems, base + i, peer(axis, step, 0)))
            self.onward.append(
                remote(relay.at[h, flip, i], dst.at[slot(2) + (part,)], sems, base + 2 + i, peer(axis, step, flip)))
        steps = (1, SIDE - 1, 0)[:2 + flip]
        parts = ((low,), (top,)) if split else ((),)
        self.direct = [
            [
                remote(src.at[unit(step) + part], dst.at[slot(step) + part], sems,
                       base + 4 + i * len(steps) + j, peer(axis, step, flip))
                for j, step in enumerate(steps)
            ]
            for i, part in enumerate(parts)
        ]

    def forward(self, i):
        self.relays[i].wait_recv()
        self.onward[i].start()

    def wait_part(self, i):
        for copy in self.direct[i] + [self.onward[1 - i]]:
            copy.wait_recv()

    def wait_recv(self):
        for copy in sum(self.direct, []) + self.onward:
            copy.wait_recv()

    def wait_src(self):
        for copy in self.relays + sum(self.direct, []):
            copy.wait_send()

    def wait_onward(self):
        for copy in self.onward:
            copy.wait_send()


def start(copies):
    for copy in copies:
        copy.start()


def experts_kernel(pay_ref, mixed_ref, gate_hbm, up_hbm, down_hbm, out_ref, near, send, x, relay_out, back, relay_in,
                   sums, parts, passed, final, gate_w, up_w, down_w, own_sem, weight_sem, sems):
    rows, width = mixed_ref.shape
    half = width // 2
    mid = rows // 2
    slots = SIDE * CAP
    top, low = pl.ds(0, mid), pl.ds(mid, mid)
    both = (0, 1)
    weights = [
        pltpu.make_async_copy(src.at[0], dst, weight_sem.at[i])
        for i, (src, dst) in enumerate(((gate_hbm, gate_w), (up_hbm, up_w), (down_hbm, down_w)))
    ]
    own = [pltpu.make_async_copy(pay_ref.at[h], near.at[h, 0], own_sem.at[h]) for h in both]
    start(own)
    greet()
    gather, passing, out, home, pass_back, last = [], [], [], [], [], []
    for h in both:
        up, down = peer(h, 1, 0), peer(h, SIDE - 1, 0)
        base = h * 54
        gather.append([
            remote(pay_ref.at[h, top], near.at[h, 3, top], sems, base, up),
            remote(pay_ref.at[h, low], near.at[h, 1, low], sems, base + 1, down),
            remote(pay_ref.at[h, low], near.at[h, 3, low], sems, base + 2, up),
            remote(pay_ref.at[h, top], near.at[h, 1, top], sems, base + 3, down),
        ])
        passing.append([
            remote(near.at[h, 3, top], near.at[h, 2, top], sems, base + 4, up),
            remote(near.at[h, 1, low], near.at[h, 2, low], sems, base + 5, down),
        ])
        out.append([Spread(h, d, send, x, relay_out, sems, base + 6 + d * Spread.copies) for d in both])
        home.append([
            Spread(h, d, send, back, relay_in, sems, base + 26 + d * Spread.copies, split=d == 1) for d in both
        ])
        pass_back.append([
            remote(parts.at[h, 1, top], passed.at[h, 0], sems, base + 46, up),
            remote(parts.at[h, 1, low], passed.at[h, 1], sems, base + 47, down),
        ])
        last.append([
            remote(parts.at[h, 0, low], final.at[h, 0, low], sems, base + 48, up),
            remote(parts.at[h, 2, top], final.at[h, 1, top], sems, base + 49, down),
            remote(parts.at[h, 0, top], final.at[h, 0, top], sems, base + 50, up),
            remote(parts.at[h, 2, low], final.at[h, 1, low], sems, base + 51, down),
        ])

    for i in range(4):
        for h in both:
            gather[h][i].start()
    start(weights)

    place = (lax.broadcasted_iota(jnp.int32, (slots, rows), 0) % CAP).astype(f32)
    step_rows = (lax.broadcasted_iota(jnp.int32, (slots, META), 0) // CAP) * 2
    meta_column = lax.broadcasted_iota(jnp.int32, (slots, META), 1)

    def choose(h, s, d):
        spread = jnp.where(meta_column == group_expert(h, step_rows + d) + 2 * EXPERTS, 1.0, 0.0).astype(bf16)
        wanted = dot_nt(spread, near[h, s, :, half:half + META])
        select = jnp.where(wanted == place, 1.0, 0.0).astype(bf16)
        chosen = dot(select, near[h, s, :, 0:half]).astype(bf16)
        for k in range(SIDE):
            send[h, 2 * k + d, lane(s) * CAP:(lane(s) + 1) * CAP] = chosen[k * CAP:(k + 1) * CAP]

    for h in both:
        own[h].wait()
        for d in both:
            choose(h, 0, d)
    for i in both:
        for h in both:
            gather[h][i].wait_recv()
            passing[h][i].start()
    for h in both:
        gather[h][2].wait_recv()
        for d in both:
            choose(h, 3, d)
        start([out[h][d].relays[0] for d in both])
    for h in both:
        gather[h][3].wait_recv()
        for d in both:
            choose(h, 1, d)
    for h in both:
        for copy in passing[h]:
            copy.wait_recv()
        choose(h, 2, 0)
        start([out[h][0].relays[1]] + out[h][0].direct[0])
    for h in both:
        choose(h, 2, 1)
        start([out[h][1].relays[1]])
    for h in both:
        x[h, 0] = send[h, 0]
    for i in both:
        for d in both:
            for h in both:
                out[h][d].forward(i)
    for h in both:
        start(out[h][1].direct[0])
    for copy in weights:
        copy.wait()

    def run_expert(d):
        def block(k, carry):
            spot = pl.ds(pl.multiple_of(lane(k) * CAP, CAP), CAP)
            a = x[0, 2 * k + d]
            b = jnp.concatenate([x[1, 2 * lane(i) + d, spot] for i in range(SIDE)], axis=0)
            gate = dot(a, gate_w[0:half]) + dot(b, gate_w[half:2 * half])
            up = dot(a, up_w[0:half]) + dot(b, up_w[half:2 * half])
            hidden = (jnp.maximum(gate, 0.0) * up).astype(bf16)
            send[0, 2 * k + d] = dot(hidden, down_w[:, 0:half]).astype(bf16)
            other = dot(hidden, down_w[:, half:2 * half]).astype(bf16)
            for i in range(SIDE):
                send[1, 2 * lane(i) + d, spot] = other[i * CAP:(i + 1) * CAP]
            return carry

        for h in both:
            out[h][d].wait_recv()
            out[h][d].wait_src()
        lax.fori_loop(0, SIDE, block, 0)

    run_expert(0)
    for h in both:
        start(home[h][0].relays + home[h][0].direct[0])
    run_expert(1)
    for h in both:
        start(home[h][1].relays[::-1])
    for i in both:
        for h in both:
            home[h][0].forward(i)
    for h in both:
        start(home[h][1].direct[0])
    for h in both:
        back[h, 0] = send[h, 0]
    for i in (1, 0):
        for h in both:
            home[h][1].forward(i)
    for h in both:
        start(home[h][1].direct[1])

    place_back = (lax.broadcasted_iota(jnp.int32, (rows, slots), 1) % CAP).astype(f32)
    meta_row = lax.broadcasted_iota(jnp.int32, (META, slots), 0)
    step_columns = (lax.broadcasted_iota(jnp.int32, (META, slots), 1) // CAP) * 2

    def weigh(h, s, d):
        meta = near[h, s, :, half:half + META]
        expert = group_expert(h, step_columns + d)
        take = lambda i: dot(meta, jnp.where(meta_row == expert + i * EXPERTS, 1.0, 0.0).astype(bf16))
        here = take(2) == place_back
        outs = jnp.concatenate([back[h, 2 * k + d, lane(s) * CAP:(lane(s) + 1) * CAP] for k in range(SIDE)], axis=0)
        high = jnp.where(here, take(0), 0.0).astype(bf16)
        rest = jnp.where(here, take(1), 0.0).astype(bf16)
        return dot(high, outs) + dot(rest, outs)

    for h in both:
        home[h][0].wait_recv()
        for s in range(SIDE):
            sums[h, s] = weigh(h, s, 0)
    for h in both:
        home[h][1].wait_part(0)
        parts[h, 1] = (sums[h, 2] + weigh(h, 2, 1)).astype(bf16)
        start(pass_back[h])
    for h in both:
        sums[h, 1] += weigh(h, 1, 1)
        parts[h, 0, mid:rows] = sums[h, 1, mid:rows].astype(bf16)
        last[h][0].start()
    for h in both:
        home[h][1].wait_part(1)
        sums[h, 3] += weigh(h, 3, 1)
        parts[h, 2, 0:mid] = sums[h, 3, 0:mid].astype(bf16)
        last[h][1].start()
    for h in both:
        pass_back[h][0].wait_recv()
        parts[h, 0, 0:mid] = (sums[h, 1, 0:mid] + passed[h, 0].astype(f32)).astype(bf16)
        last[h][2].start()
        pass_back[h][1].wait_recv()
        parts[h, 2, mid:rows] = (sums[h, 3, mid:rows] + passed[h, 1].astype(f32)).astype(bf16)
        last[h][3].start()
    for h in both:
        sums[h, 0] += weigh(h, 0, 1)
    for h in both:
        for copy in last[h]:
            copy.wait_recv()
        cols = slice(h * half, (h + 1) * half)
        out_ref[:, cols] = (
            mixed_ref[:, cols] + (sums[h, 0] + final[h, 0].astype(f32) + final[h, 1].astype(f32))
        ).astype(bf16)
    for h in both:
        for copy in gather[h] + passing[h] + pass_back[h] + last[h]:
            copy.wait_send()
        for d in both:
            out[h][d].wait_onward()
            home[h][d].wait_src()
            home[h][d].wait_onward()


def run_experts(pay, mixed, gate, up, down):
    rows, width = mixed.shape
    half, ff = width // 2, gate.shape[2]
    vmem = pl.BlockSpec(memory_space=pltpu.VMEM)
    hbm = pl.BlockSpec(memory_space=pl.ANY)
    unit = (SIDE * CAP, half)
    part = (SIDE * CAP // 2, half)
    return pl.pallas_call(
        experts_kernel,
        in_specs=[vmem, vmem, hbm, hbm, hbm],
        out_specs=vmem,
        out_shape=jax.ShapeDtypeStruct((rows, width), bf16),
        scratch_shapes=[
            pltpu.VMEM((2, SIDE, rows, half + META), bf16),
            pltpu.VMEM((2, GROUPS) + unit, bf16),
            pltpu.VMEM((2, GROUPS) + unit, bf16),
            pltpu.VMEM((2, 2, 2) + part, bf16),
            pltpu.VMEM((2, GROUPS) + unit, bf16),
            pltpu.VMEM((2, 2, 2) + part, bf16),
            pltpu.VMEM((2, SIDE, rows, half), f32),
            pltpu.VMEM((2, 3, rows, half), bf16),
            pltpu.VMEM((2, 2, rows // 2, half), bf16),
            pltpu.VMEM((2, 2, rows, half), bf16),
            pltpu.VMEM((width, ff), bf16),
            pltpu.VMEM((width, ff), bf16),
            pltpu.VMEM((ff, width), bf16),
            pltpu.SemaphoreType.DMA((2,)),
            pltpu.SemaphoreType.DMA((3,)),
            pltpu.SemaphoreType.DMA((2, 108)),
        ],
        compiler_params=pltpu.CompilerParams(collective_id=1, has_side_effects=True, vmem_limit_bytes=50 * MB),
        name="experts",
    )(pay, mixed, gate, up, down)


def shards(tokens, routes, history, cache_keys, cache_values, attn_gain, w_query, w_key, w_value, w_out,
           ffn_gain, w_router, expert_gate, expert_up, expert_down):
    rows, width = tokens.shape
    positions = history[0] + jnp.arange(rows, dtype=jnp.int32)
    cosine, sine = rope_tables(positions)
    gains = jnp.concatenate([attn_gain, ffn_gain]).astype(f32).reshape(2, width)
    keep = lambda a: pltpu.with_memory_space_constraint(a, pltpu.HBM)
    q, keys_new, values_new, keys_near, values_near = project(
        keep(tokens), gains, keep(w_query), keep(w_key), keep(w_value), cosine, sine)
    attended = attend(history, q, cache_keys, cache_values, keys_near, values_near)
    mixed, pay = finish(attended, w_out, tokens, gains, jnp.transpose(w_router), jnp.transpose(routes))
    layer_out = run_experts(pay, mixed, expert_gate, expert_up, expert_down)
    return layer_out, keys_new, values_new


def solution(mesh):
    both = ("rep", "expert")
    in_specs = (
        P(both, None), P(both, None), P(both), P(both, None, None, None), P(both, None, None, None),
        P(), P(), P(), P(), P(), P(), P(),
        P("expert", None, None), P("expert", None, None), P("expert", None, None),
    )
    out_specs = (P(both, None), P(both, None), P(both, None))
    return jax.shard_map(shards, mesh=mesh, in_specs=in_specs, out_specs=out_specs, check_vma=False)
```

```python
import functools

import jax
import jax.numpy as jnp
from jax import lax
from jax.experimental import pallas as pl
from jax.experimental.pallas import tpu as pltpu
from jax.sharding import PartitionSpec as P

HEADS = 12
KV_HEADS = 2
HEAD_DIM = 128
TOP = 4
SINK = 4
WINDOW = 4096
CAP = 64
EXPERTS = 32

theta_base = 1000000.0
eps_norm = 1e-06

f32 = jnp.float32
bf16 = jnp.bfloat16
MB = 1024 * 1024


def dot(a, b):
    return jnp.dot(a, b, preferred_element_type=f32)


def dot_nt(a, b):
    return lax.dot_general(a, b, (((1,), (1,)), ((), ())), preferred_element_type=f32)


def rope_tables(positions):
    half = HEAD_DIM // 2
    exponent = jnp.arange(half, dtype=f32) * (2.0 / HEAD_DIM)
    inverse_freq = theta_base ** (-exponent)
    angles = positions.astype(f32)[:, None] * inverse_freq[None, :]
    cosine, sine = jnp.cos(angles), jnp.sin(angles)
    return jnp.concatenate([cosine, cosine], 1), jnp.concatenate([-sine, sine], 1)


def norm_rows(x, gain):
    mean_square = jnp.mean(x * x, axis=-1, keepdims=True)
    return (x * lax.rsqrt(mean_square + eps_norm) * gain).astype(bf16)


Q_BLOCK = 512


def qkv_kernel(tok_ref, gain_ref, wq_ref, wk_ref, wv_ref, cos_ref, sin_ref, q_ref, k_ref, v_ref, k2_ref, v2_ref, normed):
    cosine, sine = cos_ref[...], sin_ref[...]

    def rope(x):
        return (x * cosine + pltpu.roll(x, HEAD_DIM // 2, 1) * sine).astype(bf16)

    @pl.when(pl.program_id(0) == 0)
    def _():
        normed[...] = norm_rows(tok_ref[...].astype(f32), gain_ref[0:1])
        keys = dot(normed[...], wk_ref[...])
        for h in range(KV_HEADS):
            turned = rope(keys[:, h * HEAD_DIM:(h + 1) * HEAD_DIM])
            k_ref[:, h * HEAD_DIM:(h + 1) * HEAD_DIM] = turned
            k2_ref[:, h * HEAD_DIM:(h + 1) * HEAD_DIM] = turned
        values = dot(normed[...], wv_ref[...]).astype(bf16)
        v_ref[...] = values
        v2_ref[...] = values

    y = dot(normed[...], wq_ref[...])
    for h in range(Q_BLOCK // HEAD_DIM):
        q_ref[h] = rope(y[:, h * HEAD_DIM:(h + 1) * HEAD_DIM])


def project(tokens, gain, w_query, w_key, w_value, cosine, sine):
    rows, width = tokens.shape
    kv = w_key.shape[1]
    heads = Q_BLOCK // HEAD_DIM
    full = lambda a: pl.BlockSpec(a.shape, lambda i: (0,) * a.ndim)
    return pl.pallas_call(
        qkv_kernel,
        grid=(w_query.shape[1] // Q_BLOCK,),
        in_specs=[
            full(tokens), full(gain),
            pl.BlockSpec((width, Q_BLOCK), lambda i: (0, i)),
            full(w_key), full(w_value), full(cosine), full(sine),
        ],
        out_specs=[
            pl.BlockSpec((heads, rows, HEAD_DIM), lambda i: (i, 0, 0)),
        ] + [pl.BlockSpec((rows, kv), lambda i: (0, 0))] * 4,
        out_shape=[
            jax.ShapeDtypeStruct((HEADS, rows, HEAD_DIM), bf16),
        ] + [jax.ShapeDtypeStruct((rows, kv), bf16)] * 4,
        scratch_shapes=[pltpu.VMEM((rows, width), bf16)],
        compiler_params=pltpu.CompilerParams(vmem_limit_bytes=32 * MB),
        name="project",
    )(tokens, gain, w_query, w_key, w_value, cosine, sine)


KB = 1024
HT = 6
EXTRA = 384
SCALE2 = HEAD_DIM ** (-0.5) * 1.4426950408889634
LOW = -1e30


def attn_kernel(past_ref, q_ref, kc_ref, vc_ref, kn_ref, vn_ref, o_ref, s_main, s_tail, m_scr, l_scr, acc, kx, vx):
    rows = kn_ref.shape[0]
    tile = HT * rows
    past = past_ref[0]

    @pl.when(pl.program_id(1) == 0)
    def _():
        for new, cache, out in ((kn_ref, kc_ref, kx), (vn_ref, vc_ref, vx)):
            out[0:rows] = new[...]
            out[rows:EXTRA] = jnp.zeros((EXTRA - rows, HEAD_DIM), bf16)
            out[rows:rows + SINK] = cache[0, 0, WINDOW:WINDOW + SINK]

    q = q_ref[...].reshape(tile, HEAD_DIM)
    row = lax.broadcasted_iota(jnp.int32, (tile, 1), 0) & (rows - 1)
    blocks = jnp.minimum((past + (KB - 1)) // KB, WINDOW // KB)

    def limit(slot):
        back = (slot - past) & (WINDOW - 1)
        return jnp.where(slot < past, jnp.where(slot < SINK, 1 << 20, back), 0)

    def lane_max(s):
        out = s[:, 0:128]
        for c in range(1, s.shape[1] // 128):
            out = jnp.maximum(out, s[:, c * 128:(c + 1) * 128])
        return out

    def lane_sum(s):
        out = s[:, 0:128]
        for c in range(1, s.shape[1] // 128):
            out = out + s[:, c * 128:(c + 1) * 128]
        return out

    column = lax.broadcasted_iota(jnp.int32, (1, EXTRA), 1)
    tail_limit = limit(column + (WINDOW - rows))
    tail_limit = jnp.where(column < rows, rows, jnp.where(column < rows + SINK, tail_limit, 0))
    first_row = jnp.where(column < rows, column, 0)
    s = dot_nt(q, kx[...]) * SCALE2
    s = jnp.where((row >= first_row) & (row < tail_limit), s, LOW)
    s_tail[...] = s
    m_scr[...] = lane_max(s)

    def score(j, carry):
        start = pl.multiple_of(j * KB, KB)
        raw = lambda: dot_nt(q, kc_ref[0, 0, pl.ds(start, KB), :]) * SCALE2
        offset = (start - past) & (WINDOW - 1)
        plain = (start + KB <= past) & (offset >= rows) & (offset + KB <= WINDOW)

        @pl.when(plain)
        def _():
            s = raw()
            s_main[j] = s
            m_scr[...] = jnp.maximum(m_scr[...], lane_max(s))

        @pl.when(jnp.logical_not(plain))
        def _():
            slot = lax.broadcasted_iota(jnp.int32, (1, KB), 1) + start
            s = jnp.where(row < limit(slot), raw(), LOW)
            s_main[j] = s
            m_scr[...] = jnp.maximum(m_scr[...], lane_max(s))

        return carry

    lax.fori_loop(0, blocks, score, 0)
    top = jnp.max(m_scr[...], axis=1, keepdims=True)
    p = jnp.exp2(s_tail[...] - top)
    l_scr[...] = lane_sum(p)
    acc[...] = dot(p.astype(bf16), vx[...])

    def weigh(j, carry):
        start = pl.multiple_of(j * KB, KB)
        p = jnp.exp2(s_main[j] - top)
        l_scr[...] += lane_sum(p)
        acc[...] += dot(p.astype(bf16), vc_ref[0, 0, pl.ds(start, KB), :])
        return carry

    lax.fori_loop(0, blocks, weigh, 0)
    total = jnp.sum(l_scr[...], axis=1, keepdims=True)
    out = (acc[...] / total).astype(bf16)
    for h in range(HT):
        o_ref[:, h * HEAD_DIM:(h + 1) * HEAD_DIM] = out[h * rows:(h + 1) * rows]


def attend(past, q, cache_keys, cache_values, keys_new, values_new):
    rows = keys_new.shape[0]
    slots = cache_keys.shape[2]
    tile = HT * rows
    per_group = HEADS // KV_HEADS // HT
    cache_spec = pl.BlockSpec((1, 1, slots, HEAD_DIM), lambda g, i, *_: (0, g, 0, 0))
    new_spec = pl.BlockSpec((rows, HEAD_DIM), lambda g, i, *_: (0, g))
    return pl.pallas_call(
        attn_kernel,
        grid_spec=pltpu.PrefetchScalarGridSpec(
            num_scalar_prefetch=1,
            grid=(KV_HEADS, per_group),
            in_specs=[
                pl.BlockSpec((HT, rows, HEAD_DIM), lambda g, i, *_: (g * per_group + i, 0, 0)),
                cache_spec, cache_spec, new_spec, new_spec,
            ],
            out_specs=pl.BlockSpec((rows, HT * HEAD_DIM), lambda g, i, *_: (0, g * per_group + i)),
            scratch_shapes=[
                pltpu.VMEM((WINDOW // KB, tile, KB), f32),
                pltpu.VMEM((tile, EXTRA), f32),
                pltpu.VMEM((tile, 128), f32),
                pltpu.VMEM((tile, 128), f32),
                pltpu.VMEM((tile, HEAD_DIM), f32),
                pltpu.VMEM((EXTRA, HEAD_DIM), bf16),
                pltpu.VMEM((EXTRA, HEAD_DIM), bf16),
            ],
        ),
        out_shape=jax.ShapeDtypeStruct((rows, HEADS * HEAD_DIM), bf16),
        compiler_params=pltpu.CompilerParams(vmem_limit_bytes=40 * MB),
        name="attend",
    )(past, q, cache_keys, cache_values, keys_new, values_new)


META = 128


SIDE = 4
GROUPS = 2 * SIDE


def position():
    me = lax.axis_index("expert")
    return me // (2 * SIDE), (me // 2) % SIDE, me % 2


def peer(axis, step, flip):
    z, y, core = position()
    if axis == 0:
        z = (z + step) % SIDE
    else:
        y = (y + step) % SIDE
    return z * 2 * SIDE + y * 2 + (core + flip) % 2


def remote(src, dst, sems, i, to):
    return pltpu.make_async_remote_copy(
        src_ref=src, dst_ref=dst, send_sem=sems.at[0, i], recv_sem=sems.at[1, i],
        device_id={"expert": to}, device_id_type=pl.DeviceIdType.MESH,
    )


def greet():
    barrier = pltpu.get_barrier_semaphore()
    others = [peer(0, 0, 1)]
    for axis in range(2):
        for step in (1, SIDE - 1):
            for flip in range(2):
                others.append(peer(axis, step, flip))
    for other in others:
        pl.semaphore_signal(barrier, inc=1, device_id={"expert": other}, device_id_type=pl.DeviceIdType.MESH)
    return lambda: pl.semaphore_wait(barrier, len(others))


def group_expert(h, index):
    z, y, core = position()
    step, flip = index >> 1, index & 1
    if h == 0:
        y = (y + step) & (SIDE - 1)
    else:
        z = (z + step) & (SIDE - 1)
    return z * (2 * SIDE) + y * 2 + ((core + flip) & 1)


def lane(s):
    return (3 * s) % SIDE


class Spread:
    copies = 10

    def __init__(self, h, flip, src, dst, relay, sems, base, split=False):
        axis, rows = 1 - h, src.shape[2]
        top, low = pl.ds(0, rows // 2), pl.ds(rows // 2, rows // 2)
        unit = lambda step: (h, step * 2 + flip)
        slot = lambda step: (h, (SIDE - step) % SIDE * 2 + flip)
        ways = (1, SIDE - 1) if flip == 0 else (SIDE - 1, 1)
        self.relays, self.onward = [], []
        for i, (step, part) in enumerate(zip(ways, (top, low))):
            self.relays.append(
                remote(src.at[unit(2) + (part,)], relay.at[h, flip, i], sems, base + i, peer(axis, step, 0)))
            self.onward.append(
                remote(relay.at[h, flip, i], dst.at[slot(2) + (part,)], sems, base + 2 + i, peer(axis, step, flip)))
        steps = (1, SIDE - 1, 0)[:2 + flip]
        parts = ((low,), (top,)) if split else ((),)
        self.direct = [
            [
                remote(src.at[unit(step) + part], dst.at[slot(step) + part], sems,
                       base + 4 + i * len(steps) + j, peer(axis, step, flip))
                for j, step in enumerate(steps)
            ]
            for i, part in enumerate(parts)
        ]

    def forward(self, i):
        self.relays[i].wait_recv()
        self.onward[i].start()

    def wait_part(self, i):
        for copy in self.direct[i] + [self.onward[1 - i]]:
            copy.wait_recv()

    def wait_recv(self):
        for copy in sum(self.direct, []) + self.onward:
            copy.wait_recv()

    def wait_src(self):
        for copy in self.relays + sum(self.direct, []):
            copy.wait_send()

    def wait_onward(self):
        for copy in self.onward:
            copy.wait_send()


def start(copies):
    for copy in copies:
        copy.start()


def experts_kernel(att_ref, wo_ref, tok_ref, gain_ref, wr_t_ref, routes_t_ref, gate_hbm, up_hbm, down_hbm, out_ref,
                   mixed, near, send, x, relay_out, back, relay_in, sums, parts, passed, final, gate_w, up_w, down_w,
                   weight_sem, sems):
    rows, width = tok_ref.shape
    experts = wr_t_ref.shape[0]
    half = width // 2
    mid = rows // 2
    slots = SIDE * CAP
    top, low = pl.ds(0, mid), pl.ds(mid, mid)
    both = (0, 1)
    weights = [
        pltpu.make_async_copy(src.at[0], dst, weight_sem.at[i])
        for i, (src, dst) in enumerate(((gate_hbm, gate_w), (up_hbm, up_w), (down_hbm, down_w)))
    ]
    all_here = greet()
    gather, passing, out, home, pass_back, last = [], [], [], [], [], []
    for h in both:
        up, down = peer(h, 1, 0), peer(h, SIDE - 1, 0)
        base = h * 54
        gather.append([
            remote(near.at[h, 0, top], near.at[h, 3, top], sems, base, up),
            remote(near.at[h, 0, low], near.at[h, 1, low], sems, base + 1, down),
            remote(near.at[h, 0, low], near.at[h, 3, low], sems, base + 2, up),
            remote(near.at[h, 0, top], near.at[h, 1, top], sems, base + 3, down),
        ])
        passing.append([
            remote(near.at[h, 3, top], near.at[h, 2, top], sems, base + 4, up),
            remote(near.at[h, 1, low], near.at[h, 2, low], sems, base + 5, down),
        ])
        out.append([Spread(h, d, send, x, relay_out, sems, base + 6 + d * Spread.copies) for d in both])
        home.append([
            Spread(h, d, send, back, relay_in, sems, base + 26 + d * Spread.copies, split=d == 1) for d in both
        ])
        pass_back.append([
            remote(parts.at[h, 1, top], passed.at[h, 0], sems, base + 46, up),
            remote(parts.at[h, 1, low], passed.at[h, 1], sems, base + 47, down),
        ])
        last.append([
            remote(parts.at[h, 0, low], final.at[h, 0, low], sems, base + 48, up),
            remote(parts.at[h, 2, top], final.at[h, 1, top], sems, base + 49, down),
            remote(parts.at[h, 0, top], final.at[h, 0, top], sems, base + 50, up),
            remote(parts.at[h, 2, low], final.at[h, 1, low], sems, base + 51, down),
        ])

    expert_row = lax.broadcasted_iota(jnp.int32, (experts, rows), 0)
    named_t = routes_t_ref[0:1] == expert_row
    for j in range(1, TOP):
        named_t = named_t | (routes_t_ref[j:j + 1] == expert_row)
    named_t = jnp.where(named_t, 1.0, 0.0).astype(bf16)
    meta_from = lax.broadcasted_iota(jnp.int32, (experts, META), 0)
    meta_to = lax.broadcasted_iota(jnp.int32, (experts, META), 1)

    def prepare(first):
        span = slice(first, first + mid)
        total = tok_ref[span].astype(f32) + dot(att_ref[span], wo_ref[...])
        mixed[span] = total
        ffn = norm_rows(total, gain_ref[1:2])
        a = lax.broadcasted_iota(jnp.int32, (mid, rows), 0) + first
        b = lax.broadcasted_iota(jnp.int32, (mid, rows), 1)
        named = dot_nt(jnp.where(a == b, 1.0, 0.0).astype(bf16), named_t) > 0.5
        ranks = dot_nt(jnp.where(b < a, 1.0, 0.0).astype(bf16), named_t)
        rank = jnp.where(named, ranks, -1.0).astype(bf16)
        score = jnp.where(named, jax.nn.sigmoid(dot_nt(ffn, wr_t_ref[...])), 0.0)
        mix = score / jnp.sum(score, axis=1, keepdims=True)
        high = mix.astype(bf16)
        rest = (mix - high.astype(f32)).astype(bf16)
        put = lambda v, i: dot(v, jnp.where(meta_to == meta_from + i * experts, 1.0, 0.0).astype(bf16))
        meta = (put(high, 0) + put(rest, 1) + put(rank, 2)).astype(bf16)
        for h in both:
            near[h, 0, span, 0:half] = ffn[:, h * half:(h + 1) * half]
            near[h, 0, span, half:half + META] = meta

    prepare(0)
    all_here()
    for i in (0, 3):
        for h in both:
            gather[h][i].start()
    prepare(mid)
    for i in (1, 2):
        for h in both:
            gather[h][i].start()
    start(weights)

    place = (lax.broadcasted_iota(jnp.int32, (slots, rows), 0) % CAP).astype(f32)
    step_rows = (lax.broadcasted_iota(jnp.int32, (slots, META), 0) // CAP) * 2
    meta_column = lax.broadcasted_iota(jnp.int32, (slots, META), 1)

    def choose(h, s, d):
        spread = jnp.where(meta_column == group_expert(h, step_rows + d) + 2 * EXPERTS, 1.0, 0.0).astype(bf16)
        wanted = dot_nt(spread, near[h, s, :, half:half + META])
        select = jnp.where(wanted == place, 1.0, 0.0).astype(bf16)
        chosen = dot(select, near[h, s, :, 0:half]).astype(bf16)
        for k in range(SIDE):
            send[h, 2 * k + d, lane(s) * CAP:(lane(s) + 1) * CAP] = chosen[k * CAP:(k + 1) * CAP]

    for h in both:
        gather[h][0].wait_recv()
        passing[h][0].start()
    for h in both:
        for d in both:
            choose(h, 0, d)
    for h in both:
        gather[h][1].wait_recv()
        passing[h][1].start()
    for h in both:
        gather[h][2].wait_recv()
        for d in both:
            choose(h, 3, d)
        start([out[h][d].relays[0] for d in both])
    for h in both:
        gather[h][3].wait_recv()
        for d in both:
            choose(h, 1, d)
    for h in both:
        for copy in passing[h]:
            copy.wait_recv()
        choose(h, 2, 0)
        start([out[h][0].relays[1]] + out[h][0].direct[0])
    for h in both:
        choose(h, 2, 1)
        start([out[h][1].relays[1]])
    for h in both:
        x[h, 0] = send[h, 0]
    for i in both:
        for d in both:
            for h in both:
                out[h][d].forward(i)
    for h in both:
        start(out[h][1].direct[0])
    for copy in weights:
        copy.wait()

    def run_expert(d):
        def block(k, carry):
            spot = pl.ds(pl.multiple_of(lane(k) * CAP, CAP), CAP)
            a = x[0, 2 * k + d]
            b = jnp.concatenate([x[1, 2 * lane(i) + d, spot] for i in range(SIDE)], axis=0)
            gate = dot(a, gate_w[0:half]) + dot(b, gate_w[half:2 * half])
            up = dot(a, up_w[0:half]) + dot(b, up_w[half:2 * half])
            hidden = (jnp.maximum(gate, 0.0) * up).astype(bf16)
            send[0, 2 * k + d] = dot(hidden, down_w[:, 0:half]).astype(bf16)
            other = dot(hidden, down_w[:, half:2 * half]).astype(bf16)
            for i in range(SIDE):
                send[1, 2 * lane(i) + d, spot] = other[i * CAP:(i + 1) * CAP]
            return carry

        for h in both:
            out[h][d].wait_recv()
            out[h][d].wait_src()
        lax.fori_loop(0, SIDE, block, 0)

    run_expert(0)
    for h in both:
        start(home[h][0].relays + home[h][0].direct[0])
    run_expert(1)
    for h in both:
        start(home[h][1].relays[::-1])
    for i in both:
        for h in both:
            home[h][0].forward(i)
    for h in both:
        start(home[h][1].direct[0])
    for h in both:
        back[h, 0] = send[h, 0]
    for i in (1, 0):
        for h in both:
            home[h][1].forward(i)
    for h in both:
        start(home[h][1].direct[1])

    place_back = (lax.broadcasted_iota(jnp.int32, (rows, slots), 1) % CAP).astype(f32)
    meta_row = lax.broadcasted_iota(jnp.int32, (META, slots), 0)
    step_columns = (lax.broadcasted_iota(jnp.int32, (META, slots), 1) // CAP) * 2

    def weigh(h, s, d):
        meta = near[h, s, :, half:half + META]
        expert = group_expert(h, step_columns + d)
        take = lambda i: dot(meta, jnp.where(meta_row == expert + i * EXPERTS, 1.0, 0.0).astype(bf16))
        here = take(2) == place_back
        outs = jnp.concatenate([back[h, 2 * k + d, lane(s) * CAP:(lane(s) + 1) * CAP] for k in range(SIDE)], axis=0)
        high = jnp.where(here, take(0), 0.0).astype(bf16)
        rest = jnp.where(here, take(1), 0.0).astype(bf16)
        return dot(high, outs) + dot(rest, outs)

    for h in both:
        home[h][0].wait_recv()
        for s in range(SIDE):
            sums[h, s] = weigh(h, s, 0)
    for h in both:
        home[h][1].wait_part(0)
        parts[h, 1] = (sums[h, 2] + weigh(h, 2, 1)).astype(bf16)
        start(pass_back[h])
    for h in both:
        sums[h, 1] += weigh(h, 1, 1)
        parts[h, 0, mid:rows] = sums[h, 1, mid:rows].astype(bf16)
        last[h][0].start()
    for h in both:
        home[h][1].wait_part(1)
        sums[h, 3] += weigh(h, 3, 1)
        parts[h, 2, 0:mid] = sums[h, 3, 0:mid].astype(bf16)
        last[h][1].start()
    for h in both:
        pass_back[h][0].wait_recv()
        parts[h, 0, 0:mid] = (sums[h, 1, 0:mid] + passed[h, 0].astype(f32)).astype(bf16)
        last[h][2].start()
        pass_back[h][1].wait_recv()
        parts[h, 2, mid:rows] = (sums[h, 3, mid:rows] + passed[h, 1].astype(f32)).astype(bf16)
        last[h][3].start()
    for h in both:
        sums[h, 0] += weigh(h, 0, 1)
    for h in both:
        for copy in last[h]:
            copy.wait_recv()
        cols = slice(h * half, (h + 1) * half)
        out_ref[:, cols] = (
            mixed[:, cols] + (sums[h, 0] + final[h, 0].astype(f32) + final[h, 1].astype(f32))
        ).astype(bf16)
    for h in both:
        for copy in gather[h] + passing[h] + pass_back[h] + last[h]:
            copy.wait_send()
        for d in both:
            out[h][d].wait_onward()
            home[h][d].wait_src()
            home[h][d].wait_onward()


def run_experts(attended, w_out, tokens, gains, router_t, routes_t, gate, up, down):
    rows, width = tokens.shape
    half, ff = width // 2, gate.shape[2]
    vmem = pl.BlockSpec(memory_space=pltpu.VMEM)
    hbm = pl.BlockSpec(memory_space=pl.ANY)
    unit = (SIDE * CAP, half)
    part = (SIDE * CAP // 2, half)
    return pl.pallas_call(
        experts_kernel,
        in_specs=[vmem] * 6 + [hbm] * 3,
        out_specs=vmem,
        out_shape=jax.ShapeDtypeStruct((rows, width), bf16),
        scratch_shapes=[
            pltpu.VMEM((rows, width), f32),
            pltpu.VMEM((2, SIDE, rows, half + META), bf16),
            pltpu.VMEM((2, GROUPS) + unit, bf16),
            pltpu.VMEM((2, GROUPS) + unit, bf16),
            pltpu.VMEM((2, 2, 2) + part, bf16),
            pltpu.VMEM((2, GROUPS) + unit, bf16),
            pltpu.VMEM((2, 2, 2) + part, bf16),
            pltpu.VMEM((2, SIDE, rows, half), f32),
            pltpu.VMEM((2, 3, rows, half), bf16),
            pltpu.VMEM((2, 2, rows // 2, half), bf16),
            pltpu.VMEM((2, 2, rows, half), bf16),
            pltpu.VMEM((width, ff), bf16),
            pltpu.VMEM((width, ff), bf16),
            pltpu.VMEM((ff, width), bf16),
            pltpu.SemaphoreType.DMA((3,)),
            pltpu.SemaphoreType.DMA((2, 108)),
        ],
        compiler_params=pltpu.CompilerParams(collective_id=1, has_side_effects=True, vmem_limit_bytes=45 * MB),
        name="experts",
    )(attended, w_out, tokens, gains, router_t, routes_t, gate, up, down)


def shards(tokens, routes, history, cache_keys, cache_values, attn_gain, w_query, w_key, w_value, w_out,
           ffn_gain, w_router, expert_gate, expert_up, expert_down):
    rows, width = tokens.shape
    positions = history[0] + jnp.arange(rows, dtype=jnp.int32)
    cosine, sine = rope_tables(positions)
    gains = jnp.concatenate([attn_gain, ffn_gain]).astype(f32).reshape(2, width)
    keep = lambda a: pltpu.with_memory_space_constraint(a, pltpu.HBM)
    q, keys_new, values_new, keys_near, values_near = project(
        keep(tokens), gains, keep(w_query), keep(w_key), keep(w_value), cosine, sine)
    attended = attend(history, q, cache_keys, cache_values, keys_near, values_near)
    layer_out = run_experts(
        attended, w_out, tokens, gains, jnp.transpose(w_router), jnp.transpose(routes),
        keep(expert_gate), keep(expert_up), keep(expert_down))
    return layer_out, keys_new, values_new


def solution(mesh):
    both = ("rep", "expert")
    in_specs = (
        P(both, None), P(both, None), P(both), P(both, None, None, None), P(both, None, None, None),
        P(), P(), P(), P(), P(), P(), P(),
        P("expert", None, None), P("expert", None, None), P("expert", None, None),
    )
    out_specs = (P(both, None), P(both, None), P(both, None))
    return jax.shard_map(shards, mesh=mesh, in_specs=in_specs, out_specs=out_specs, check_vma=False)
```

```python
import functools

import jax
import jax.numpy as jnp
from jax import lax
from jax.experimental import pallas as pl
from jax.experimental.pallas import tpu as pltpu
from jax.sharding import PartitionSpec as P

HEADS = 12
KV_HEADS = 2
HEAD_DIM = 128
TOP = 4
SINK = 4
WINDOW = 4096
CAP = 64
EXPERTS = 32

theta_base = 1000000.0
eps_norm = 1e-06

f32 = jnp.float32
bf16 = jnp.bfloat16
MB = 1024 * 1024


def dot(a, b):
    return jnp.dot(a, b, preferred_element_type=f32)


def dot_nt(a, b):
    return lax.dot_general(a, b, (((1,), (1,)), ((), ())), preferred_element_type=f32)


def rope_tables(positions):
    half = HEAD_DIM // 2
    exponent = jnp.arange(half, dtype=f32) * (2.0 / HEAD_DIM)
    inverse_freq = theta_base ** (-exponent)
    angles = positions.astype(f32)[:, None] * inverse_freq[None, :]
    cosine, sine = jnp.cos(angles), jnp.sin(angles)
    return jnp.concatenate([cosine, cosine], 1), jnp.concatenate([-sine, sine], 1)


def norm_rows(x, gain):
    mean_square = jnp.mean(x * x, axis=-1, keepdims=True)
    return (x * lax.rsqrt(mean_square + eps_norm) * gain).astype(bf16)


Q_BLOCK = 512


def qkv_kernel(tok_ref, gain_ref, wq_ref, wk_ref, wv_ref, cos_ref, sin_ref, q_ref, k_ref, v_ref, k2_ref, v2_ref, normed):
    cosine, sine = cos_ref[...], sin_ref[...]

    def rope(x):
        return (x * cosine + pltpu.roll(x, HEAD_DIM // 2, 1) * sine).astype(bf16)

    @pl.when(pl.program_id(0) == 0)
    def _():
        normed[...] = norm_rows(tok_ref[...].astype(f32), gain_ref[0:1])
        keys = dot(normed[...], wk_ref[...])
        for h in range(KV_HEADS):
            turned = rope(keys[:, h * HEAD_DIM:(h + 1) * HEAD_DIM])
            k_ref[:, h * HEAD_DIM:(h + 1) * HEAD_DIM] = turned
            k2_ref[:, h * HEAD_DIM:(h + 1) * HEAD_DIM] = turned
        values = dot(normed[...], wv_ref[...]).astype(bf16)
        v_ref[...] = values
        v2_ref[...] = values

    y = dot(normed[...], wq_ref[...])
    for h in range(Q_BLOCK // HEAD_DIM):
        q_ref[h] = rope(y[:, h * HEAD_DIM:(h + 1) * HEAD_DIM])


def project(tokens, gain, w_query, w_key, w_value, cosine, sine):
    rows, width = tokens.shape
    kv = w_key.shape[1]
    heads = Q_BLOCK // HEAD_DIM
    full = lambda a: pl.BlockSpec(a.shape, lambda i: (0,) * a.ndim)
    return pl.pallas_call(
        qkv_kernel,
        grid=(w_query.shape[1] // Q_BLOCK,),
        in_specs=[
            full(tokens), full(gain),
            pl.BlockSpec((width, Q_BLOCK), lambda i: (0, i)),
            full(w_key), full(w_value), full(cosine), full(sine),
        ],
        out_specs=[
            pl.BlockSpec((heads, rows, HEAD_DIM), lambda i: (i, 0, 0)),
        ] + [pl.BlockSpec((rows, kv), lambda i: (0, 0))] * 4,
        out_shape=[
            jax.ShapeDtypeStruct((HEADS, rows, HEAD_DIM), bf16),
        ] + [jax.ShapeDtypeStruct((rows, kv), bf16)] * 4,
        scratch_shapes=[pltpu.VMEM((rows, width), bf16)],
        compiler_params=pltpu.CompilerParams(vmem_limit_bytes=32 * MB),
        name="project",
    )(tokens, gain, w_query, w_key, w_value, cosine, sine)


KB = 1024
HT = 6
EXTRA = 384
SCALE2 = HEAD_DIM ** (-0.5) * 1.4426950408889634
LOW = -1e30


def attn_kernel(past_ref, q_ref, kc_ref, vc_ref, kn_ref, vn_ref, o_ref, s_main, s_tail, m_scr, l_scr, acc, kx, vx):
    rows = kn_ref.shape[0]
    tile = HT * rows
    past = past_ref[0]

    @pl.when(pl.program_id(1) == 0)
    def _():
        for new, cache, out in ((kn_ref, kc_ref, kx), (vn_ref, vc_ref, vx)):
            out[0:rows] = new[...]
            out[rows:EXTRA] = jnp.zeros((EXTRA - rows, HEAD_DIM), bf16)
            out[rows:rows + SINK] = cache[0, 0, WINDOW:WINDOW + SINK]

    q = q_ref[...].reshape(tile, HEAD_DIM)
    row = lax.broadcasted_iota(jnp.int32, (tile, 1), 0) & (rows - 1)
    blocks = jnp.minimum((past + (KB - 1)) // KB, WINDOW // KB)

    def limit(slot):
        back = (slot - past) & (WINDOW - 1)
        return jnp.where(slot < past, jnp.where(slot < SINK, 1 << 20, back), 0)

    def lane_max(s):
        out = s[:, 0:128]
        for c in range(1, s.shape[1] // 128):
            out = jnp.maximum(out, s[:, c * 128:(c + 1) * 128])
        return out

    def lane_sum(s):
        out = s[:, 0:128]
        for c in range(1, s.shape[1] // 128):
            out = out + s[:, c * 128:(c + 1) * 128]
        return out

    column = lax.broadcasted_iota(jnp.int32, (1, EXTRA), 1)
    tail_limit = limit(column + (WINDOW - rows))
    tail_limit = jnp.where(column < rows, rows, jnp.where(column < rows + SINK, tail_limit, 0))
    first_row = jnp.where(column < rows, column, 0)
    s = dot_nt(q, kx[...]) * SCALE2
    s = jnp.where((row >= first_row) & (row < tail_limit), s, LOW)
    s_tail[...] = s
    m_scr[...] = lane_max(s)

    def score(j, carry):
        start = pl.multiple_of(j * KB, KB)
        raw = lambda: dot_nt(q, kc_ref[0, 0, pl.ds(start, KB), :]) * SCALE2
        offset = (start - past) & (WINDOW - 1)
        plain = (start + KB <= past) & (offset >= rows) & (offset + KB <= WINDOW)

        @pl.when(plain)
        def _():
            s = raw()
            s_main[j] = s
            m_scr[...] = jnp.maximum(m_scr[...], lane_max(s))

        @pl.when(jnp.logical_not(plain))
        def _():
            slot = lax.broadcasted_iota(jnp.int32, (1, KB), 1) + start
            s = jnp.where(row < limit(slot), raw(), LOW)
            s_main[j] = s
            m_scr[...] = jnp.maximum(m_scr[...], lane_max(s))

        return carry

    lax.fori_loop(0, blocks, score, 0)
    top = jnp.max(m_scr[...], axis=1, keepdims=True)
    p = jnp.exp2(s_tail[...] - top)
    l_scr[...] = lane_sum(p)
    acc[...] = dot(p.astype(bf16), vx[...])

    def weigh(j, carry):
        start = pl.multiple_of(j * KB, KB)
        p = jnp.exp2(s_main[j] - top)
        l_scr[...] += lane_sum(p)
        acc[...] += dot(p.astype(bf16), vc_ref[0, 0, pl.ds(start, KB), :])
        return carry

    lax.fori_loop(0, blocks, weigh, 0)
    total = jnp.sum(l_scr[...], axis=1, keepdims=True)
    out = (acc[...] / total).astype(bf16)
    for h in range(HT):
        o_ref[:, h * HEAD_DIM:(h + 1) * HEAD_DIM] = out[h * rows:(h + 1) * rows]


def attend(past, q, cache_keys, cache_values, keys_new, values_new):
    rows = keys_new.shape[0]
    slots = cache_keys.shape[2]
    tile = HT * rows
    per_group = HEADS // KV_HEADS // HT
    cache_spec = pl.BlockSpec((1, 1, slots, HEAD_DIM), lambda g, i, *_: (0, g, 0, 0))
    new_spec = pl.BlockSpec((rows, HEAD_DIM), lambda g, i, *_: (0, g))
    return pl.pallas_call(
        attn_kernel,
        grid_spec=pltpu.PrefetchScalarGridSpec(
            num_scalar_prefetch=1,
            grid=(KV_HEADS, per_group),
            in_specs=[
                pl.BlockSpec((HT, rows, HEAD_DIM), lambda g, i, *_: (g * per_group + i, 0, 0)),
                cache_spec, cache_spec, new_spec, new_spec,
            ],
            out_specs=pl.BlockSpec((rows, HT * HEAD_DIM), lambda g, i, *_: (0, g * per_group + i)),
            scratch_shapes=[
                pltpu.VMEM((WINDOW // KB, tile, KB), f32),
                pltpu.VMEM((tile, EXTRA), f32),
                pltpu.VMEM((tile, 128), f32),
                pltpu.VMEM((tile, 128), f32),
                pltpu.VMEM((tile, HEAD_DIM), f32),
                pltpu.VMEM((EXTRA, HEAD_DIM), bf16),
                pltpu.VMEM((EXTRA, HEAD_DIM), bf16),
            ],
        ),
        out_shape=jax.ShapeDtypeStruct((rows, HEADS * HEAD_DIM), bf16),
        compiler_params=pltpu.CompilerParams(vmem_limit_bytes=40 * MB),
        name="attend",
    )(past, q, cache_keys, cache_values, keys_new, values_new)


META = 128


SIDE = 4
GROUPS = 2 * SIDE


def position():
    me = lax.axis_index("expert")
    return me // (2 * SIDE), (me // 2) % SIDE, me % 2


def peer(axis, step, flip):
    z, y, core = position()
    if axis == 0:
        z = (z + step) % SIDE
    else:
        y = (y + step) % SIDE
    return z * 2 * SIDE + y * 2 + (core + flip) % 2


def remote(src, dst, sems, i, to):
    return pltpu.make_async_remote_copy(
        src_ref=src, dst_ref=dst, send_sem=sems.at[0, i], recv_sem=sems.at[1, i],
        device_id={"expert": to}, device_id_type=pl.DeviceIdType.MESH,
    )


def greet():
    barrier = pltpu.get_barrier_semaphore()
    others = [peer(0, 0, 1)]
    for axis in range(2):
        for step in (1, SIDE - 1):
            for flip in range(2):
                others.append(peer(axis, step, flip))
    for other in others:
        pl.semaphore_signal(barrier, inc=1, device_id={"expert": other}, device_id_type=pl.DeviceIdType.MESH)
    return lambda: pl.semaphore_wait(barrier, len(others))


def group_expert(h, index):
    z, y, core = position()
    step, flip = index >> 1, index & 1
    if h == 0:
        y = (y + step) & (SIDE - 1)
    else:
        z = (z + step) & (SIDE - 1)
    return z * (2 * SIDE) + y * 2 + ((core + flip) & 1)


def lane(s):
    return (3 * s) % SIDE


class Spread:
    copies = 8

    def __init__(self, h, flip, src, dst, sems, base):
        axis, rows = 1 - h, src.shape[2]
        steps = (2, 1, SIDE - 1, 0)[:3 + flip]
        self.parts = [
            [
                remote(src.at[h, step * 2 + flip, part], dst.at[h, (SIDE - step) % SIDE * 2 + flip, part], sems,
                       base + i * len(steps) + j, peer(axis, step, flip))
                for j, step in enumerate(steps)
            ]
            for i, part in enumerate((pl.ds(rows // 2, rows // 2), pl.ds(0, rows // 2)))
        ]

    def wait_part(self, i):
        for copy in self.parts[i]:
            copy.wait_recv()

    def wait_recv(self):
        self.wait_part(0)
        self.wait_part(1)

    def wait_src(self):
        for copy in self.parts[0] + self.parts[1]:
            copy.wait_send()


def start(copies):
    for copy in copies:
        copy.start()


def experts_kernel(att_ref, wo_ref, tok_ref, gain_ref, wr_t_ref, routes_t_ref, gate_hbm, up_hbm, down_hbm, out_ref,
                   mixed, near, send, x, back, sums, parts, passed, final, gate_w, up_w, down_w, weight_sem, sems):
    rows, width = tok_ref.shape
    experts = wr_t_ref.shape[0]
    half = width // 2
    mid = rows // 2
    slots = SIDE * CAP
    top, low = pl.ds(0, mid), pl.ds(mid, mid)
    both = (0, 1)
    weights = [
        pltpu.make_async_copy(src.at[0], dst, weight_sem.at[i])
        for i, (src, dst) in enumerate(((gate_hbm, gate_w), (up_hbm, up_w), (down_hbm, down_w)))
    ]
    all_here = greet()
    gather, passing, out, home, pass_back, last = [], [], [], [], [], []
    for h in both:
        up, down = peer(h, 1, 0), peer(h, SIDE - 1, 0)
        base = h * 44
        gather.append([
            remote(near.at[h, 0, top], near.at[h, 3, top], sems, base, up),
            remote(near.at[h, 0, low], near.at[h, 1, low], sems, base + 1, down),
            remote(near.at[h, 0, low], near.at[h, 3, low], sems, base + 2, up),
            remote(near.at[h, 0, top], near.at[h, 1, top], sems, base + 3, down),
        ])
        passing.append([
            remote(near.at[h, 3, top], near.at[h, 2, top], sems, base + 4, up),
            remote(near.at[h, 1, low], near.at[h, 2, low], sems, base + 5, down),
        ])
        out.append([Spread(h, d, send, x, sems, base + 6 + d * Spread.copies) for d in both])
        home.append([Spread(h, d, send, back, sems, base + 22 + d * Spread.copies) for d in both])
        pass_back.append([
            remote(parts.at[h, 1, top], passed.at[h, 0], sems, base + 38, up),
            remote(parts.at[h, 1, low], passed.at[h, 1], sems, base + 39, down),
        ])
        last.append([
            remote(parts.at[h, 0, low], final.at[h, 0, low], sems, base + 40, up),
            remote(parts.at[h, 2, top], final.at[h, 1, top], sems, base + 41, down),
            remote(parts.at[h, 0, top], final.at[h, 0, top], sems, base + 42, up),
            remote(parts.at[h, 2, low], final.at[h, 1, low], sems, base + 43, down),
        ])

    expert_row = lax.broadcasted_iota(jnp.int32, (experts, rows), 0)
    named_t = routes_t_ref[0:1] == expert_row
    for j in range(1, TOP):
        named_t = named_t | (routes_t_ref[j:j + 1] == expert_row)
    named_t = jnp.where(named_t, 1.0, 0.0).astype(bf16)
    meta_from = lax.broadcasted_iota(jnp.int32, (experts, META), 0)
    meta_to = lax.broadcasted_iota(jnp.int32, (experts, META), 1)

    def prepare(first):
        span = slice(first, first + mid)
        total = tok_ref[span].astype(f32) + dot(att_ref[span], wo_ref[...])
        mixed[span] = total
        ffn = norm_rows(total, gain_ref[1:2])
        a = lax.broadcasted_iota(jnp.int32, (mid, rows), 0) + first
        b = lax.broadcasted_iota(jnp.int32, (mid, rows), 1)
        named = dot_nt(jnp.where(a == b, 1.0, 0.0).astype(bf16), named_t) > 0.5
        ranks = dot_nt(jnp.where(b < a, 1.0, 0.0).astype(bf16), named_t)
        rank = jnp.where(named, ranks, -1.0).astype(bf16)
        score = jnp.where(named, jax.nn.sigmoid(dot_nt(ffn, wr_t_ref[...])), 0.0)
        mix = score / jnp.sum(score, axis=1, keepdims=True)
        high = mix.astype(bf16)
        rest = (mix - high.astype(f32)).astype(bf16)
        put = lambda v, i: dot(v, jnp.where(meta_to == meta_from + i * experts, 1.0, 0.0).astype(bf16))
        meta = (put(high, 0) + put(rest, 1) + put(rank, 2)).astype(bf16)
        for h in both:
            near[h, 0, span, 0:half] = ffn[:, h * half:(h + 1) * half]
            near[h, 0, span, half:half + META] = meta

    prepare(0)
    all_here()
    for i in (0, 3):
        for h in both:
            gather[h][i].start()
    prepare(mid)
    for i in (1, 2):
        for h in both:
            gather[h][i].start()
    start(weights)

    place = (lax.broadcasted_iota(jnp.int32, (slots, rows), 0) % CAP).astype(f32)
    step_rows = (lax.broadcasted_iota(jnp.int32, (slots, META), 0) // CAP) * 2
    meta_column = lax.broadcasted_iota(jnp.int32, (slots, META), 1)

    def choose(h, s, d):
        spread = jnp.where(meta_column == group_expert(h, step_rows + d) + 2 * EXPERTS, 1.0, 0.0).astype(bf16)
        wanted = dot_nt(spread, near[h, s, :, half:half + META])
        select = jnp.where(wanted == place, 1.0, 0.0).astype(bf16)
        chosen = dot(select, near[h, s, :, 0:half]).astype(bf16)
        for k in range(SIDE):
            send[h, 2 * k + d, lane(s) * CAP:(lane(s) + 1) * CAP] = chosen[k * CAP:(k + 1) * CAP]

    for h in both:
        gather[h][0].wait_recv()
        passing[h][0].start()
    for h in both:
        for d in both:
            choose(h, 0, d)
    for h in both:
        gather[h][1].wait_recv()
        passing[h][1].start()
    for h in both:
        gather[h][2].wait_recv()
        for d in both:
            choose(h, 3, d)
        start([out[h][d].parts[1][0] for d in both])
    for h in both:
        gather[h][3].wait_recv()
        for d in both:
            choose(h, 1, d)
    for h in both:
        for copy in passing[h]:
            copy.wait_recv()
        choose(h, 2, 0)
        start(out[h][0].parts[0] + out[h][0].parts[1][1:])
    for h in both:
        choose(h, 2, 1)
    for h in both:
        x[h, 0] = send[h, 0]
    for h in both:
        start(out[h][1].parts[0] + out[h][1].parts[1][1:])
    for copy in weights:
        copy.wait()

    def run_expert(d):
        def block(k, carry):
            spot = pl.ds(pl.multiple_of(lane(k) * CAP, CAP), CAP)
            a = x[0, 2 * k + d]
            b = jnp.concatenate([x[1, 2 * lane(i) + d, spot] for i in range(SIDE)], axis=0)
            gate = dot(a, gate_w[0:half]) + dot(b, gate_w[half:2 * half])
            up = dot(a, up_w[0:half]) + dot(b, up_w[half:2 * half])
            hidden = (jnp.maximum(gate, 0.0) * up).astype(bf16)
            send[0, 2 * k + d] = dot(hidden, down_w[:, 0:half]).astype(bf16)
            other = dot(hidden, down_w[:, half:2 * half]).astype(bf16)
            for i in range(SIDE):
                send[1, 2 * lane(i) + d, spot] = other[i * CAP:(i + 1) * CAP]
            return carry

        for h in both:
            out[h][d].wait_recv()
            out[h][d].wait_src()
        lax.fori_loop(0, SIDE, block, 0)

    run_expert(0)
    for h in both:
        start(home[h][0].parts[0] + home[h][0].parts[1])
    run_expert(1)
    for i in both:
        for h in both:
            start(home[h][1].parts[i])
    for h in both:
        back[h, 0] = send[h, 0]

    place_back = (lax.broadcasted_iota(jnp.int32, (rows, slots), 1) % CAP).astype(f32)
    meta_row = lax.broadcasted_iota(jnp.int32, (META, slots), 0)
    step_columns = (lax.broadcasted_iota(jnp.int32, (META, slots), 1) // CAP) * 2

    def weigh(h, s, d):
        meta = near[h, s, :, half:half + META]
        expert = group_expert(h, step_columns + d)
        take = lambda i: dot(meta, jnp.where(meta_row == expert + i * EXPERTS, 1.0, 0.0).astype(bf16))
        here = take(2) == place_back
        outs = jnp.concatenate([back[h, 2 * k + d, lane(s) * CAP:(lane(s) + 1) * CAP] for k in range(SIDE)], axis=0)
        high = jnp.where(here, take(0), 0.0).astype(bf16)
        rest = jnp.where(here, take(1), 0.0).astype(bf16)
        return dot(high, outs) + dot(rest, outs)

    for h in both:
        home[h][0].wait_recv()
        for s in range(SIDE):
            sums[h, s] = weigh(h, s, 0)
    for h in both:
        home[h][1].wait_part(0)
        parts[h, 1] = (sums[h, 2] + weigh(h, 2, 1)).astype(bf16)
        start(pass_back[h])
    for h in both:
        sums[h, 1] += weigh(h, 1, 1)
        parts[h, 0, mid:rows] = sums[h, 1, mid:rows].astype(bf16)
        last[h][0].start()
    for h in both:
        home[h][1].wait_part(1)
        sums[h, 3] += weigh(h, 3, 1)
        parts[h, 2, 0:mid] = sums[h, 3, 0:mid].astype(bf16)
        last[h][1].start()
    for h in both:
        pass_back[h][0].wait_recv()
        parts[h, 0, 0:mid] = (sums[h, 1, 0:mid] + passed[h, 0].astype(f32)).astype(bf16)
        last[h][2].start()
        pass_back[h][1].wait_recv()
        parts[h, 2, mid:rows] = (sums[h, 3, mid:rows] + passed[h, 1].astype(f32)).astype(bf16)
        last[h][3].start()
    for h in both:
        sums[h, 0] += weigh(h, 0, 1)
    for h in both:
        for copy in last[h]:
            copy.wait_recv()
        cols = slice(h * half, (h + 1) * half)
        out_ref[:, cols] = (
            mixed[:, cols] + (sums[h, 0] + final[h, 0].astype(f32) + final[h, 1].astype(f32))
        ).astype(bf16)
    for h in both:
        for copy in gather[h] + passing[h] + pass_back[h] + last[h]:
            copy.wait_send()
        for d in both:
            home[h][d].wait_src()


def run_experts(attended, w_out, tokens, gains, router_t, routes_t, gate, up, down):
    rows, width = tokens.shape
    half, ff = width // 2, gate.shape[2]
    vmem = pl.BlockSpec(memory_space=pltpu.VMEM)
    hbm = pl.BlockSpec(memory_space=pl.ANY)
    unit = (SIDE * CAP, half)
    return pl.pallas_call(
        experts_kernel,
        in_specs=[vmem] * 6 + [hbm] * 3,
        out_specs=vmem,
        out_shape=jax.ShapeDtypeStruct((rows, width), bf16),
        scratch_shapes=[
            pltpu.VMEM((rows, width), f32),
            pltpu.VMEM((2, SIDE, rows, half + META), bf16),
            pltpu.VMEM((2, GROUPS) + unit, bf16),
            pltpu.VMEM((2, GROUPS) + unit, bf16),
            pltpu.VMEM((2, GROUPS) + unit, bf16),
            pltpu.VMEM((2, SIDE, rows, half), f32),
            pltpu.VMEM((2, 3, rows, half), bf16),
            pltpu.VMEM((2, 2, rows // 2, half), bf16),
            pltpu.VMEM((2, 2, rows, half), bf16),
            pltpu.VMEM((width, ff), bf16),
            pltpu.VMEM((width, ff), bf16),
            pltpu.VMEM((ff, width), bf16),
            pltpu.SemaphoreType.DMA((3,)),
            pltpu.SemaphoreType.DMA((2, 88)),
        ],
        compiler_params=pltpu.CompilerParams(collective_id=1, has_side_effects=True, vmem_limit_bytes=45 * MB),
        name="experts",
    )(attended, w_out, tokens, gains, router_t, routes_t, gate, up, down)


def shards(tokens, routes, history, cache_keys, cache_values, attn_gain, w_query, w_key, w_value, w_out,
           ffn_gain, w_router, expert_gate, expert_up, expert_down):
    rows, width = tokens.shape
    positions = history[0] + jnp.arange(rows, dtype=jnp.int32)
    cosine, sine = rope_tables(positions)
    gains = jnp.concatenate([attn_gain, ffn_gain]).astype(f32).reshape(2, width)
    keep = lambda a: pltpu.with_memory_space_constraint(a, pltpu.HBM)
    q, keys_new, values_new, keys_near, values_near = project(
        keep(tokens), gains, keep(w_query), keep(w_key), keep(w_value), cosine, sine)
    attended = attend(history, q, cache_keys, cache_values, keys_near, values_near)
    layer_out = run_experts(
        attended, w_out, tokens, gains, jnp.transpose(w_router), jnp.transpose(routes),
        keep(expert_gate), keep(expert_up), keep(expert_down))
    return layer_out, keys_new, values_new


def solution(mesh):
    both = ("rep", "expert")
    in_specs = (
        P(both, None), P(both, None), P(both), P(both, None, None, None), P(both, None, None, None),
        P(), P(), P(), P(), P(), P(), P(),
        P("expert", None, None), P("expert", None, None), P("expert", None, None),
    )
    out_specs = (P(both, None), P(both, None), P(both, None))
    return jax.shard_map(shards, mesh=mesh, in_specs=in_specs, out_specs=out_specs, check_vma=False)
```

```python
import functools

import jax
import jax.numpy as jnp
from jax import lax
from jax.experimental import pallas as pl
from jax.experimental.pallas import tpu as pltpu
from jax.sharding import PartitionSpec as P

HEADS = 12
KV_HEADS = 2
HEAD_DIM = 128
TOP = 4
SINK = 4
WINDOW = 4096
CAP = 64
EXPERTS = 32

theta_base = 1000000.0
eps_norm = 1e-06

f32 = jnp.float32
bf16 = jnp.bfloat16
MB = 1024 * 1024


def dot(a, b):
    return jnp.dot(a, b, preferred_element_type=f32)


def dot_nt(a, b):
    return lax.dot_general(a, b, (((1,), (1,)), ((), ())), preferred_element_type=f32)


def rope_tables(positions):
    half = HEAD_DIM // 2
    exponent = jnp.arange(half, dtype=f32) * (2.0 / HEAD_DIM)
    inverse_freq = theta_base ** (-exponent)
    angles = positions.astype(f32)[:, None] * inverse_freq[None, :]
    cosine, sine = jnp.cos(angles), jnp.sin(angles)
    return jnp.concatenate([cosine, cosine], 1), jnp.concatenate([-sine, sine], 1)


def norm_rows(x, gain):
    mean_square = jnp.mean(x * x, axis=-1, keepdims=True)
    return (x * lax.rsqrt(mean_square + eps_norm) * gain).astype(bf16)


Q_BLOCK = 512


def qkv_kernel(tok_ref, gain_ref, wq_ref, wk_ref, wv_ref, cos_ref, sin_ref, q_ref, k_ref, v_ref, k2_ref, v2_ref, normed):
    cosine, sine = cos_ref[...], sin_ref[...]

    def rope(x):
        return (x * cosine + pltpu.roll(x, HEAD_DIM // 2, 1) * sine).astype(bf16)

    @pl.when(pl.program_id(0) == 0)
    def _():
        normed[...] = norm_rows(tok_ref[...].astype(f32), gain_ref[0:1])
        keys = dot(normed[...], wk_ref[...])
        for h in range(KV_HEADS):
            turned = rope(keys[:, h * HEAD_DIM:(h + 1) * HEAD_DIM])
            k_ref[:, h * HEAD_DIM:(h + 1) * HEAD_DIM] = turned
            k2_ref[:, h * HEAD_DIM:(h + 1) * HEAD_DIM] = turned
        values = dot(normed[...], wv_ref[...]).astype(bf16)
        v_ref[...] = values
        v2_ref[...] = values

    y = dot(normed[...], wq_ref[...])
    for h in range(Q_BLOCK // HEAD_DIM):
        q_ref[h] = rope(y[:, h * HEAD_DIM:(h + 1) * HEAD_DIM])


def project(tokens, gain, w_query, w_key, w_value, cosine, sine):
    rows, width = tokens.shape
    kv = w_key.shape[1]
    heads = Q_BLOCK // HEAD_DIM
    full = lambda a: pl.BlockSpec(a.shape, lambda i: (0,) * a.ndim)
    return pl.pallas_call(
        qkv_kernel,
        grid=(w_query.shape[1] // Q_BLOCK,),
        in_specs=[
            full(tokens), full(gain),
            pl.BlockSpec((width, Q_BLOCK), lambda i: (0, i)),
            full(w_key), full(w_value), full(cosine), full(sine),
        ],
        out_specs=[
            pl.BlockSpec((heads, rows, HEAD_DIM), lambda i: (i, 0, 0)),
        ] + [pl.BlockSpec((rows, kv), lambda i: (0, 0))] * 4,
        out_shape=[
            jax.ShapeDtypeStruct((HEADS, rows, HEAD_DIM), bf16),
        ] + [jax.ShapeDtypeStruct((rows, kv), bf16)] * 4,
        scratch_shapes=[pltpu.VMEM((rows, width), bf16)],
        compiler_params=pltpu.CompilerParams(vmem_limit_bytes=32 * MB),
        name="project",
    )(tokens, gain, w_query, w_key, w_value, cosine, sine)


KB = 1024
HT = 6
EXTRA = 384
SCALE2 = HEAD_DIM ** (-0.5) * 1.4426950408889634
LOW = -1e30


def attn_kernel(past_ref, q_ref, kc_ref, vc_ref, kn_ref, vn_ref, o_ref, s_main, s_tail, m_scr, acc, kx, vx):
    rows = kn_ref.shape[0]
    tile = HT * rows
    past = past_ref[0]

    @pl.when(pl.program_id(1) == 0)
    def _():
        for new, cache, out in ((kn_ref, kc_ref, kx), (vn_ref, vc_ref, vx)):
            out[0:rows] = new[...]
            out[rows:EXTRA] = jnp.zeros((EXTRA - rows, HEAD_DIM), bf16)
            out[rows:rows + SINK] = cache[0, 0, WINDOW:WINDOW + SINK]

    q = q_ref[...].reshape(tile, HEAD_DIM)
    row = lax.broadcasted_iota(jnp.int32, (tile, 1), 0) & (rows - 1)
    blocks = jnp.minimum((past + (KB - 1)) // KB, WINDOW // KB)

    def limit(slot):
        back = (slot - past) & (WINDOW - 1)
        return jnp.where(slot < past, jnp.where(slot < SINK, 1 << 20, back), 0)

    def lane_max(s):
        out = s[:, 0:128]
        for c in range(1, s.shape[1] // 128):
            out = jnp.maximum(out, s[:, c * 128:(c + 1) * 128])
        return out

    column = lax.broadcasted_iota(jnp.int32, (1, EXTRA), 1)
    tail_limit = limit(column + (WINDOW - rows))
    tail_limit = jnp.where(column < rows, rows, jnp.where(column < rows + SINK, tail_limit, 0))
    first_row = jnp.where(column < rows, column, 0)
    s = dot_nt(q, kx[...]) * SCALE2
    s = jnp.where((row >= first_row) & (row < tail_limit), s, LOW)
    s_tail[...] = s
    m_scr[...] = lane_max(s)

    def score(j, carry):
        start = pl.multiple_of(j * KB, KB)
        raw = lambda: dot_nt(q, kc_ref[0, 0, pl.ds(start, KB), :]) * SCALE2
        offset = (start - past) & (WINDOW - 1)
        plain = (start + KB <= past) & (offset >= rows) & (offset + KB <= WINDOW)

        @pl.when(plain)
        def _():
            s = raw()
            s_main[j] = s
            m_scr[...] = jnp.maximum(m_scr[...], lane_max(s))

        @pl.when(jnp.logical_not(plain))
        def _():
            slot = lax.broadcasted_iota(jnp.int32, (1, KB), 1) + start
            s = jnp.where(row < limit(slot), raw(), LOW)
            s_main[j] = s
            m_scr[...] = jnp.maximum(m_scr[...], lane_max(s))

        return carry

    lax.fori_loop(0, blocks, score, 0)
    top = jnp.max(m_scr[...], axis=1, keepdims=True)
    ones = jnp.ones((KB, HEAD_DIM), bf16)
    p = jnp.exp2(s_tail[...] - top).astype(bf16)
    acc[...] = dot(p, jnp.concatenate([vx[...], ones[:EXTRA]], axis=1))

    def weigh(j, carry):
        start = pl.multiple_of(j * KB, KB)
        p = jnp.exp2(s_main[j] - top).astype(bf16)
        acc[...] += dot(p, jnp.concatenate([vc_ref[0, 0, pl.ds(start, KB), :], ones], axis=1))
        return carry

    lax.fori_loop(0, blocks, weigh, 0)
    out = (acc[:, 0:HEAD_DIM] / acc[:, HEAD_DIM:2 * HEAD_DIM]).astype(bf16)
    for h in range(HT):
        o_ref[:, h * HEAD_DIM:(h + 1) * HEAD_DIM] = out[h * rows:(h + 1) * rows]


def attend(past, q, cache_keys, cache_values, keys_new, values_new):
    rows = keys_new.shape[0]
    slots = cache_keys.shape[2]
    tile = HT * rows
    per_group = HEADS // KV_HEADS // HT
    cache_spec = pl.BlockSpec((1, 1, slots, HEAD_DIM), lambda g, i, *_: (0, g, 0, 0))
    new_spec = pl.BlockSpec((rows, HEAD_DIM), lambda g, i, *_: (0, g))
    return pl.pallas_call(
        attn_kernel,
        grid_spec=pltpu.PrefetchScalarGridSpec(
            num_scalar_prefetch=1,
            grid=(KV_HEADS, per_group),
            in_specs=[
                pl.BlockSpec((HT, rows, HEAD_DIM), lambda g, i, *_: (g * per_group + i, 0, 0)),
                cache_spec, cache_spec, new_spec, new_spec,
            ],
            out_specs=pl.BlockSpec((rows, HT * HEAD_DIM), lambda g, i, *_: (0, g * per_group + i)),
            scratch_shapes=[
                pltpu.VMEM((WINDOW // KB, tile, KB), f32),
                pltpu.VMEM((tile, EXTRA), f32),
                pltpu.VMEM((tile, 128), f32),
                pltpu.VMEM((tile, 2 * HEAD_DIM), f32),
                pltpu.VMEM((EXTRA, HEAD_DIM), bf16),
                pltpu.VMEM((EXTRA, HEAD_DIM), bf16),
            ],
        ),
        out_shape=jax.ShapeDtypeStruct((rows, HEADS * HEAD_DIM), bf16),
        compiler_params=pltpu.CompilerParams(vmem_limit_bytes=40 * MB),
        name="attend",
    )(past, q, cache_keys, cache_values, keys_new, values_new)


META = 4 * TOP


SIDE = 4
GROUPS = 2 * SIDE


def position():
    me = lax.axis_index("expert")
    return me // (2 * SIDE), (me // 2) % SIDE, me % 2


def peer(axis, step, flip):
    z, y, core = position()
    if axis == 0:
        z = (z + step) % SIDE
    else:
        y = (y + step) % SIDE
    return z * 2 * SIDE + y * 2 + (core + flip) % 2


def remote(src, dst, sems, i, to):
    return pltpu.make_async_remote_copy(
        src_ref=src, dst_ref=dst, send_sem=sems.at[0, i], recv_sem=sems.at[1, i],
        device_id={"expert": to}, device_id_type=pl.DeviceIdType.MESH,
    )


def greet():
    barrier = pltpu.get_barrier_semaphore()
    others = [peer(0, 0, 1)]
    for axis in range(2):
        for step in (1, SIDE - 1):
            for flip in range(2):
                others.append(peer(axis, step, flip))
    for other in others:
        pl.semaphore_signal(barrier, inc=1, device_id={"expert": other}, device_id_type=pl.DeviceIdType.MESH)
    return lambda: pl.semaphore_wait(barrier, len(others))


def group_expert(h, index):
    z, y, core = position()
    step, flip = index >> 1, index & 1
    if h == 0:
        y = (y + step) & (SIDE - 1)
    else:
        z = (z + step) & (SIDE - 1)
    return z * (2 * SIDE) + y * 2 + ((core + flip) & 1)


def lane(s):
    return (3 * s) % SIDE


class Spread:
    copies = 8

    def __init__(self, h, flip, src, dst, sems, base):
        axis, rows = 1 - h, src.shape[2]
        steps = (2, 1, SIDE - 1, 0)[:3 + flip]
        self.parts = [
            [
                remote(src.at[h, step * 2 + flip, part], dst.at[h, (SIDE - step) % SIDE * 2 + flip, part], sems,
                       base + i * len(steps) + j, peer(axis, step, flip))
                for j, step in enumerate(steps)
            ]
            for i, part in enumerate((pl.ds(rows // 2, rows // 2), pl.ds(0, rows // 2)))
        ]

    def wait_part(self, i):
        for copy in self.parts[i]:
            copy.wait_recv()

    def wait_recv(self):
        self.wait_part(0)
        self.wait_part(1)

    def wait_src(self):
        for copy in self.parts[0] + self.parts[1]:
            copy.wait_send()


def start(copies):
    for copy in copies:
        copy.start()


def experts_kernel(att_ref, wo_ref, tok_ref, gain_ref, wr_t_ref, routes_t_ref, gate_hbm, up_hbm, down_hbm, out_ref,
                   mixed, near, notes, send, x, back, sums, parts, passed, final, gate_w, up_w, down_w, weight_sem, sems):
    rows, width = tok_ref.shape
    experts = wr_t_ref.shape[0]
    half = width // 2
    mid = rows // 2
    slots = SIDE * CAP
    top, low = pl.ds(0, mid), pl.ds(mid, mid)
    both = (0, 1)
    weights = [
        pltpu.make_async_copy(src.at[0], dst, weight_sem.at[i])
        for i, (src, dst) in enumerate(((gate_hbm, gate_w), (up_hbm, up_w), (down_hbm, down_w)))
    ]
    all_here = greet()
    gather, passing, noted, out, home, pass_back, last = [], [], [], [], [], [], []
    for h in both:
        up, down = peer(h, 1, 0), peer(h, SIDE - 1, 0)
        base = h * 48
        gather.append([
            remote(near.at[h, 0, top], near.at[h, 3, top], sems, base, up),
            remote(near.at[h, 0, low], near.at[h, 1, low], sems, base + 1, down),
            remote(near.at[h, 0, low], near.at[h, 3, low], sems, base + 2, up),
            remote(near.at[h, 0, top], near.at[h, 1, top], sems, base + 3, down),
        ])
        passing.append([
            remote(near.at[h, 3, top], near.at[h, 2, top], sems, base + 4, up),
            remote(near.at[h, 1, low], near.at[h, 2, low], sems, base + 5, down),
        ])
        noted.append([
            remote(notes.at[h, 0], notes.at[h, SIDE - step], sems, base + 43 + step, peer(h, step, 0))
            for step in range(1, SIDE)
        ])
        out.append([Spread(h, d, send, x, sems, base + 6 + d * Spread.copies) for d in both])
        home.append([Spread(h, d, send, back, sems, base + 22 + d * Spread.copies) for d in both])
        pass_back.append([
            remote(parts.at[h, 1, top], passed.at[h, 0], sems, base + 38, up),
            remote(parts.at[h, 1, low], passed.at[h, 1], sems, base + 39, down),
        ])
        last.append([
            remote(parts.at[h, 0, low], final.at[h, 0, low], sems, base + 40, up),
            remote(parts.at[h, 2, top], final.at[h, 1, top], sems, base + 41, down),
            remote(parts.at[h, 0, top], final.at[h, 0, top], sems, base + 42, up),
            remote(parts.at[h, 2, low], final.at[h, 1, low], sems, base + 43, down),
        ])

    expert_row = lax.broadcasted_iota(jnp.int32, (experts, rows), 0)
    named_t = routes_t_ref[0:1] == expert_row
    for j in range(1, TOP):
        named_t = named_t | (routes_t_ref[j:j + 1] == expert_row)
    named_t = jnp.where(named_t, 1.0, 0.0).astype(bf16)
    note_row = lax.broadcasted_iota(jnp.int32, (META, mid), 0)

    def prepare(first):
        span = slice(first, first + mid)
        total = tok_ref[span].astype(f32) + dot(att_ref[span], wo_ref[...])
        mixed[span] = total
        ffn = norm_rows(total, gain_ref[1:2])
        for h in both:
            near[h, 0, span] = ffn[:, h * half:(h + 1) * half]
        a = lax.broadcasted_iota(jnp.int32, (mid, rows), 0) + first
        b = lax.broadcasted_iota(jnp.int32, (mid, rows), 1)
        ranks = dot_nt(named_t, jnp.where(b < a, 1.0, 0.0).astype(bf16))
        score = jax.nn.sigmoid(dot_nt(wr_t_ref[...], ffn))
        chosen = [routes_t_ref[j:j + 1, span] for j in range(TOP)]
        pick = lambda j, v: jnp.sum(jnp.where(chosen[j] == expert_row[:, span], v, 0.0), axis=0, keepdims=True)
        shares = [pick(j, score) for j in range(TOP)]
        whole = (shares[0] + shares[1]) + (shares[2] + shares[3])
        note = jnp.zeros((META, mid), f32)
        for j in range(TOP):
            mix = shares[j] / whole
            high = mix.astype(bf16).astype(f32)
            for i, value in enumerate((chosen[j].astype(f32), pick(j, ranks), high, mix - high)):
                note = jnp.where(note_row == i * TOP + j, value, note)
        for h in both:
            notes[h, 0, :, span] = note.astype(bf16)

    prepare(0)
    all_here()
    for i in (0, 3):
        for h in both:
            gather[h][i].start()
    prepare(mid)
    for h in both:
        start([noted[h][0], noted[h][2]])
    for i in (1, 2):
        for h in both:
            gather[h][i].start()
    start(weights)

    slot = lax.broadcasted_iota(jnp.int32, (slots, rows), 0)

    def slot_key(h, d, slot):
        return (group_expert(h, (slot // CAP) * 2 + d) * CAP + slot % CAP).astype(f32)

    def choose(h, s, d):
        note = notes[h, s].astype(f32)
        wanted = slot_key(h, d, slot)
        select = jnp.zeros((slots, rows), f32)
        for j in range(TOP):
            select = jnp.where(note[j:j + 1] * CAP + note[TOP + j:TOP + j + 1] == wanted, 1.0, select)
        select = select.astype(bf16)
        chosen = dot(select, near[h, s]).astype(bf16)
        for k in range(SIDE):
            send[h, 2 * k + d, lane(s) * CAP:(lane(s) + 1) * CAP] = chosen[k * CAP:(k + 1) * CAP]

    for h in both:
        gather[h][0].wait_recv()
        start([passing[h][0], noted[h][1]])
    for h in both:
        for d in both:
            choose(h, 0, d)
    for h in both:
        gather[h][1].wait_recv()
        passing[h][1].start()
    for h in both:
        gather[h][2].wait_recv()
        noted[h][0].wait_recv()
        for d in both:
            choose(h, 3, d)
        start([out[h][d].parts[1][0] for d in both])
    for h in both:
        gather[h][3].wait_recv()
        noted[h][2].wait_recv()
        for d in both:
            choose(h, 1, d)
    for h in both:
        for copy in passing[h] + [noted[h][1]]:
            copy.wait_recv()
        choose(h, 2, 0)
        start(out[h][0].parts[0] + out[h][0].parts[1][1:])
    for h in both:
        choose(h, 2, 1)
    for h in both:
        x[h, 0] = send[h, 0]
    for h in both:
        start(out[h][1].parts[0] + out[h][1].parts[1][1:])
    for copy in weights:
        copy.wait()

    def run_expert(d):
        def block(k, carry):
            spot = pl.ds(pl.multiple_of(lane(k) * CAP, CAP), CAP)
            a = x[0, 2 * k + d]
            b = jnp.concatenate([x[1, 2 * lane(i) + d, spot] for i in range(SIDE)], axis=0)
            gate = dot(a, gate_w[0:half]) + dot(b, gate_w[half:2 * half])
            up = dot(a, up_w[0:half]) + dot(b, up_w[half:2 * half])
            hidden = (jnp.maximum(gate, 0.0) * up).astype(bf16)
            send[0, 2 * k + d] = dot(hidden, down_w[:, 0:half]).astype(bf16)
            other = dot(hidden, down_w[:, half:2 * half]).astype(bf16)
            for i in range(SIDE):
                send[1, 2 * lane(i) + d, spot] = other[i * CAP:(i + 1) * CAP]
            return carry

        for h in both:
            out[h][d].wait_recv()
            out[h][d].wait_src()
        lax.fori_loop(0, SIDE, block, 0)

    run_expert(0)
    for h in both:
        start(home[h][0].parts[0] + home[h][0].parts[1])
    run_expert(1)
    for i in both:
        for h in both:
            start(home[h][1].parts[i])
    for h in both:
        back[h, 0] = send[h, 0]

    slot_back = lax.broadcasted_iota(jnp.int32, (rows, slots), 1)
    a = lax.broadcasted_iota(jnp.int32, (rows, rows), 0)
    b = lax.broadcasted_iota(jnp.int32, (rows, rows), 1)
    same = jnp.where(a == b, 1.0, 0.0).astype(bf16)

    def weigh(h, s, d):
        note = dot_nt(same, notes[h, s])
        here = slot_key(h, d, slot_back)
        high, rest = jnp.zeros((rows, slots), f32), jnp.zeros((rows, slots), f32)
        for j in range(TOP):
            column = lambda i: note[:, i * TOP + j:i * TOP + j + 1]
            hit = column(0) * CAP + column(1) == here
            high = jnp.where(hit, column(2), high)
            rest = jnp.where(hit, column(3), rest)
        high, rest = high.astype(bf16), rest.astype(bf16)
        outs = jnp.concatenate([back[h, 2 * k + d, lane(s) * CAP:(lane(s) + 1) * CAP] for k in range(SIDE)], axis=0)
        return dot(high, outs) + dot(rest, outs)

    for h in both:
        home[h][0].wait_recv()
        for s in range(SIDE):
            sums[h, s] = weigh(h, s, 0)
    for h in both:
        home[h][1].wait_part(0)
        parts[h, 1] = (sums[h, 2] + weigh(h, 2, 1)).astype(bf16)
        start(pass_back[h])
    for h in both:
        sums[h, 1] += weigh(h, 1, 1)
        parts[h, 0, mid:rows] = sums[h, 1, mid:rows].astype(bf16)
        last[h][0].start()
    for h in both:
        home[h][1].wait_part(1)
        sums[h, 3] += weigh(h, 3, 1)
        parts[h, 2, 0:mid] = sums[h, 3, 0:mid].astype(bf16)
        last[h][1].start()
    for h in both:
        pass_back[h][0].wait_recv()
        parts[h, 0, 0:mid] = (sums[h, 1, 0:mid] + passed[h, 0].astype(f32)).astype(bf16)
        last[h][2].start()
        pass_back[h][1].wait_recv()
        parts[h, 2, mid:rows] = (sums[h, 3, mid:rows] + passed[h, 1].astype(f32)).astype(bf16)
        last[h][3].start()
    for h in both:
        sums[h, 0] += weigh(h, 0, 1)
    for h in both:
        for copy in last[h]:
            copy.wait_recv()
        cols = slice(h * half, (h + 1) * half)
        out_ref[:, cols] = (
            mixed[:, cols] + (sums[h, 0] + final[h, 0].astype(f32) + final[h, 1].astype(f32))
        ).astype(bf16)
    for h in both:
        for copy in gather[h] + passing[h] + noted[h] + pass_back[h] + last[h]:
            copy.wait_send()
        for d in both:
            home[h][d].wait_src()


def run_experts(attended, w_out, tokens, gains, router_t, routes_t, gate, up, down):
    rows, width = tokens.shape
    half, ff = width // 2, gate.shape[2]
    vmem = pl.BlockSpec(memory_space=pltpu.VMEM)
    hbm = pl.BlockSpec(memory_space=pl.ANY)
    unit = (SIDE * CAP, half)
    return pl.pallas_call(
        experts_kernel,
        in_specs=[vmem] * 6 + [hbm] * 3,
        out_specs=vmem,
        out_shape=jax.ShapeDtypeStruct((rows, width), bf16),
        scratch_shapes=[
            pltpu.VMEM((rows, width), f32),
            pltpu.VMEM((2, SIDE, rows, half), bf16),
            pltpu.VMEM((2, SIDE, META, rows), bf16),
            pltpu.VMEM((2, GROUPS) + unit, bf16),
            pltpu.VMEM((2, GROUPS) + unit, bf16),
            pltpu.VMEM((2, GROUPS) + unit, bf16),
            pltpu.VMEM((2, SIDE, rows, half), f32),
            pltpu.VMEM((2, 3, rows, half), bf16),
            pltpu.VMEM((2, 2, rows // 2, half), bf16),
            pltpu.VMEM((2, 2, rows, half), bf16),
            pltpu.VMEM((width, ff), bf16),
            pltpu.VMEM((width, ff), bf16),
            pltpu.VMEM((ff, width), bf16),
            pltpu.SemaphoreType.DMA((3,)),
            pltpu.SemaphoreType.DMA((2, 96)),
        ],
        compiler_params=pltpu.CompilerParams(collective_id=1, has_side_effects=True, vmem_limit_bytes=45 * MB),
        name="experts",
    )(attended, w_out, tokens, gains, router_t, routes_t, gate, up, down)


def shards(tokens, routes, history, cache_keys, cache_values, attn_gain, w_query, w_key, w_value, w_out,
           ffn_gain, w_router, expert_gate, expert_up, expert_down):
    rows, width = tokens.shape
    positions = history[0] + jnp.arange(rows, dtype=jnp.int32)
    cosine, sine = rope_tables(positions)
    gains = jnp.concatenate([attn_gain, ffn_gain]).astype(f32).reshape(2, width)
    keep = lambda a: pltpu.with_memory_space_constraint(a, pltpu.HBM)
    q, keys_new, values_new, keys_near, values_near = project(
        keep(tokens), gains, keep(w_query), keep(w_key), keep(w_value), cosine, sine)
    attended = attend(history, q, cache_keys, cache_values, keys_near, values_near)
    layer_out = run_experts(
        attended, w_out, tokens, gains, jnp.transpose(w_router), jnp.transpose(routes),
        keep(expert_gate), keep(expert_up), keep(expert_down))
    return layer_out, keys_new, values_new


def solution(mesh):
    both = ("rep", "expert")
    in_specs = (
        P(both, None), P(both, None), P(both), P(both, None, None, None), P(both, None, None, None),
        P(), P(), P(), P(), P(), P(), P(),
        P("expert", None, None), P("expert", None, None), P("expert", None, None),
    )
    out_specs = (P(both, None), P(both, None), P(both, None))
    return jax.shard_map(shards, mesh=mesh, in_specs=in_specs, out_specs=out_specs, check_vma=False)
```

```python
import functools

import jax
import jax.numpy as jnp
from jax import lax
from jax.experimental import pallas as pl
from jax.experimental.pallas import tpu as pltpu
from jax.sharding import PartitionSpec as P

HEADS = 12
KV_HEADS = 2
HEAD_DIM = 128
TOP = 4
SINK = 4
WINDOW = 4096
CAP = 64
EXPERTS = 32

theta_base = 1000000.0
eps_norm = 1e-06

f32 = jnp.float32
bf16 = jnp.bfloat16
MB = 1024 * 1024


def dot(a, b):
    return jnp.dot(a, b, preferred_element_type=f32)


def dot_nt(a, b):
    return lax.dot_general(a, b, (((1,), (1,)), ((), ())), preferred_element_type=f32)


def rope_tables(positions):
    half = HEAD_DIM // 2
    exponent = jnp.arange(half, dtype=f32) * (2.0 / HEAD_DIM)
    inverse_freq = theta_base ** (-exponent)
    angles = positions.astype(f32)[:, None] * inverse_freq[None, :]
    cosine, sine = jnp.cos(angles), jnp.sin(angles)
    return jnp.concatenate([cosine, cosine], 1), jnp.concatenate([-sine, sine], 1)


def norm_rows(x, gain):
    mean_square = jnp.mean(x * x, axis=-1, keepdims=True)
    return (x * lax.rsqrt(mean_square + eps_norm) * gain).astype(bf16)


Q_BLOCK = 512


def qkv_kernel(tok_ref, gain_ref, wq_ref, wk_ref, wv_ref, cos_ref, sin_ref, q_ref, k_ref, v_ref, k2_ref, v2_ref, normed):
    cosine, sine = cos_ref[...], sin_ref[...]

    def rope(x):
        return (x * cosine + pltpu.roll(x, HEAD_DIM // 2, 1) * sine).astype(bf16)

    @pl.when(pl.program_id(0) == 0)
    def _():
        normed[...] = norm_rows(tok_ref[...].astype(f32), gain_ref[...].astype(f32)[None])
        keys = dot(normed[...], wk_ref[...])
        for h in range(KV_HEADS):
            turned = rope(keys[:, h * HEAD_DIM:(h + 1) * HEAD_DIM])
            k_ref[:, h * HEAD_DIM:(h + 1) * HEAD_DIM] = turned
            k2_ref[:, h * HEAD_DIM:(h + 1) * HEAD_DIM] = turned
        values = dot(normed[...], wv_ref[...]).astype(bf16)
        v_ref[...] = values
        v2_ref[...] = values

    y = dot(normed[...], wq_ref[...])
    for h in range(Q_BLOCK // HEAD_DIM):
        q_ref[h] = rope(y[:, h * HEAD_DIM:(h + 1) * HEAD_DIM])


def project(tokens, gain, w_query, w_key, w_value, cosine, sine):
    rows, width = tokens.shape
    kv = w_key.shape[1]
    heads = Q_BLOCK // HEAD_DIM
    full = lambda a: pl.BlockSpec(a.shape, lambda i: (0,) * a.ndim)
    return pl.pallas_call(
        qkv_kernel,
        grid=(w_query.shape[1] // Q_BLOCK,),
        in_specs=[
            full(tokens), full(gain),
            pl.BlockSpec((width, Q_BLOCK), lambda i: (0, i)),
            full(w_key), full(w_value), full(cosine), full(sine),
        ],
        out_specs=[
            pl.BlockSpec((heads, rows, HEAD_DIM), lambda i: (i, 0, 0)),
        ] + [pl.BlockSpec((rows, kv), lambda i: (0, 0))] * 4,
        out_shape=[
            jax.ShapeDtypeStruct((HEADS, rows, HEAD_DIM), bf16),
        ] + [jax.ShapeDtypeStruct((rows, kv), bf16)] * 4,
        scratch_shapes=[pltpu.VMEM((rows, width), bf16)],
        compiler_params=pltpu.CompilerParams(vmem_limit_bytes=32 * MB),
        name="project",
    )(tokens, gain, w_query, w_key, w_value, cosine, sine)


KB = 1024
HT = 6
EXTRA = 384
SCALE2 = HEAD_DIM ** (-0.5) * 1.4426950408889634
LOW = -1e30


def attn_kernel(past_ref, q_ref, kc_ref, vc_ref, kn_ref, vn_ref, o_ref, s_main, s_tail, m_scr, acc, kx, vx):
    rows = kn_ref.shape[0]
    tile = HT * rows
    past = past_ref[0]

    @pl.when(pl.program_id(1) == 0)
    def _():
        for new, cache, out in ((kn_ref, kc_ref, kx), (vn_ref, vc_ref, vx)):
            out[0:rows] = new[...]
            out[rows:EXTRA] = jnp.zeros((EXTRA - rows, HEAD_DIM), bf16)
            out[rows:rows + SINK] = cache[0, 0, WINDOW:WINDOW + SINK]

    q = q_ref[...].reshape(tile, HEAD_DIM)
    row = lax.broadcasted_iota(jnp.int32, (tile, 1), 0) & (rows - 1)
    blocks = jnp.minimum((past + (KB - 1)) // KB, WINDOW // KB)

    def limit(slot):
        back = (slot - past) & (WINDOW - 1)
        return jnp.where(slot < past, jnp.where(slot < SINK, 1 << 20, back), 0)

    def lane_max(s):
        out = s[:, 0:128]
        for c in range(1, s.shape[1] // 128):
            out = jnp.maximum(out, s[:, c * 128:(c + 1) * 128])
        return out

    column = lax.broadcasted_iota(jnp.int32, (1, EXTRA), 1)
    tail_limit = limit(column + (WINDOW - rows))
    tail_limit = jnp.where(column < rows, rows, jnp.where(column < rows + SINK, tail_limit, 0))
    first_row = jnp.where(column < rows, column, 0)
    s = dot_nt(q, kx[...]) * SCALE2
    s = jnp.where((row >= first_row) & (row < tail_limit), s, LOW)
    s_tail[...] = s
    m_scr[...] = lane_max(s)

    def score(j, carry):
        start = pl.multiple_of(j * KB, KB)
        raw = lambda: dot_nt(q, kc_ref[0, 0, pl.ds(start, KB), :]) * SCALE2
        offset = (start - past) & (WINDOW - 1)
        plain = (start + KB <= past) & (offset >= rows) & (offset + KB <= WINDOW)

        @pl.when(plain)
        def _():
            s = raw()
            s_main[j] = s
            m_scr[...] = jnp.maximum(m_scr[...], lane_max(s))

        @pl.when(jnp.logical_not(plain))
        def _():
            slot = lax.broadcasted_iota(jnp.int32, (1, KB), 1) + start
            s = jnp.where(row < limit(slot), raw(), LOW)
            s_main[j] = s
            m_scr[...] = jnp.maximum(m_scr[...], lane_max(s))

        return carry

    lax.fori_loop(0, blocks, score, 0)
    top = jnp.max(m_scr[...], axis=1, keepdims=True)
    ones = jnp.ones((KB, HEAD_DIM), bf16)
    p = jnp.exp2(s_tail[...] - top).astype(bf16)
    acc[...] = dot(p, jnp.concatenate([vx[...], ones[:EXTRA]], axis=1))

    def weigh(j, carry):
        start = pl.multiple_of(j * KB, KB)
        p = jnp.exp2(s_main[j] - top).astype(bf16)
        acc[...] += dot(p, jnp.concatenate([vc_ref[0, 0, pl.ds(start, KB), :], ones], axis=1))
        return carry

    lax.fori_loop(0, blocks, weigh, 0)
    out = (acc[:, 0:HEAD_DIM] / acc[:, HEAD_DIM:2 * HEAD_DIM]).astype(bf16)
    for h in range(HT):
        o_ref[:, h * HEAD_DIM:(h + 1) * HEAD_DIM] = out[h * rows:(h + 1) * rows]


def attend(past, q, cache_keys, cache_values, keys_new, values_new):
    rows = keys_new.shape[0]
    slots = cache_keys.shape[2]
    tile = HT * rows
    per_group = HEADS // KV_HEADS // HT
    cache_spec = pl.BlockSpec((1, 1, slots, HEAD_DIM), lambda g, i, *_: (0, g, 0, 0))
    new_spec = pl.BlockSpec((rows, HEAD_DIM), lambda g, i, *_: (0, g))
    return pl.pallas_call(
        attn_kernel,
        grid_spec=pltpu.PrefetchScalarGridSpec(
            num_scalar_prefetch=1,
            grid=(KV_HEADS, per_group),
            in_specs=[
                pl.BlockSpec((HT, rows, HEAD_DIM), lambda g, i, *_: (g * per_group + i, 0, 0)),
                cache_spec, cache_spec, new_spec, new_spec,
            ],
            out_specs=pl.BlockSpec((rows, HT * HEAD_DIM), lambda g, i, *_: (0, g * per_group + i)),
            scratch_shapes=[
                pltpu.VMEM((WINDOW // KB, tile, KB), f32),
                pltpu.VMEM((tile, EXTRA), f32),
                pltpu.VMEM((tile, 128), f32),
                pltpu.VMEM((tile, 2 * HEAD_DIM), f32),
                pltpu.VMEM((EXTRA, HEAD_DIM), bf16),
                pltpu.VMEM((EXTRA, HEAD_DIM), bf16),
            ],
        ),
        out_shape=jax.ShapeDtypeStruct((rows, HEADS * HEAD_DIM), bf16),
        compiler_params=pltpu.CompilerParams(vmem_limit_bytes=40 * MB),
        name="attend",
    )(past, q, cache_keys, cache_values, keys_new, values_new)


META = 4 * TOP


SIDE = 4
GROUPS = 2 * SIDE


def position():
    me = lax.axis_index("expert")
    return me // (2 * SIDE), (me // 2) % SIDE, me % 2


def peer(axis, step, flip):
    z, y, core = position()
    if axis == 0:
        z = (z + step) % SIDE
    else:
        y = (y + step) % SIDE
    return z * 2 * SIDE + y * 2 + (core + flip) % 2


def remote(src, dst, sems, i, to):
    return pltpu.make_async_remote_copy(
        src_ref=src, dst_ref=dst, send_sem=sems.at[0, i], recv_sem=sems.at[1, i],
        device_id={"expert": to}, device_id_type=pl.DeviceIdType.MESH,
    )


def greet():
    barrier = pltpu.get_barrier_semaphore()
    others = [peer(0, 0, 1)]
    for axis in range(2):
        for step in (1, SIDE - 1):
            for flip in range(2):
                others.append(peer(axis, step, flip))
    for other in others:
        pl.semaphore_signal(barrier, inc=1, device_id={"expert": other}, device_id_type=pl.DeviceIdType.MESH)
    return lambda: pl.semaphore_wait(barrier, len(others))


def group_expert(h, index):
    z, y, core = position()
    step, flip = index >> 1, index & 1
    if h == 0:
        y = (y + step) & (SIDE - 1)
    else:
        z = (z + step) & (SIDE - 1)
    return z * (2 * SIDE) + y * 2 + ((core + flip) & 1)


def lane(s):
    return (3 * s) % SIDE


class Spread:
    copies = 8

    def __init__(self, h, flip, src, dst, sems, base):
        axis, rows = 1 - h, src.shape[2]
        steps = (2, 1, SIDE - 1, 0)[:3 + flip]
        self.parts = [
            [
                remote(src.at[h, step * 2 + flip, part], dst.at[h, (SIDE - step) % SIDE * 2 + flip, part], sems,
                       base + i * len(steps) + j, peer(axis, step, flip))
                for j, step in enumerate(steps)
            ]
            for i, part in enumerate((pl.ds(rows // 2, rows // 2), pl.ds(0, rows // 2)))
        ]

    def wait_part(self, i):
        for copy in self.parts[i]:
            copy.wait_recv()

    def wait_recv(self):
        self.wait_part(0)
        self.wait_part(1)

    def wait_src(self):
        for copy in self.parts[0] + self.parts[1]:
            copy.wait_send()


def start(copies):
    for copy in copies:
        copy.start()


def experts_kernel(att_ref, wo_ref, tok_ref, gain_ref, wr_t_ref, routes_t_ref, gate_hbm, up_hbm, down_hbm, out_ref,
                   mixed, near, notes, send, x, back, sums, parts, passed, final, gate_w, up_w, down_w, weight_sem, sems):
    rows, width = tok_ref.shape
    experts = wr_t_ref.shape[0]
    half = width // 2
    mid = rows // 2
    slots = SIDE * CAP
    top, low = pl.ds(0, mid), pl.ds(mid, mid)
    both = (0, 1)
    weights = [
        pltpu.make_async_copy(src.at[0], dst, weight_sem.at[i])
        for i, (src, dst) in enumerate(((gate_hbm, gate_w), (up_hbm, up_w), (down_hbm, down_w)))
    ]
    all_here = greet()
    gather, passing, noted, out, home, pass_back, last = [], [], [], [], [], [], []
    for h in both:
        up, down = peer(h, 1, 0), peer(h, SIDE - 1, 0)
        base = h * 48
        gather.append([
            remote(near.at[h, 0, top], near.at[h, 3, top], sems, base, up),
            remote(near.at[h, 0, low], near.at[h, 1, low], sems, base + 1, down),
            remote(near.at[h, 0, low], near.at[h, 3, low], sems, base + 2, up),
            remote(near.at[h, 0, top], near.at[h, 1, top], sems, base + 3, down),
        ])
        passing.append([
            remote(near.at[h, 3, top], near.at[h, 2, top], sems, base + 4, up),
            remote(near.at[h, 1, low], near.at[h, 2, low], sems, base + 5, down),
        ])
        noted.append([
            remote(notes.at[h, 0], notes.at[h, SIDE - step], sems, base + 43 + step, peer(h, step, 0))
            for step in range(1, SIDE)
        ])
        out.append([Spread(h, d, send, x, sems, base + 6 + d * Spread.copies) for d in both])
        home.append([Spread(h, d, send, back, sems, base + 22 + d * Spread.copies) for d in both])
        pass_back.append([
            remote(parts.at[h, 1, top], passed.at[h, 0], sems, base + 38, up),
            remote(parts.at[h, 1, low], passed.at[h, 1], sems, base + 39, down),
        ])
        last.append([
            remote(parts.at[h, 0, low], final.at[h, 0, low], sems, base + 40, up),
            remote(parts.at[h, 2, top], final.at[h, 1, top], sems, base + 41, down),
            remote(parts.at[h, 0, top], final.at[h, 0, top], sems, base + 42, up),
            remote(parts.at[h, 2, low], final.at[h, 1, low], sems, base + 43, down),
        ])

    expert_row = lax.broadcasted_iota(jnp.int32, (experts, rows), 0)
    named_t = routes_t_ref[0:1] == expert_row
    for j in range(1, TOP):
        named_t = named_t | (routes_t_ref[j:j + 1] == expert_row)
    named_t = jnp.where(named_t, 1.0, 0.0).astype(bf16)
    note_row = lax.broadcasted_iota(jnp.int32, (META, mid), 0)

    def prepare(first):
        span = slice(first, first + mid)
        total = tok_ref[span].astype(f32) + dot(att_ref[span], wo_ref[...])
        mixed[span] = total
        ffn = norm_rows(total, gain_ref[...].astype(f32)[None])
        for h in both:
            near[h, 0, span] = ffn[:, h * half:(h + 1) * half]
        a = lax.broadcasted_iota(jnp.int32, (mid, rows), 0) + first
        b = lax.broadcasted_iota(jnp.int32, (mid, rows), 1)
        ranks = dot_nt(named_t, jnp.where(b < a, 1.0, 0.0).astype(bf16))
        score = jax.nn.sigmoid(dot_nt(wr_t_ref[...], ffn))
        chosen = [routes_t_ref[j:j + 1, span] for j in range(TOP)]
        pick = lambda j, v: jnp.sum(jnp.where(chosen[j] == expert_row[:, span], v, 0.0), axis=0, keepdims=True)
        shares = [pick(j, score) for j in range(TOP)]
        whole = (shares[0] + shares[1]) + (shares[2] + shares[3])
        note = jnp.zeros((META, mid), f32)
        for j in range(TOP):
            mix = shares[j] / whole
            high = mix.astype(bf16).astype(f32)
            for i, value in enumerate((chosen[j].astype(f32), pick(j, ranks), high, mix - high)):
                note = jnp.where(note_row == i * TOP + j, value, note)
        for h in both:
            notes[h, 0, :, span] = note.astype(bf16)

    prepare(0)
    all_here()
    for i in (0, 3):
        for h in both:
            gather[h][i].start()
    prepare(mid)
    for h in both:
        start([noted[h][0], noted[h][2]])
    for i in (1, 2):
        for h in both:
            gather[h][i].start()
    start(weights)

    slot = lax.broadcasted_iota(jnp.int32, (slots, rows), 0)

    def slot_key(h, d, slot):
        return (group_expert(h, (slot // CAP) * 2 + d) * CAP + slot % CAP).astype(f32)

    def choose(h, s, d):
        note = notes[h, s].astype(f32)
        wanted = slot_key(h, d, slot)
        select = jnp.zeros((slots, rows), f32)
        for j in range(TOP):
            select = jnp.where(note[j:j + 1] * CAP + note[TOP + j:TOP + j + 1] == wanted, 1.0, select)
        select = select.astype(bf16)
        chosen = dot(select, near[h, s]).astype(bf16)
        for k in range(SIDE):
            send[h, 2 * k + d, lane(s) * CAP:(lane(s) + 1) * CAP] = chosen[k * CAP:(k + 1) * CAP]

    for h in both:
        gather[h][0].wait_recv()
        start([passing[h][0], noted[h][1]])
    for h in both:
        for d in both:
            choose(h, 0, d)
    for h in both:
        gather[h][1].wait_recv()
        passing[h][1].start()
    for h in both:
        gather[h][2].wait_recv()
        noted[h][0].wait_recv()
        for d in both:
            choose(h, 3, d)
        start([out[h][d].parts[1][0] for d in both])
    for h in both:
        gather[h][3].wait_recv()
        noted[h][2].wait_recv()
        for d in both:
            choose(h, 1, d)
    for h in both:
        for copy in passing[h] + [noted[h][1]]:
            copy.wait_recv()
        choose(h, 2, 0)
        start(out[h][0].parts[0] + out[h][0].parts[1][1:])
    for h in both:
        choose(h, 2, 1)
    for h in both:
        x[h, 0] = send[h, 0]
    for h in both:
        start(out[h][1].parts[0] + out[h][1].parts[1][1:])
    for copy in weights:
        copy.wait()

    def run_expert(d):
        def block(k, carry):
            spot = pl.ds(pl.multiple_of(lane(k) * CAP, CAP), CAP)
            a = x[0, 2 * k + d]
            b = jnp.concatenate([x[1, 2 * lane(i) + d, spot] for i in range(SIDE)], axis=0)
            gate = dot(a, gate_w[0:half]) + dot(b, gate_w[half:2 * half])
            up = dot(a, up_w[0:half]) + dot(b, up_w[half:2 * half])
            hidden = (jnp.maximum(gate, 0.0) * up).astype(bf16)
            send[0, 2 * k + d] = dot(hidden, down_w[:, 0:half]).astype(bf16)
            other = dot(hidden, down_w[:, half:2 * half]).astype(bf16)
            for i in range(SIDE):
                send[1, 2 * lane(i) + d, spot] = other[i * CAP:(i + 1) * CAP]
            return carry

        for h in both:
            out[h][d].wait_recv()
            out[h][d].wait_src()
        lax.fori_loop(0, SIDE, block, 0)

    run_expert(0)
    for h in both:
        start(home[h][0].parts[0] + home[h][0].parts[1])
    run_expert(1)
    for i in both:
        for h in both:
            start(home[h][1].parts[i])
    for h in both:
        back[h, 0] = send[h, 0]

    slot_back = lax.broadcasted_iota(jnp.int32, (rows, slots), 1)
    a = lax.broadcasted_iota(jnp.int32, (rows, rows), 0)
    b = lax.broadcasted_iota(jnp.int32, (rows, rows), 1)
    same = jnp.where(a == b, 1.0, 0.0).astype(bf16)

    def weigh(h, s, d):
        note = dot_nt(same, notes[h, s])
        here = slot_key(h, d, slot_back)
        high, rest = jnp.zeros((rows, slots), f32), jnp.zeros((rows, slots), f32)
        for j in range(TOP):
            column = lambda i: note[:, i * TOP + j:i * TOP + j + 1]
            hit = column(0) * CAP + column(1) == here
            high = jnp.where(hit, column(2), high)
            rest = jnp.where(hit, column(3), rest)
        high, rest = high.astype(bf16), rest.astype(bf16)
        outs = jnp.concatenate([back[h, 2 * k + d, lane(s) * CAP:(lane(s) + 1) * CAP] for k in range(SIDE)], axis=0)
        return dot(high, outs) + dot(rest, outs)

    for h in both:
        home[h][0].wait_recv()
        for s in range(SIDE):
            sums[h, s] = weigh(h, s, 0)
    for h in both:
        home[h][1].wait_part(0)
        parts[h, 1] = (sums[h, 2] + weigh(h, 2, 1)).astype(bf16)
        start(pass_back[h])
    for h in both:
        sums[h, 1] += weigh(h, 1, 1)
        parts[h, 0, mid:rows] = sums[h, 1, mid:rows].astype(bf16)
        last[h][0].start()
    for h in both:
        home[h][1].wait_part(1)
        sums[h, 3] += weigh(h, 3, 1)
        parts[h, 2, 0:mid] = sums[h, 3, 0:mid].astype(bf16)
        last[h][1].start()
    for h in both:
        pass_back[h][0].wait_recv()
        parts[h, 0, 0:mid] = (sums[h, 1, 0:mid] + passed[h, 0].astype(f32)).astype(bf16)
        last[h][2].start()
        pass_back[h][1].wait_recv()
        parts[h, 2, mid:rows] = (sums[h, 3, mid:rows] + passed[h, 1].astype(f32)).astype(bf16)
        last[h][3].start()
    for h in both:
        sums[h, 0] += weigh(h, 0, 1)
    for h in both:
        for copy in last[h]:
            copy.wait_recv()
        cols = slice(h * half, (h + 1) * half)
        out_ref[:, cols] = (
            mixed[:, cols] + (sums[h, 0] + final[h, 0].astype(f32) + final[h, 1].astype(f32))
        ).astype(bf16)
    for h in both:
        for copy in gather[h] + passing[h] + noted[h] + pass_back[h] + last[h]:
            copy.wait_send()
        for d in both:
            home[h][d].wait_src()


def run_experts(attended, w_out, tokens, gain, router_t, routes_t, gate, up, down):
    rows, width = tokens.shape
    half, ff = width // 2, gate.shape[2]
    vmem = pl.BlockSpec(memory_space=pltpu.VMEM)
    hbm = pl.BlockSpec(memory_space=pl.ANY)
    unit = (SIDE * CAP, half)
    return pl.pallas_call(
        experts_kernel,
        in_specs=[vmem] * 6 + [hbm] * 3,
        out_specs=vmem,
        out_shape=jax.ShapeDtypeStruct((rows, width), bf16),
        scratch_shapes=[
            pltpu.VMEM((rows, width), f32),
            pltpu.VMEM((2, SIDE, rows, half), bf16),
            pltpu.VMEM((2, SIDE, META, rows), bf16),
            pltpu.VMEM((2, GROUPS) + unit, bf16),
            pltpu.VMEM((2, GROUPS) + unit, bf16),
            pltpu.VMEM((2, GROUPS) + unit, bf16),
            pltpu.VMEM((2, SIDE, rows, half), f32),
            pltpu.VMEM((2, 3, rows, half), bf16),
            pltpu.VMEM((2, 2, rows // 2, half), bf16),
            pltpu.VMEM((2, 2, rows, half), bf16),
            pltpu.VMEM((width, ff), bf16),
            pltpu.VMEM((width, ff), bf16),
            pltpu.VMEM((ff, width), bf16),
            pltpu.SemaphoreType.DMA((3,)),
            pltpu.SemaphoreType.DMA((2, 96)),
        ],
        compiler_params=pltpu.CompilerParams(collective_id=1, has_side_effects=True, vmem_limit_bytes=45 * MB),
        name="experts",
    )(attended, w_out, tokens, gain, router_t, routes_t, gate, up, down)


def shards(tokens, routes, history, cache_keys, cache_values, attn_gain, w_query, w_key, w_value, w_out,
           ffn_gain, w_router, expert_gate, expert_up, expert_down):
    rows, width = tokens.shape
    positions = history[0] + jnp.arange(rows, dtype=jnp.int32)
    cosine, sine = rope_tables(positions)
    keep = lambda a: pltpu.with_memory_space_constraint(a, pltpu.HBM)
    q, keys_new, values_new, keys_near, values_near = project(
        keep(tokens), keep(attn_gain), keep(w_query), keep(w_key), keep(w_value), cosine, sine)
    attended = attend(history, q, cache_keys, cache_values, keys_near, values_near)
    layer_out = run_experts(
        attended, w_out, tokens, ffn_gain, jnp.transpose(w_router), jnp.transpose(routes),
        keep(expert_gate), keep(expert_up), keep(expert_down))
    return layer_out, keys_new, values_new


def solution(mesh):
    both = ("rep", "expert")
    in_specs = (
        P(both, None), P(both, None), P(both), P(both, None, None, None), P(both, None, None, None),
        P(), P(), P(), P(), P(), P(), P(),
        P("expert", None, None), P("expert", None, None), P("expert", None, None),
    )
    out_specs = (P(both, None), P(both, None), P(both, None))
    return jax.shard_map(shards, mesh=mesh, in_specs=in_specs, out_specs=out_specs, check_vma=False)
```

```python
import functools

import jax
import jax.numpy as jnp
from jax import lax
from jax.experimental import pallas as pl
from jax.experimental.pallas import tpu as pltpu
from jax.sharding import PartitionSpec as P

HEADS = 12
KV_HEADS = 2
HEAD_DIM = 128
TOP = 4
SINK = 4
WINDOW = 4096
CAP = 64
EXPERTS = 32

theta_base = 1000000.0
eps_norm = 1e-06

f32 = jnp.float32
bf16 = jnp.bfloat16
MB = 1024 * 1024


def dot(a, b):
    return jnp.dot(a, b, preferred_element_type=f32)


def dot_nt(a, b):
    return lax.dot_general(a, b, (((1,), (1,)), ((), ())), preferred_element_type=f32)


def rope_tables(positions):
    half = HEAD_DIM // 2
    exponent = jnp.arange(half, dtype=f32) * (2.0 / HEAD_DIM)
    inverse_freq = theta_base ** (-exponent)
    angles = positions.astype(f32)[:, None] * inverse_freq[None, :]
    cosine, sine = jnp.cos(angles), jnp.sin(angles)
    return jnp.concatenate([cosine, cosine], 1), jnp.concatenate([-sine, sine], 1)


def norm_rows(x, gain):
    mean_square = jnp.mean(x * x, axis=-1, keepdims=True)
    return (x * lax.rsqrt(mean_square + eps_norm) * gain).astype(bf16)


Q_BLOCK = 512


def qkv_kernel(tok_ref, gain_ref, wq_ref, wk_ref, wv_ref, cos_ref, sin_ref, q_ref, k_ref, v_ref, k2_ref, v2_ref, normed):
    cosine, sine = cos_ref[...], sin_ref[...]

    def rope(x):
        return (x * cosine + pltpu.roll(x, HEAD_DIM // 2, 1) * sine).astype(bf16)

    @pl.when(pl.program_id(0) == 0)
    def _():
        normed[...] = norm_rows(tok_ref[...].astype(f32), gain_ref[...].astype(f32)[None])
        keys = dot(normed[...], wk_ref[...])
        for h in range(KV_HEADS):
            turned = rope(keys[:, h * HEAD_DIM:(h + 1) * HEAD_DIM])
            k_ref[:, h * HEAD_DIM:(h + 1) * HEAD_DIM] = turned
            k2_ref[:, h * HEAD_DIM:(h + 1) * HEAD_DIM] = turned
        values = dot(normed[...], wv_ref[...]).astype(bf16)
        v_ref[...] = values
        v2_ref[...] = values

    y = dot(normed[...], wq_ref[...])
    for h in range(Q_BLOCK // HEAD_DIM):
        q_ref[h] = rope(y[:, h * HEAD_DIM:(h + 1) * HEAD_DIM])


def project(tokens, gain, w_query, w_key, w_value, cosine, sine):
    rows, width = tokens.shape
    kv = w_key.shape[1]
    heads = Q_BLOCK // HEAD_DIM
    full = lambda a: pl.BlockSpec(a.shape, lambda i: (0,) * a.ndim)
    return pl.pallas_call(
        qkv_kernel,
        grid=(w_query.shape[1] // Q_BLOCK,),
        in_specs=[
            full(tokens), full(gain),
            pl.BlockSpec((width, Q_BLOCK), lambda i: (0, i)),
            full(w_key), full(w_value), full(cosine), full(sine),
        ],
        out_specs=[
            pl.BlockSpec((heads, rows, HEAD_DIM), lambda i: (i, 0, 0)),
        ] + [pl.BlockSpec((rows, kv), lambda i: (0, 0))] * 4,
        out_shape=[
            jax.ShapeDtypeStruct((HEADS, rows, HEAD_DIM), bf16),
        ] + [jax.ShapeDtypeStruct((rows, kv), bf16)] * 4,
        scratch_shapes=[pltpu.VMEM((rows, width), bf16)],
        compiler_params=pltpu.CompilerParams(vmem_limit_bytes=32 * MB),
        name="project",
    )(tokens, gain, w_query, w_key, w_value, cosine, sine)


KB = 1024
HT = 6
EXTRA = 384
SCALE2 = HEAD_DIM ** (-0.5) * 1.4426950408889634
LOW = -1e30


def attn_kernel(past_ref, q_ref, kc_ref, vc_ref, kn_ref, vn_ref, o_ref, s_main, s_tail, m_scr, acc, kx, vx):
    rows = kn_ref.shape[0]
    tile = HT * rows
    past = past_ref[0]

    @pl.when(pl.program_id(1) == 0)
    def _():
        for new, cache, out in ((kn_ref, kc_ref, kx), (vn_ref, vc_ref, vx)):
            out[0:rows] = new[...]
            out[rows:EXTRA] = jnp.zeros((EXTRA - rows, HEAD_DIM), bf16)
            out[rows:rows + SINK] = cache[0, 0, WINDOW:WINDOW + SINK]

    q = q_ref[...].reshape(tile, HEAD_DIM)
    row = lax.broadcasted_iota(jnp.int32, (tile, 1), 0) & (rows - 1)
    blocks = jnp.minimum((past + (KB - 1)) // KB, WINDOW // KB)

    def limit(slot):
        back = (slot - past) & (WINDOW - 1)
        return jnp.where(slot < past, jnp.where(slot < SINK, 1 << 20, back), 0)

    def lane_max(s):
        out = s[:, 0:128]
        for c in range(1, s.shape[1] // 128):
            out = jnp.maximum(out, s[:, c * 128:(c + 1) * 128])
        return out

    column = lax.broadcasted_iota(jnp.int32, (1, EXTRA), 1)
    tail_limit = limit(column + (WINDOW - rows))
    tail_limit = jnp.where(column < rows, rows, jnp.where(column < rows + SINK, tail_limit, 0))
    first_row = jnp.where(column < rows, column, 0)
    s = dot_nt(q, kx[...]) * SCALE2
    s = jnp.where((row >= first_row) & (row < tail_limit), s, LOW)
    s_tail[...] = s
    m_scr[...] = lane_max(s)

    def score(j, carry):
        start = pl.multiple_of(j * KB, KB)
        raw = lambda: dot_nt(q, kc_ref[0, 0, pl.ds(start, KB), :]) * SCALE2
        offset = (start - past) & (WINDOW - 1)
        plain = (start + KB <= past) & (offset >= rows) & (offset + KB <= WINDOW)

        @pl.when(plain)
        def _():
            s = raw()
            s_main[j] = s
            m_scr[...] = jnp.maximum(m_scr[...], lane_max(s))

        @pl.when(jnp.logical_not(plain))
        def _():
            slot = lax.broadcasted_iota(jnp.int32, (1, KB), 1) + start
            s = jnp.where(row < limit(slot), raw(), LOW)
            s_main[j] = s
            m_scr[...] = jnp.maximum(m_scr[...], lane_max(s))

        return carry

    lax.fori_loop(0, blocks, score, 0)
    top = jnp.max(m_scr[...], axis=1, keepdims=True)
    ones = jnp.ones((KB, HEAD_DIM), bf16)
    p = jnp.exp2(s_tail[...] - top).astype(bf16)
    acc[...] = dot(p, jnp.concatenate([vx[...], ones[:EXTRA]], axis=1))

    def weigh(j, carry):
        start = pl.multiple_of(j * KB, KB)
        p = jnp.exp2(s_main[j] - top).astype(bf16)
        acc[...] += dot(p, jnp.concatenate([vc_ref[0, 0, pl.ds(start, KB), :], ones], axis=1))
        return carry

    lax.fori_loop(0, blocks, weigh, 0)
    out = (acc[:, 0:HEAD_DIM] / acc[:, HEAD_DIM:2 * HEAD_DIM]).astype(bf16)
    for h in range(HT):
        o_ref[:, h * HEAD_DIM:(h + 1) * HEAD_DIM] = out[h * rows:(h + 1) * rows]


def attend(past, q, cache_keys, cache_values, keys_new, values_new):
    rows = keys_new.shape[0]
    slots = cache_keys.shape[2]
    tile = HT * rows
    per_group = HEADS // KV_HEADS // HT
    cache_spec = pl.BlockSpec((1, 1, slots, HEAD_DIM), lambda g, i, *_: (0, g, 0, 0))
    new_spec = pl.BlockSpec((rows, HEAD_DIM), lambda g, i, *_: (0, g))
    return pl.pallas_call(
        attn_kernel,
        grid_spec=pltpu.PrefetchScalarGridSpec(
            num_scalar_prefetch=1,
            grid=(KV_HEADS, per_group),
            in_specs=[
                pl.BlockSpec((HT, rows, HEAD_DIM), lambda g, i, *_: (g * per_group + i, 0, 0)),
                cache_spec, cache_spec, new_spec, new_spec,
            ],
            out_specs=pl.BlockSpec((rows, HT * HEAD_DIM), lambda g, i, *_: (0, g * per_group + i)),
            scratch_shapes=[
                pltpu.VMEM((WINDOW // KB, tile, KB), f32),
                pltpu.VMEM((tile, EXTRA), f32),
                pltpu.VMEM((tile, 128), f32),
                pltpu.VMEM((tile, 2 * HEAD_DIM), f32),
                pltpu.VMEM((EXTRA, HEAD_DIM), bf16),
                pltpu.VMEM((EXTRA, HEAD_DIM), bf16),
            ],
        ),
        out_shape=jax.ShapeDtypeStruct((rows, HEADS * HEAD_DIM), bf16),
        compiler_params=pltpu.CompilerParams(vmem_limit_bytes=40 * MB),
        name="attend",
    )(past, q, cache_keys, cache_values, keys_new, values_new)


META = 4 * TOP


SIDE = 4
GROUPS = 2 * SIDE


def position():
    me = lax.axis_index("expert")
    return me // (2 * SIDE), (me // 2) % SIDE, me % 2


def peer(axis, step, flip):
    z, y, core = position()
    if axis == 0:
        z = (z + step) % SIDE
    else:
        y = (y + step) % SIDE
    return z * 2 * SIDE + y * 2 + (core + flip) % 2


def remote(src, dst, sems, i, to):
    return pltpu.make_async_remote_copy(
        src_ref=src, dst_ref=dst, send_sem=sems.at[0, i], recv_sem=sems.at[1, i],
        device_id={"expert": to}, device_id_type=pl.DeviceIdType.MESH,
    )


def greet():
    barrier = pltpu.get_barrier_semaphore()
    others = [peer(0, 0, 1)]
    for axis in range(2):
        for step in (1, SIDE - 1):
            for flip in range(2):
                others.append(peer(axis, step, flip))
    for other in others:
        pl.semaphore_signal(barrier, inc=1, device_id={"expert": other}, device_id_type=pl.DeviceIdType.MESH)
    return lambda: pl.semaphore_wait(barrier, len(others))


def group_expert(h, index):
    z, y, core = position()
    step, flip = index >> 1, index & 1
    if h == 0:
        y = (y + step) & (SIDE - 1)
    else:
        z = (z + step) & (SIDE - 1)
    return z * (2 * SIDE) + y * 2 + ((core + flip) & 1)


def lane(s):
    return (3 * s) % SIDE


class Spread:
    copies = 8

    def __init__(self, h, flip, src, dst, sems, base):
        axis, rows = 1 - h, src.shape[2]
        steps = (2, 1, SIDE - 1, 0)[:3 + flip]
        self.parts = [
            [
                remote(src.at[h, step * 2 + flip, part], dst.at[h, (SIDE - step) % SIDE * 2 + flip, part], sems,
                       base + i * len(steps) + j, peer(axis, step, flip))
                for j, step in enumerate(steps)
            ]
            for i, part in enumerate((pl.ds(rows // 2, rows // 2), pl.ds(0, rows // 2)))
        ]

    def wait_part(self, i):
        for copy in self.parts[i]:
            copy.wait_recv()

    def wait_recv(self):
        self.wait_part(0)
        self.wait_part(1)

    def wait_src(self):
        for copy in self.parts[0] + self.parts[1]:
            copy.wait_send()


def start(copies):
    for copy in copies:
        copy.start()


def experts_kernel(att_ref, wo_ref, tok_ref, gain_ref, wr_t_ref, routes_t_ref, gate_hbm, up_hbm, down_hbm, out_ref,
                   mixed, near, notes, send, x, back, sums, parts, passed, final, gate_w, up_w, down_w, weight_sem, sems):
    rows, width = tok_ref.shape
    experts = wr_t_ref.shape[0]
    half = width // 2
    mid = rows // 2
    slots = SIDE * CAP
    top, low = pl.ds(0, mid), pl.ds(mid, mid)
    both = (0, 1)
    weights = [
        pltpu.make_async_copy(src.at[0], dst, weight_sem.at[i])
        for i, (src, dst) in enumerate(((gate_hbm, gate_w), (up_hbm, up_w), (down_hbm, down_w)))
    ]
    all_here = greet()
    gather, passing, noted, out, home, pass_back, last = [], [], [], [], [], [], []
    for h in both:
        up, down = peer(h, 1, 0), peer(h, SIDE - 1, 0)
        base = h * 48
        gather.append([
            remote(near.at[h, 0, top], near.at[h, 3, top], sems, base, up),
            remote(near.at[h, 0, low], near.at[h, 1, low], sems, base + 1, down),
            remote(near.at[h, 0, low], near.at[h, 3, low], sems, base + 2, up),
            remote(near.at[h, 0, top], near.at[h, 1, top], sems, base + 3, down),
        ])
        passing.append([
            remote(near.at[h, 3, top], near.at[h, 2, top], sems, base + 4, up),
            remote(near.at[h, 1, low], near.at[h, 2, low], sems, base + 5, down),
        ])
        noted.append([
            remote(notes.at[h, 0], notes.at[h, SIDE - step], sems, base + 43 + step, peer(h, step, 0))
            for step in range(1, SIDE)
        ])
        out.append([Spread(h, d, send, x, sems, base + 6 + d * Spread.copies) for d in both])
        home.append([Spread(h, d, send, back, sems, base + 22 + d * Spread.copies) for d in both])
        pass_back.append([
            remote(parts.at[h, 1, top], passed.at[h, 0], sems, base + 38, up),
            remote(parts.at[h, 1, low], passed.at[h, 1], sems, base + 39, down),
        ])
        last.append([
            remote(parts.at[h, 0, low], final.at[h, 0, low], sems, base + 40, up),
            remote(parts.at[h, 2, top], final.at[h, 1, top], sems, base + 41, down),
            remote(parts.at[h, 0, top], final.at[h, 0, top], sems, base + 42, up),
            remote(parts.at[h, 2, low], final.at[h, 1, low], sems, base + 43, down),
        ])

    expert_row = lax.broadcasted_iota(jnp.int32, (experts, rows), 0)
    named_t = routes_t_ref[0:1] == expert_row
    for j in range(1, TOP):
        named_t = named_t | (routes_t_ref[j:j + 1] == expert_row)
    named_t = jnp.where(named_t, 1.0, 0.0).astype(bf16)
    note_row = lax.broadcasted_iota(jnp.int32, (META, mid), 0)

    def prepare(first):
        span = slice(first, first + mid)
        total = tok_ref[span].astype(f32) + dot(att_ref[span], wo_ref[...])
        mixed[span] = total
        ffn = norm_rows(total, gain_ref[...].astype(f32)[None])
        for h in both:
            near[h, 0, span] = ffn[:, h * half:(h + 1) * half]
        a = lax.broadcasted_iota(jnp.int32, (mid, rows), 0) + first
        b = lax.broadcasted_iota(jnp.int32, (mid, rows), 1)
        ranks = dot_nt(named_t, jnp.where(b < a, 1.0, 0.0).astype(bf16))
        score = jax.nn.sigmoid(dot_nt(wr_t_ref[...], ffn))
        chosen = [routes_t_ref[j:j + 1, span] for j in range(TOP)]
        pick = lambda j, v: jnp.sum(jnp.where(chosen[j] == expert_row[:, span], v, 0.0), axis=0, keepdims=True)
        shares = [pick(j, score) for j in range(TOP)]
        whole = (shares[0] + shares[1]) + (shares[2] + shares[3])
        note = jnp.zeros((META, mid), f32)
        for j in range(TOP):
            mix = shares[j] / whole
            high = mix.astype(bf16).astype(f32)
            for i, value in enumerate((chosen[j].astype(f32), pick(j, ranks), high, mix - high)):
                note = jnp.where(note_row == i * TOP + j, value, note)
        for h in both:
            notes[h, 0, :, span] = note.astype(bf16)

    prepare(0)
    all_here()
    for i in (0, 3):
        for h in both:
            gather[h][i].start()
    prepare(mid)
    for h in both:
        start([noted[h][0], noted[h][2]])
    for i in (1, 2):
        for h in both:
            gather[h][i].start()
    start(weights)

    slot = lax.broadcasted_iota(jnp.int32, (slots, rows), 0)

    def slot_key(h, d, slot):
        return (group_expert(h, (slot // CAP) * 2 + d) * CAP + slot % CAP).astype(f32)

    def choose(h, s, d):
        note = notes[h, s].astype(f32)
        wanted = slot_key(h, d, slot)
        select = jnp.zeros((slots, rows), f32)
        for j in range(TOP):
            select = jnp.where(note[j:j + 1] * CAP + note[TOP + j:TOP + j + 1] == wanted, 1.0, select)
        select = select.astype(bf16)
        chosen = dot(select, near[h, s]).astype(bf16)
        for k in range(SIDE):
            send[h, 2 * k + d, lane(s) * CAP:(lane(s) + 1) * CAP] = chosen[k * CAP:(k + 1) * CAP]

    for h in both:
        gather[h][0].wait_recv()
        start([passing[h][0], noted[h][1]])
    for h in both:
        for d in both:
            choose(h, 0, d)
    for h in both:
        gather[h][1].wait_recv()
        passing[h][1].start()
    for h in both:
        gather[h][2].wait_recv()
        noted[h][0].wait_recv()
        for d in both:
            choose(h, 3, d)
        start([out[h][d].parts[1][0] for d in both])
    for h in both:
        gather[h][3].wait_recv()
        noted[h][2].wait_recv()
        for d in both:
            choose(h, 1, d)
    for h in both:
        for copy in passing[h] + [noted[h][1]]:
            copy.wait_recv()
        choose(h, 2, 0)
        start(out[h][0].parts[0] + out[h][0].parts[1][1:])
    for h in both:
        choose(h, 2, 1)
    for h in both:
        x[h, 0] = send[h, 0]
    for h in both:
        start(out[h][1].parts[0] + out[h][1].parts[1][1:])
    for copy in weights:
        copy.wait()

    def run_expert(d):
        def block(k, carry):
            spot = pl.ds(pl.multiple_of(lane(k) * CAP, CAP), CAP)
            a = x[0, 2 * k + d]
            b = jnp.concatenate([x[1, 2 * lane(i) + d, spot] for i in range(SIDE)], axis=0)
            gate = dot(a, gate_w[0:half]) + dot(b, gate_w[half:2 * half])
            up = dot(a, up_w[0:half]) + dot(b, up_w[half:2 * half])
            hidden = (jnp.maximum(gate, 0.0) * up).astype(bf16)
            send[0, 2 * k + d] = dot(hidden, down_w[:, 0:half]).astype(bf16)
            other = dot(hidden, down_w[:, half:2 * half]).astype(bf16)
            for i in range(SIDE):
                send[1, 2 * lane(i) + d, spot] = other[i * CAP:(i + 1) * CAP]
            return carry

        for h in both:
            out[h][d].wait_recv()
            out[h][d].wait_src()
        lax.fori_loop(0, SIDE, block, 0)

    run_expert(0)
    for h in both:
        start(home[h][0].parts[0] + home[h][0].parts[1])
    run_expert(1)
    for i in both:
        for h in both:
            start(home[h][1].parts[i])
    for h in both:
        back[h, 0] = send[h, 0]

    slot_back = lax.broadcasted_iota(jnp.int32, (rows, slots), 1)
    a = lax.broadcasted_iota(jnp.int32, (rows, rows), 0)
    b = lax.broadcasted_iota(jnp.int32, (rows, rows), 1)
    same = jnp.where(a == b, 1.0, 0.0).astype(bf16)

    def weigh(h, s, d):
        note = dot_nt(same, notes[h, s])
        here = slot_key(h, d, slot_back)
        high, rest = jnp.zeros((rows, slots), f32), jnp.zeros((rows, slots), f32)
        for j in range(TOP):
            column = lambda i: note[:, i * TOP + j:i * TOP + j + 1]
            hit = column(0) * CAP + column(1) == here
            high = jnp.where(hit, column(2), high)
            rest = jnp.where(hit, column(3), rest)
        high, rest = high.astype(bf16), rest.astype(bf16)
        outs = jnp.concatenate([back[h, 2 * k + d, lane(s) * CAP:(lane(s) + 1) * CAP] for k in range(SIDE)], axis=0)
        return dot(high, outs) + dot(rest, outs)

    for h in both:
        home[h][0].wait_recv()
        for s in range(SIDE):
            sums[h, s] = weigh(h, s, 0)
    for h in both:
        home[h][1].wait_part(0)
        parts[h, 1] = (sums[h, 2] + weigh(h, 2, 1)).astype(bf16)
        start(pass_back[h])
    for h in both:
        sums[h, 1] += weigh(h, 1, 1)
        parts[h, 0, mid:rows] = sums[h, 1, mid:rows].astype(bf16)
        last[h][0].start()
    for h in both:
        home[h][1].wait_part(1)
        sums[h, 3] += weigh(h, 3, 1)
        parts[h, 2, 0:mid] = sums[h, 3, 0:mid].astype(bf16)
        last[h][1].start()
    for h in both:
        pass_back[h][0].wait_recv()
        parts[h, 0, 0:mid] = (sums[h, 1, 0:mid] + passed[h, 0].astype(f32)).astype(bf16)
        last[h][2].start()
        pass_back[h][1].wait_recv()
        parts[h, 2, mid:rows] = (sums[h, 3, mid:rows] + passed[h, 1].astype(f32)).astype(bf16)
        last[h][3].start()
    for h in both:
        sums[h, 0] += weigh(h, 0, 1) + mixed[:, h * half:(h + 1) * half]
    for h in both:
        for copy in last[h]:
            copy.wait_recv()
        cols = slice(h * half, (h + 1) * half)
        out_ref[:, cols] = (
            sums[h, 0] + (final[h, 0].astype(f32) + final[h, 1].astype(f32))
        ).astype(bf16)
    for h in both:
        for copy in gather[h] + passing[h] + noted[h] + pass_back[h] + last[h]:
            copy.wait_send()
        for d in both:
            home[h][d].wait_src()


def run_experts(attended, w_out, tokens, gain, router_t, routes_t, gate, up, down):
    rows, width = tokens.shape
    half, ff = width // 2, gate.shape[2]
    vmem = pl.BlockSpec(memory_space=pltpu.VMEM)
    hbm = pl.BlockSpec(memory_space=pl.ANY)
    unit = (SIDE * CAP, half)
    return pl.pallas_call(
        experts_kernel,
        in_specs=[vmem] * 6 + [hbm] * 3,
        out_specs=vmem,
        out_shape=jax.ShapeDtypeStruct((rows, width), bf16),
        scratch_shapes=[
            pltpu.VMEM((rows, width), f32),
            pltpu.VMEM((2, SIDE, rows, half), bf16),
            pltpu.VMEM((2, SIDE, META, rows), bf16),
            pltpu.VMEM((2, GROUPS) + unit, bf16),
            pltpu.VMEM((2, GROUPS) + unit, bf16),
            pltpu.VMEM((2, GROUPS) + unit, bf16),
            pltpu.VMEM((2, SIDE, rows, half), f32),
            pltpu.VMEM((2, 3, rows, half), bf16),
            pltpu.VMEM((2, 2, rows // 2, half), bf16),
            pltpu.VMEM((2, 2, rows, half), bf16),
            pltpu.VMEM((width, ff), bf16),
            pltpu.VMEM((width, ff), bf16),
            pltpu.VMEM((ff, width), bf16),
            pltpu.SemaphoreType.DMA((3,)),
            pltpu.SemaphoreType.DMA((2, 96)),
        ],
        compiler_params=pltpu.CompilerParams(collective_id=1, has_side_effects=True, vmem_limit_bytes=45 * MB),
        name="experts",
    )(attended, w_out, tokens, gain, router_t, routes_t, gate, up, down)


def shards(tokens, routes, history, cache_keys, cache_values, attn_gain, w_query, w_key, w_value, w_out,
           ffn_gain, w_router, expert_gate, expert_up, expert_down):
    rows, width = tokens.shape
    positions = history[0] + jnp.arange(rows, dtype=jnp.int32)
    cosine, sine = rope_tables(positions)
    keep = lambda a: pltpu.with_memory_space_constraint(a, pltpu.HBM)
    q, keys_new, values_new, keys_near, values_near = project(
        keep(tokens), keep(attn_gain), keep(w_query), keep(w_key), keep(w_value), cosine, sine)
    attended = attend(history, q, cache_keys, cache_values, keys_near, values_near)
    layer_out = run_experts(
        attended, w_out, tokens, ffn_gain, jnp.transpose(w_router), jnp.transpose(routes),
        keep(expert_gate), keep(expert_up), keep(expert_down))
    return layer_out, keys_new, values_new


def solution(mesh):
    both = ("rep", "expert")
    in_specs = (
        P(both, None), P(both, None), P(both), P(both, None, None, None), P(both, None, None, None),
        P(), P(), P(), P(), P(), P(), P(),
        P("expert", None, None), P("expert", None, None), P("expert", None, None),
    )
    out_specs = (P(both, None), P(both, None), P(both, None))
    return jax.shard_map(shards, mesh=mesh, in_specs=in_specs, out_specs=out_specs, check_vma=False)
```
